32 devices in a mesh: fsdp: 16 (over z, y, x), dp: 2 (over core).
Axes of the slice: x: 2, y: 2, z: 4, core: 2. Of those that a mesh axis runs over, the one named last changes fastest.
Arguments:
- tokens: bfloat16 [2, 2048, 2048], P('dp', 'fsdp'), may hold values from -6 to 6
- segment_ids: int32 [2, 2048], P('dp'), may hold values from 0 to 7, never falling along the last dimension, each value on 1 to 1280 neighbouring positions
- gain_attn: float32 [2048], replicated, may hold values from 0.5 to 1.5
- gain_mlp: float32 [2048], replicated, may hold values from 0.5 to 1.5
- query_matrix: bfloat16 [2048, 2048], P('fsdp'), may hold values from -0.125 to 0.125
- key_matrix: bfloat16 [2048, 256], P('fsdp'), may hold values from -0.125 to 0.125
- value_matrix: bfloat16 [2048, 256], P('fsdp'), may hold values from -0.125 to 0.125
- output_matrix: bfloat16 [2048, 2048], P('fsdp'), may hold values from -1 to 1
- gate_matrix: bfloat16 [16384, 2048], P('fsdp'), may hold values from -0.125 to 0.125
- upward_matrix: bfloat16 [16384, 2048], P('fsdp'), may hold values from -0.125 to 0.125
- down_matrix: bfloat16 [16384, 2048], P('fsdp'), may hold values from -0.046875 to 0.046875
- query_factor_first: bfloat16 [2048, 256], replicated, may hold values from -0.125 to 0.125
- query_factor_second: bfloat16 [256, 2048], replicated, may hold values from -0.1875 to 0.1875
- key_factor_first: bfloat16 [2048, 256], replicated, may hold values from -0.125 to 0.125
- key_factor_second: bfloat16 [256, 256], replicated, may hold values from -0.1875 to 0.1875
- value_factor_first: bfloat16 [2048, 256], replicated, may hold values from -0.125 to 0.125
- value_factor_second: bfloat16 [256, 256], replicated, may hold values from -0.1875 to 0.1875
- output_factor_first: bfloat16 [2048, 256], replicated, may hold values from -1 to 1
- output_factor_second: bfloat16 [256, 2048], replicated, may hold values from -0.1875 to 0.1875
- gate_factor_first: bfloat16 [2048, 256], replicated, may hold values from -0.125 to 0.125
- gate_factor_second: bfloat16 [256, 16384], replicated, may hold values from -0.1875 to 0.1875
- upward_factor_first: bfloat16 [2048, 256], replicated, may hold values from -0.125 to 0.125
- upward_factor_second: bfloat16 [256, 16384], replicated, may hold values from -0.1875 to 0.1875
- down_factor_first: bfloat16 [16384, 256], replicated, may hold values from -0.046875 to 0.046875
- down_factor_second: bfloat16 [256, 2048], replicated, may hold values from -0.1875 to 0.1875
- cotangent: bfloat16 [2, 2048, 2048], P('dp', 'fsdp'), may hold values from -6 to 6
Outputs:
- output: bfloat16 [2, 2048, 2048], P('dp', 'fsdp')
- grad_tokens: float32 [2, 2048, 2048], P('dp', 'fsdp')
- grad_gain_attn: float32 [2048], P('fsdp')
- grad_gain_mlp: float32 [2048], P('fsdp')
- grad_query_weight: float32 [2048, 2048], P('fsdp')
- grad_key_weight: float32 [2048, 256], P('fsdp')
- grad_value_weight: float32 [2048, 256], P('fsdp')
- grad_output_weight: float32 [2048, 2048], P('fsdp')
- grad_gate_weight: float32 [16384, 2048], P('fsdp')
- grad_up_weight: float32 [16384, 2048], P('fsdp')
- grad_down_weight: float32 [16384, 2048], P('fsdp')
- grad_query_in: float32 [2048, 256], P('fsdp')
- grad_query_out: float32 [256, 2048], P('fsdp')
- grad_key_in: float32 [2048, 256], P('fsdp')
- grad_key_out: float32 [256, 256], P('fsdp')
- grad_value_in: float32 [2048, 256], P('fsdp')
- grad_value_out: float32 [256, 256], P('fsdp')
- grad_output_in: float32 [2048, 256], P('fsdp')
- grad_output_out: float32 [256, 2048], P('fsdp')
- grad_gate_in: float32 [2048, 256], P('fsdp')
- grad_gate_out: float32 [256, 16384], P(None, 'fsdp')
- grad_up_in: float32 [2048, 256], P('fsdp')
- grad_up_out: float32 [256, 16384], P(None, 'fsdp')
- grad_down_in: float32 [16384, 256], P('fsdp')
- grad_down_out: float32 [256, 2048], P('fsdp')
The draws below stay inside these ranges and needn't reach their ends.
Inputs may be any that keep to these rules, and one draw needn't show every extreme that they name: `segment_ids`: along each sequence the ids never fall; each of the 8 ids covers 1 to 1280 consecutive positions, and one covers exactly 1280.
All inputs are finite; a program needn't handle non-finite values.
Results may differ from the reference program's by a relative error of at most 0.017.
Values may be sent and summed in bfloat16 or wider, within the bound.
A program may use at most 448 MiB of HBM per device.

```python
import math
import jax
import jax.numpy as jnp
import numpy as np
from jax import lax

D = 2048
HEADS = 8
HD = 256
FF = 16384
RANK = 256
TOK_DEV = 128
DOCS = 8
SEQS = 2
LEN = 2048
DOC_MOST = 1280
N_FSDP = 16


def strengthened(drawn, key, source, target, blocks, factor):
    def block_of(position):
        return (jnp.arange(drawn.shape[position]) // (drawn.shape[position] // blocks)).reshape((-1,) + (1,) * (drawn.ndim - 1 - position))

    near = jax.random.permutation(key, blocks)[block_of(target)]
    other_side = (block_of(target) + blocks // 2) % blocks
    return jnp.where((block_of(source) == near) | (block_of(source) == other_side), factor * drawn, drawn)


def block_scale(own_key, dims, shards, low, top_value):
    factor_of = 1.0
    for dim, blocks in shards:
        heights = jax.random.uniform(jax.random.fold_in(jax.random.fold_in(own_key, 6), dim), (blocks,), jnp.float32, low / len(shards), top_value / len(shards))
        factor_of = factor_of * jnp.repeat(jnp.exp(heights), dims[dim] // blocks).reshape((-1,) + (1,) * (len(dims) - 1 - dim))
    return factor_of


def profile(number_of, total, most, lean):
    loads = [(1 << 20) // math.isqrt(grade ** lean) + 1 for grade in range(2, number_of + 1)]
    spare, holding = total - most - (number_of - 1), [1] * (number_of - 1)
    while spare > 0:
        free = [i for i in range(number_of - 1) if holding[i] < most]
        pool, remaining = sum([loads[i] for i in free]), spare
        for i in free:
            more = min(most - holding[i], max(1, remaining * loads[i] // pool), spare)
            holding[i] = holding[i] + more
            spare = spare - more
    return np.array([most] + holding)


def ragged(key, number_of, total, limit, slope):
    if number_of == 2:
        one = jax.random.randint(key, (), max(1, total - limit), min(limit, total - 1) + 1)
        return jnp.stack([one, total - one])
    sizes = jnp.asarray(profile(number_of, total, limit, slope), jnp.int32)
    twos = (number_of - 1) // 2
    giver, taker = sizes[1:1 + 2 * twos:2], sizes[2:2 + 2 * twos:2]
    slack = jnp.minimum(giver - 1, limit - taker)
    shifted = jax.random.randint(jax.random.fold_in(key, 1), (twos,), 0, 1 << 20) % (slack + 1)
    sizes = sizes.at[1:1 + 2 * twos:2].set(giver - shifted).at[2:2 + 2 * twos:2].set(taker + shifted)
    return sizes[jax.random.permutation(jax.random.fold_in(key, 2), number_of)]


def bell_draw(stream_key, dims, scale, reach, shards=(), kind=jnp.bfloat16):
    values = scale * jax.random.normal(stream_key, dims, jnp.float32)
    if shards:
        values = values * block_scale(stream_key, dims, shards, -0.22, 0.18)
    return jnp.clip(values, -reach, reach).astype(kind)


def gaussian_with(own_key, shape, width, most, split, heavy, kind=jnp.bfloat16):
    values = width * jax.random.normal(own_key, shape, jnp.float32)
    if split:
        values = values * block_scale(own_key, shape, split, -0.22, 0.18)
    return jnp.clip(strengthened(values, jax.random.fold_in(own_key, 3), *heavy), -most, most).astype(kind)


def setup_inputs(seed: int = 0) -> dict:
    key_list = jax.random.split(jax.random.key(seed), 27)
    tokens = gaussian_with(key_list[0], (SEQS, LEN, D), 1.0, 6.0, ((0, 2), (1, 16)), (1, 2, 16, 2.0))
    segment_ids = jax.vmap(lambda own: jnp.searchsorted(jnp.cumsum(ragged(own, DOCS, LEN, DOC_MOST, 2)), jnp.arange(LEN), side="right"))(jax.random.split(key_list[1], SEQS)).reshape((SEQS, LEN)).astype(jnp.int32)
    gain_attn = jnp.clip(1.0 + 0.1 * jax.random.normal(key_list[2], (D,), jnp.float32), 0.5, 1.5)
    gain_mlp = jnp.clip(1.0 + 0.1 * jax.random.normal(key_list[3], (D,), jnp.float32), 0.5, 1.5)
    query_matrix = bell_draw(key_list[4], (D, HEADS * HD), D ** -0.5, 0.125, ((0, 16),))
    key_matrix = bell_draw(key_list[5], (D, HD), D ** -0.5, 0.125, ((0, 16),))
    value_matrix = bell_draw(key_list[6], (D, HD), D ** -0.5, 0.125, ((0, 16),))
    output_matrix = bell_draw(key_list[7], (HEADS * HD, D), (max(1, HEADS * HD * 32 // (TOK_DEV * N_FSDP))) ** -0.5, 1.0, ((0, 16),))
    gate_matrix = bell_draw(key_list[8], (FF, D), D ** -0.5, 0.125, ((0, 16),))
    upward_matrix = bell_draw(key_list[9], (FF, D), D ** -0.5, 0.125, ((0, 16),))
    down_matrix = bell_draw(key_list[10], (FF, D), FF ** -0.5, 0.046875, ((0, 16),))
    query_factor_first = bell_draw(key_list[11], (D, RANK), D ** -0.5, 0.125)
    query_factor_second = bell_draw(key_list[12], (RANK, HEADS * HD), (4 * RANK) ** -0.5, 0.1875)
    key_factor_first = bell_draw(key_list[13], (D, RANK), D ** -0.5, 0.125)
    key_factor_second = bell_draw(key_list[14], (RANK, HD), (4 * RANK) ** -0.5, 0.1875)
    value_factor_first = bell_draw(key_list[15], (D, RANK), D ** -0.5, 0.125)
    value_factor_second = bell_draw(key_list[16], (RANK, HD), (4 * RANK) ** -0.5, 0.1875)
    output_factor_first = bell_draw(key_list[17], (HEADS * HD, RANK), (max(1, HEADS * HD * 32 // (TOK_DEV * N_FSDP))) ** -0.5, 1.0)
    output_factor_second = bell_draw(key_list[18], (RANK, D), (4 * RANK) ** -0.5, 0.1875)
    gate_factor_first = bell_draw(key_list[19], (D, RANK), D ** -0.5, 0.125)
    gate_factor_second = bell_draw(key_list[20], (RANK, FF), (4 * RANK) ** -0.5, 0.1875)
    upward_factor_first = bell_draw(key_list[21], (D, RANK), D ** -0.5, 0.125)
    upward_factor_second = bell_draw(key_list[22], (RANK, FF), (4 * RANK) ** -0.5, 0.1875)
    down_factor_first = bell_draw(key_list[23], (FF, RANK), FF ** -0.5, 0.046875)
    down_factor_second = bell_draw(key_list[24], (RANK, D), (4 * RANK) ** -0.5, 0.1875)
    cotangent = bell_draw(key_list[25], (SEQS, LEN, D), 1.0, 6.0, ((0, 2), (1, 16)))
    return dict(tokens=tokens, segment_ids=segment_ids, gain_attn=gain_attn, gain_mlp=gain_mlp, query_matrix=query_matrix, key_matrix=key_matrix, value_matrix=value_matrix, output_matrix=output_matrix, gate_matrix=gate_matrix, upward_matrix=upward_matrix, down_matrix=down_matrix, query_factor_first=query_factor_first, query_factor_second=query_factor_second, key_factor_first=key_factor_first, key_factor_second=key_factor_second, value_factor_first=value_factor_first, value_factor_second=value_factor_second, output_factor_first=output_factor_first, output_factor_second=output_factor_second, gate_factor_first=gate_factor_first, gate_factor_second=gate_factor_second, upward_factor_first=upward_factor_first, upward_factor_second=upward_factor_second, down_factor_first=down_factor_first, down_factor_second=down_factor_second, cotangent=cotangent)


EPS = 1e-06

@jax.custom_vjp
def reduced_precision(v):
    return lax.optimization_barrier(v.astype(jnp.bfloat16)).astype(jnp.float32)

@jax.custom_vjp
def reduced_backward(v):
    return v

def low_keep(v):
    return (reduced_precision(v), None)

def low_pass(kept, grad):
    return (grad,)

def back_keep(v):
    return (v, None)

def back_low(kept, grad):
    return (reduced_precision(grad),)
reduced_precision.defvjp(low_keep, low_pass)
reduced_backward.defvjp(back_keep, back_low)

def precise_format(left, right):
    return jnp.dot(left, right, precision=lax.Precision.HIGHEST, preferred_element_type=jnp.float32)

def rms_norm(values, gain):
    factor = lax.rsqrt(lax.optimization_barrier(jnp.mean(values * values, axis=-1, keepdims=True)) + EPS)
    return values * factor * gain

def rotate(values, cosines, sines):
    half = values.shape[-1] // 2
    first = values[..., :half]
    second = values[..., half:]
    return jnp.concatenate([first * cosines - second * sines, second * cosines + first * sines], axis=-1)

def doc_positions(segments):
    length = segments.shape[0]
    index = jnp.arange(length, dtype=jnp.int32)
    starts = jnp.concatenate([jnp.ones((1,), dtype=bool), segments[1:] != segments[:-1]])
    first = lax.cummax(jnp.where(starts, index, jnp.zeros_like(index)), axis=0)
    return index - first

def attend(query, keys, values, segments):
    length = keys.shape[0]
    block = min(512, length)
    scale = HD ** (-0.5)
    key_index = jnp.arange(length, dtype=jnp.int32)

    def one_block(start):
        query_block = lax.dynamic_slice_in_dim(query, start, block, 0)
        seg_block = lax.dynamic_slice_in_dim(segments, start, block, 0)
        raw = jnp.einsum('thd,kd->thk', query_block, keys, precision=lax.Precision.HIGHEST)
        raw = reduced_backward(raw)
        query_index = start + jnp.arange(block, dtype=jnp.int32)
        allowed = (seg_block[:, None] == segments[None, :]) & (key_index[None, :] <= query_index[:, None])
        logits = jnp.where(allowed[:, None, :], raw * scale, -1e+30)
        top = lax.optimization_barrier(jnp.max(logits, axis=-1, keepdims=True))
        weights = jnp.exp(logits - top)
        probs = weights / lax.optimization_barrier(jnp.sum(weights, axis=-1, keepdims=True))
        return jnp.einsum('thk,kd->thd', reduced_precision(probs), values, precision=lax.Precision.HIGHEST)
    starts = jnp.arange(0, length, block, dtype=jnp.int32)
    blocks = lax.map(jax.checkpoint(one_block), starts)
    return blocks.reshape(length, query.shape[1], query.shape[2])

def layer(input_rows, segments, params):
    gain_attn, gain_mlp, query_matrix, key_matrix, value_matrix, output_matrix, gate_matrix, upward_matrix, down_matrix, query_factor_first, query_factor_second, key_factor_first, key_factor_second, value_factor_first, value_factor_second, output_factor_first, output_factor_second, gate_factor_first, gate_factor_second, upward_factor_first, upward_factor_second, down_factor_first, down_factor_second = params
    length = input_rows.shape[0]
    positions = doc_positions(segments)
    half = HD // 2
    inverse = 10000.0 ** (-(jnp.arange(half, dtype=jnp.float32) * 2.0 / HD))
    angles = positions.astype(jnp.float32)[:, None] * inverse[None, :]
    cosines = jnp.cos(angles)
    sines = jnp.sin(angles)
    attention_input = reduced_precision(rms_norm(input_rows, gain_attn))
    query_adapter = reduced_precision(reduced_backward(precise_format(attention_input, query_factor_first)))
    key_adapter = reduced_precision(reduced_backward(precise_format(attention_input, key_factor_first)))
    value_adapter = reduced_precision(reduced_backward(precise_format(attention_input, value_factor_first)))
    query_linear = reduced_backward(precise_format(attention_input, query_matrix) + precise_format(query_adapter, query_factor_second))
    key_linear = reduced_backward(precise_format(attention_input, key_matrix) + precise_format(key_adapter, key_factor_second))
    value_reduced = reduced_precision(reduced_backward(precise_format(attention_input, value_matrix) + precise_format(value_adapter, value_factor_second)))
    query_rot = reduced_precision(rotate(query_linear.reshape(length, HEADS, HD), cosines[:, None, :], sines[:, None, :]))
    key_rot = reduced_precision(rotate(key_linear, cosines, sines))
    attention_result = reduced_precision(reduced_backward(attend(query_rot, key_rot, value_reduced, segments).reshape(length, HEADS * HD)))
    output_adapter = reduced_precision(reduced_backward(precise_format(attention_result, output_factor_first)))
    attention_branch = reduced_backward(precise_format(attention_result, output_matrix) + precise_format(output_adapter, output_factor_second))
    residual_stream = input_rows + attention_branch
    perceptron_input = reduced_precision(rms_norm(residual_stream, gain_mlp))
    gate_adapter = reduced_precision(reduced_backward(precise_format(perceptron_input, gate_factor_first)))
    upward_adapter = reduced_precision(reduced_backward(precise_format(perceptron_input, upward_factor_first)))
    gate_activation = reduced_backward(precise_format(perceptron_input, gate_matrix.T) + precise_format(gate_adapter, gate_factor_second))
    upper_bound = reduced_backward(precise_format(perceptron_input, upward_matrix.T) + precise_format(upward_adapter, upward_factor_second))
    hidden_activated_value = reduced_precision(jax.nn.gelu(gate_activation, approximate=True) * upper_bound)
    down_lowrank_adapter = reduced_precision(reduced_backward(precise_format(hidden_activated_value, down_factor_first)))
    perceptron_branch = reduced_backward(precise_format(hidden_activated_value, down_matrix) + precise_format(down_lowrank_adapter, down_factor_second))
    return residual_stream + perceptron_branch

def reference(tokens, segment_ids, gain_attn, gain_mlp, query_matrix, key_matrix, value_matrix, output_matrix, gate_matrix, upward_matrix, down_matrix, query_factor_first, query_factor_second, key_factor_first, key_factor_second, value_factor_first, value_factor_second, output_factor_first, output_factor_second, gate_factor_first, gate_factor_second, upward_factor_first, upward_factor_second, down_factor_first, down_factor_second, cotangent):
    params = tuple((item.astype(jnp.float32) for item in (gain_attn, gain_mlp, query_matrix, key_matrix, value_matrix, output_matrix, gate_matrix, upward_matrix, down_matrix, query_factor_first, query_factor_second, key_factor_first, key_factor_second, value_factor_first, value_factor_second, output_factor_first, output_factor_second, gate_factor_first, gate_factor_second, upward_factor_first, upward_factor_second, down_factor_first, down_factor_second)))
    input_rows = tokens.astype(jnp.float32)

    def forward(values, weights):

        def one_sequence(pair):
            return layer(pair[0], pair[1], weights)
        return lax.map(jax.checkpoint(one_sequence), (values, segment_ids))
    result, pullback = jax.vjp(forward, input_rows, params)
    grad_inputs, grads = pullback(cotangent.astype(jnp.float32))
    g_gain_attn, g_gain_mlp, g_query_weight, g_key_weight, g_value_weight, g_output_weight, g_gate_weight, g_up_weight, g_down_weight, g_query_in, g_query_out, g_key_in, g_key_out, g_value_in, g_value_out, g_output_in, g_output_out, g_gate_in, g_gate_out, g_up_in, g_up_out, g_down_in, g_down_out = grads
    return (result.astype(jnp.bfloat16), grad_inputs, g_gain_attn, g_gain_mlp, g_query_weight, g_key_weight, g_value_weight, g_output_weight, g_gate_weight, g_up_weight, g_down_weight, g_query_in, g_query_out, g_key_in, g_key_out, g_value_in, g_value_out, g_output_in, g_output_out, g_gate_in, g_gate_out, g_up_in, g_up_out, g_down_in, g_down_out)
```

```python
import jax
import jax.numpy as jnp
from jax import lax
from jax.sharding import PartitionSpec as P

EPS = 1e-06


def matrix_product(left, right):
    return jnp.dot(left, right, preferred_element_type=jnp.float32)


def left_matrix_product(left, right):
    return lax.dot_general(
        left, right, (((0,), (0,)), ((), ())), preferred_element_type=jnp.float32
    )


def right_product(left, right):
    return lax.dot_general(
        left, right, (((1,), (1,)), ((), ())), preferred_element_type=jnp.float32
    )


def rms_norm(values, gain):
    factor = lax.rsqrt(jnp.mean(values * values, axis=-1, keepdims=True) + EPS)
    return values * factor * gain


def rotate(values, cosines, sines):
    half = values.shape[-1] // 2
    first = values[..., :half]
    second = values[..., half:]
    return jnp.concatenate(
        [first * cosines - second * sines, second * cosines + first * sines], axis=-1
    )


def doc_positions(segments):
    length = segments.shape[0]
    index = jnp.arange(length, dtype=jnp.int32)
    starts = jnp.concatenate([jnp.ones((1,), dtype=bool), segments[1:] != segments[:-1]])
    first = lax.cummax(jnp.where(starts, index, jnp.zeros_like(index)), axis=0)
    return index - first


def geglu(gate, up):
    return jax.nn.gelu(gate, approximate=True) * up


def gather_shared(first, second, core):
    own = jnp.where(core == 0, first, second)
    gathered = lax.all_gather(own, "fsdp", axis=0, tiled=True)
    return gathered, lax.ppermute(gathered, "dp", [(0, 1), (1, 0)])


def scatter_shared(terms, core):
    half = terms.shape[2] // 2
    swap = [(0, 1), (1, 0)]
    own = lax.dynamic_slice_in_dim(terms, core * half, half, 2)
    away = lax.dynamic_slice_in_dim(terms, (1 - core) * half, half, 2)
    both = own + lax.ppermute(away, "dp", swap)
    mine = lax.psum_scatter(both, "fsdp", scatter_dimension=0, tiled=False)
    theirs = lax.ppermute(mine, "dp", swap)
    return jnp.where(
        core == 0,
        jnp.concatenate([mine, theirs], axis=1),
        jnp.concatenate([theirs, mine], axis=1),
    )


def local(
    tokens,
    segment_ids,
    gain_attn,
    gain_mlp,
    query_matrix,
    key_matrix,
    value_matrix,
    output_matrix,
    gate_matrix,
    upward_matrix,
    down_matrix,
    query_factor_first,
    query_factor_second,
    key_factor_first,
    key_factor_second,
    value_factor_first,
    value_factor_second,
    output_factor_first,
    output_factor_second,
    gate_factor_first,
    gate_factor_second,
    upward_factor_first,
    upward_factor_second,
    down_factor_first,
    down_factor_second,
    cotangent,
):
    bf16 = jnp.bfloat16
    f32 = jnp.float32
    tok_rows = tokens.shape[1]
    width = tokens.shape[2]
    length = segment_ids.shape[1]
    head_size = key_matrix.shape[1]
    heads = query_matrix.shape[1] // head_size
    unit_rows = gate_matrix.shape[0]
    in_rows = query_matrix.shape[0]
    shards = length // tok_rows
    rank = query_factor_first.shape[1]
    place = lax.axis_index("fsdp")
    core = lax.axis_index("dp")
    offset = place * tok_rows
    input_rows = tokens[0].astype(f32)
    seg_all = segment_ids[0]
    seg_own = lax.dynamic_slice_in_dim(seg_all, offset, tok_rows, 0)
    positions = lax.dynamic_slice_in_dim(doc_positions(seg_all), offset, tok_rows, 0)
    half = head_size // 2
    inverse = 10000.0 ** (-(jnp.arange(half, dtype=f32) * 2.0 / head_size))
    angles = positions.astype(f32)[:, None] * inverse[None, :]
    cosines = jnp.cos(angles)
    sines = jnp.sin(angles)

    def merged_rows(matrix, first, second):
        rows = lax.dynamic_slice_in_dim(first, place * in_rows, in_rows, 0)
        return (matrix.astype(f32) + matrix_product(rows, second)).astype(bf16)

    own_first = jnp.concatenate(
        [
            merged_rows(query_matrix, query_factor_first, query_factor_second),
            merged_rows(key_matrix, key_factor_first, key_factor_second),
        ],
        axis=1,
    )
    own_second = jnp.concatenate(
        [
            merged_rows(output_matrix, output_factor_first, output_factor_second),
            merged_rows(value_matrix, value_factor_first, value_factor_second),
        ],
        axis=1,
    )
    gathered, other = gather_shared(own_first, own_second, core)
    query_key = jnp.where(core == 0, gathered, other)
    output_value = jnp.where(core == 0, other, gathered)
    query_weight = query_key[:, : heads * head_size]
    key_weight = query_key[:, heads * head_size :]
    output_weight = output_value[:, :width]
    value_weight = output_value[:, width:]

    cot_own = cotangent[0]
    cot_all = lax.all_gather(cot_own, "fsdp", axis=0, tiled=True)

    normed_attn, pull_attn = jax.vjp(rms_norm, input_rows, gain_attn)
    attn_in = normed_attn.astype(bf16)
    query_lin = matrix_product(attn_in, query_weight)
    key_lin = matrix_product(attn_in, key_weight)
    value = matrix_product(attn_in, value_weight).astype(bf16)
    query = rotate(
        query_lin.reshape(tok_rows, heads, head_size), cosines[:, None, :], sines[:, None, :]
    ).astype(bf16)
    key = rotate(key_lin, cosines, sines).astype(bf16)
    key_value = lax.all_gather(
        jnp.concatenate([key, value], axis=1), "fsdp", axis=0, tiled=True
    )
    keys_all = key_value[:, :head_size]
    values_all = key_value[:, head_size:]
    block = min(512, length)
    scale = head_size ** (-0.5)
    query_index = offset + jnp.arange(tok_rows, dtype=jnp.int32)
    needed = (offset + tok_rows + block - 1) // block
    first_block = (offset - positions[0]) // block

    def scores_of(start):
        key_block = lax.dynamic_slice_in_dim(keys_all, start, block, 0)
        value_block = lax.dynamic_slice_in_dim(values_all, start, block, 0)
        seg_block = lax.dynamic_slice_in_dim(seg_all, start, block, 0)
        key_index = start + jnp.arange(block, dtype=jnp.int32)
        allowed = (seg_own[:, None] == seg_block[None, :]) & (
            key_index[None, :] <= query_index[:, None]
        )
        allowed = allowed[:, None, :]
        raw = jnp.einsum("thd,kd->thk", query, key_block, preferred_element_type=f32)
        return (jnp.where(allowed, raw * scale, -1e30), allowed, key_block, value_block)

    def max_step(index, carry):
        top, total = carry
        logits, allowed, key_block, value_block = scores_of(index * block)
        new_top = jnp.maximum(top, jnp.max(logits, axis=-1, keepdims=True))
        weights = jnp.where(allowed, jnp.exp(logits - new_top), 0.0)
        return (new_top, total * jnp.exp(top - new_top) + jnp.sum(weights, axis=-1, keepdims=True))

    start_top = jnp.full((tok_rows, heads, 1), -1e30, f32)
    start_total = jnp.zeros((tok_rows, heads, 1), f32)
    top, total = lax.fori_loop(first_block, needed, max_step, (start_top, start_total))
    log_total = top + jnp.log(total)

    def probs_of(start):
        logits, allowed, key_block, value_block = scores_of(start)
        return (jnp.where(allowed, jnp.exp(logits - log_total), 0.0), key_block, value_block)

    def out_step(index, acc):
        probs, key_block, value_block = probs_of(index * block)
        return acc + jnp.einsum(
            "thk,kd->thd", probs.astype(bf16), value_block, preferred_element_type=f32
        )

    attn_raw = lax.fori_loop(
        first_block, needed, out_step, jnp.zeros((tok_rows, heads, head_size), f32)
    )
    attn = attn_raw.reshape(tok_rows, heads * head_size).astype(bf16)
    resid = input_rows + matrix_product(attn, output_weight)
    normed_mlp, pull_mlp = jax.vjp(rms_norm, resid, gain_mlp)
    mlp_in = normed_mlp.astype(bf16)
    mlp_all = lax.all_gather(mlp_in, "fsdp", axis=0, tiled=True)

    first_unit = place * unit_rows
    gate_second = lax.dynamic_slice_in_dim(gate_factor_second, first_unit, unit_rows, 1)
    up_second = lax.dynamic_slice_in_dim(upward_factor_second, first_unit, unit_rows, 1)
    down_first = lax.dynamic_slice_in_dim(down_factor_first, first_unit, unit_rows, 0)

    def merged_units(matrix, first, second):
        low = lax.dot_general(
            second, first, (((0,), (1,)), ((), ())), preferred_element_type=f32
        )
        return (matrix.astype(f32) + low).astype(bf16)

    gate_weight = merged_units(gate_matrix, gate_factor_first, gate_second)
    up_weight = merged_units(upward_matrix, upward_factor_first, up_second)
    down_weight = (
        down_matrix.astype(f32) + matrix_product(down_first, down_factor_second)
    ).astype(bf16)

    gate = right_product(mlp_all, gate_weight)
    up = right_product(mlp_all, up_weight)
    hidden_full, pull_geglu = jax.vjp(geglu, gate, up)
    hidden = hidden_full.astype(bf16)
    down_sum = lax.psum_scatter(
        matrix_product(hidden, down_weight).astype(bf16), "fsdp", scatter_dimension=0, tiled=True
    )
    grad_hidden = right_product(cot_all, down_weight)
    grad_gate_full, grad_up_full = pull_geglu(grad_hidden)
    grad_gate = grad_gate_full.astype(bf16)
    grad_up = grad_up_full.astype(bf16)
    grad_mlp_in = lax.psum_scatter(
        (matrix_product(grad_gate, gate_weight) + matrix_product(grad_up, up_weight)).astype(bf16),
        "fsdp",
        scatter_dimension=0,
        tiled=True,
    ).astype(f32)
    gate_rows = left_matrix_product(grad_gate, mlp_all)
    up_rows = left_matrix_product(grad_up, mlp_all)
    down_rows = left_matrix_product(hidden, cot_all)
    gate_rows_low = gate_rows.astype(bf16)
    up_rows_low = up_rows.astype(bf16)
    down_rows_low = down_rows.astype(bf16)
    swap = [(0, 1), (1, 0)]
    g_gate_rows = gate_rows + lax.ppermute(gate_rows_low, "dp", swap).astype(f32)
    g_up_rows = up_rows + lax.ppermute(up_rows_low, "dp", swap).astype(f32)
    g_down_rows = down_rows + lax.ppermute(down_rows_low, "dp", swap).astype(f32)

    def columns_of(first, rows):
        return lax.dot_general(
            first, rows.astype(bf16), (((0,), (1,)), ((), ())), preferred_element_type=f32
        )

    g_gate_out = columns_of(gate_factor_first, g_gate_rows)
    g_up_out = columns_of(upward_factor_first, g_up_rows)
    g_down_in = right_product(g_down_rows.astype(bf16), down_factor_second)
    gate_in_term = lax.dot_general(
        gate_rows_low, gate_second, (((0,), (1,)), ((), ())), preferred_element_type=f32
    )
    up_in_term = lax.dot_general(
        up_rows_low, up_second, (((0,), (1,)), ((), ())), preferred_element_type=f32
    )
    down_out_term = left_matrix_product(down_first, down_rows_low)

    output = (resid + down_sum.astype(f32)).astype(bf16)
    grad_resid_norm, gain_mlp_term = pull_mlp(grad_mlp_in)
    grad_resid = cot_own.astype(f32) + grad_resid_norm
    grad_branch = grad_resid.astype(bf16)
    grad_attn = right_product(grad_branch, output_weight).astype(bf16)
    lora_output = matrix_product(attn, output_factor_first).astype(bf16)
    lora_query = matrix_product(attn_in, query_factor_first).astype(bf16)
    lora_key = matrix_product(attn_in, key_factor_first).astype(bf16)
    lora_value = matrix_product(attn_in, value_factor_first).astype(bf16)
    grad_attn_heads = grad_attn.reshape(tok_rows, heads, head_size)
    delta = jnp.sum(
        grad_attn_heads.astype(f32) * attn_raw, axis=-1, keepdims=True
    )

    def grad_step(index, carry):
        grad_query_acc, key_terms = carry
        start = index * block
        probs, key_block, value_block = probs_of(start)
        grad_probs = jnp.einsum(
            "thd,kd->thk", grad_attn_heads, value_block, preferred_element_type=f32
        )
        grad_scores = (scale * probs * (grad_probs - delta)).astype(bf16)
        grad_query_acc = grad_query_acc + jnp.einsum(
            "thk,kd->thd", grad_scores, key_block, preferred_element_type=f32
        )
        key_part = jnp.einsum("thk,thd->kd", grad_scores, query, preferred_element_type=f32)
        value_part = jnp.einsum(
            "thk,thd->kd", probs.astype(bf16), grad_attn_heads, preferred_element_type=f32
        )
        both = jnp.concatenate([key_part, value_part], axis=1).astype(bf16)
        key_terms = lax.dynamic_update_slice_in_dim(key_terms, both, start, 0)
        return (grad_query_acc, key_terms)

    grad_query_rot, key_terms = lax.fori_loop(
        first_block,
        needed,
        grad_step,
        (
            jnp.zeros((tok_rows, heads, head_size), f32),
            jnp.zeros((length, 2 * head_size), bf16),
        ),
    )
    key_sums = lax.psum_scatter(key_terms, "fsdp", scatter_dimension=0, tiled=True).astype(f32)
    grad_query_lin = (
        rotate(grad_query_rot, cosines[:, None, :], -sines[:, None, :])
        .reshape(tok_rows, heads * head_size)
        .astype(bf16)
    )
    grad_key_lin = rotate(key_sums[:, :head_size], cosines, -sines).astype(bf16)
    grad_value_lin = key_sums[:, head_size:].astype(bf16)
    grad_attn_in = (
        right_product(grad_query_lin, query_weight)
        + right_product(grad_key_lin, key_weight)
        + right_product(grad_value_lin, value_weight)
    )
    grad_inputs_norm, gain_attn_term = pull_attn(grad_attn_in)
    grad_inputs = grad_resid + grad_inputs_norm

    def low_term(left, right):
        return left_matrix_product(left, right).astype(bf16)

    per = in_rows
    few = rank // shards
    narrow = jnp.concatenate(
        [
            low_term(attn_in, grad_key_lin),
            low_term(attn_in, grad_value_lin),
            gate_in_term.astype(bf16),
            up_in_term.astype(bf16),
        ],
        axis=1,
    ).reshape(shards, 2, per // 2, 4 * head_size)
    tiny = jnp.concatenate(
        [
            low_term(lora_key, grad_key_lin).reshape(shards, few, head_size),
            low_term(lora_value, grad_value_lin).reshape(shards, few, head_size),
            gain_attn_term.astype(bf16).reshape(shards, few, -1),
            gain_mlp_term.astype(bf16).reshape(shards, few, -1),
        ],
        axis=2,
    )
    tiny = jnp.pad(tiny, ((0, 0), (0, 0), (0, width - tiny.shape[2])))
    terms = jnp.concatenate(
        [
            low_term(attn_in, grad_query_lin).reshape(shards, per, width),
            low_term(attn, grad_branch).reshape(shards, per, width),
            low_term(lora_query, grad_query_lin).reshape(shards, few, width),
            low_term(lora_output, grad_branch).reshape(shards, few, width),
            down_out_term.astype(bf16).reshape(shards, few, width),
            jnp.concatenate([narrow[:, 0], narrow[:, 1]], axis=2),
            tiny,
        ],
        axis=1,
    )
    sums = scatter_shared(terms, core).astype(f32)
    at = [0]

    def take(rows):
        at[0] += rows
        return sums[at[0] - rows : at[0]]

    g_query_weight = take(per)
    g_output_weight = take(per)
    g_query_out = take(few)
    g_output_out = take(few)
    g_down_out = take(few)
    pair = take(per // 2)
    pair = jnp.concatenate([pair[:, : width // 2], pair[:, width // 2 :]], axis=0)
    g_key_weight = pair[:, :head_size]
    g_value_weight = pair[:, head_size : 2 * head_size]
    g_gate_in = pair[:, 2 * head_size : 3 * head_size]
    g_up_in = pair[:, 3 * head_size :]
    last = take(few)
    g_key_out = last[:, :head_size]
    g_value_out = last[:, head_size : 2 * head_size]
    each = per // few
    g_gain_attn = last[:, 2 * head_size : 2 * head_size + each].reshape(per)
    g_gain_mlp = last[:, 2 * head_size + each : 2 * head_size + 2 * each].reshape(per)
    g_query_in = right_product(g_query_weight.astype(bf16), query_factor_second)
    g_output_in = right_product(g_output_weight.astype(bf16), output_factor_second)
    g_key_in = right_product(g_key_weight.astype(bf16), key_factor_second)
    g_value_in = right_product(g_value_weight.astype(bf16), value_factor_second)
    return (
        output[None],
        grad_inputs[None],
        g_gain_attn,
        g_gain_mlp,
        g_query_weight,
        g_key_weight,
        g_value_weight,
        g_output_weight,
        g_gate_rows,
        g_up_rows,
        g_down_rows,
        g_query_in,
        g_query_out,
        g_key_in,
        g_key_out,
        g_value_in,
        g_value_out,
        g_output_in,
        g_output_out,
        g_gate_in,
        g_gate_out,
        g_up_in,
        g_up_out,
        g_down_in,
        g_down_out,
    )


def solution(mesh):
    in_specs = (
        P("dp", "fsdp", None),
        P("dp", None),
        P(),
        P(),
        P("fsdp", None),
        P("fsdp", None),
        P("fsdp", None),
        P("fsdp", None),
        P("fsdp", None),
        P("fsdp", None),
        P("fsdp", None),
        P(),
        P(),
        P(),
        P(),
        P(),
        P(),
        P(),
        P(),
        P(),
        P(),
        P(),
        P(),
        P(),
        P(),
        P("dp", "fsdp", None),
    )
    out_specs = (
        P("dp", "fsdp", None),
        P("dp", "fsdp", None),
        P("fsdp"),
        P("fsdp"),
        P("fsdp", None),
        P("fsdp", None),
        P("fsdp", None),
        P("fsdp", None),
        P("fsdp", None),
        P("fsdp", None),
        P("fsdp", None),
        P("fsdp", None),
        P("fsdp", None),
        P("fsdp", None),
        P("fsdp", None),
        P("fsdp", None),
        P("fsdp", None),
        P("fsdp", None),
        P("fsdp", None),
        P("fsdp", None),
        P(None, "fsdp"),
        P("fsdp", None),
        P(None, "fsdp"),
        P("fsdp", None),
        P("fsdp", None),
    )
    return jax.shard_map(local, mesh=mesh, in_specs=in_specs, out_specs=out_specs, check_vma=False)
```

```python
import functools

import jax
import jax.numpy as jnp
from jax import lax
from jax.experimental import pallas as pl
from jax.experimental.pallas import tpu as pltpu
from jax.sharding import PartitionSpec as P

EPS = 1e-06
MESH = pl.DeviceIdType.MESH
LINE = 4


def matrix_product(left, right):
    return jnp.dot(left, right, preferred_element_type=jnp.float32)


def left_matrix_product(left, right):
    return lax.dot_general(
        left, right, (((0,), (0,)), ((), ())), preferred_element_type=jnp.float32
    )


def right_product(left, right):
    return lax.dot_general(
        left, right, (((1,), (1,)), ((), ())), preferred_element_type=jnp.float32
    )


def rms_norm(values, gain):
    factor = lax.rsqrt(jnp.mean(values * values, axis=-1, keepdims=True) + EPS)
    return values * factor * gain


def rotate(values, cosines, sines):
    half = values.shape[-1] // 2
    first = values[..., :half]
    second = values[..., half:]
    return jnp.concatenate(
        [first * cosines - second * sines, second * cosines + first * sines], axis=-1
    )


def doc_positions(segments):
    length = segments.shape[0]
    index = jnp.arange(length, dtype=jnp.int32)
    starts = jnp.concatenate([jnp.ones((1,), dtype=bool), segments[1:] != segments[:-1]])
    first = lax.cummax(jnp.where(starts, index, jnp.zeros_like(index)), axis=0)
    return index - first


def geglu(gate, up):
    return jax.nn.gelu(gate, approximate=True) * up


def place_of():
    f = lax.axis_index("fsdp")
    z, y, x = f // 4, (f // 2) % 2, f % 2
    near_end = z // 2
    inner = (z + near_end) % 2
    visits = []
    for k in range(LINE):
        u = k + inner * (1 if k == 0 else -1 if k == 1 else 0)
        visits.append(u + near_end * (3 - 2 * u))
    return f, z, y, x, f + 1 - 2 * x, f + 2 - 4 * y, visits


def greet(f, z, fx, fy, with_core):
    barrier = pltpu.get_barrier_semaphore()

    def signal(target):
        pl.semaphore_signal(barrier, inc=1, device_id=target, device_id_type=MESH)

    signal({"fsdp": fx})
    signal({"fsdp": fy})
    if with_core:
        signal({"dp": 1 - lax.axis_index("dp")})

    @pl.when(z > 0)
    def _():
        signal({"fsdp": f - 4})

    @pl.when(z < LINE - 1)
    def _():
        signal({"fsdp": f + 4})

    peers = 3 if with_core else 2
    ends = jnp.where(z > 0, 1, 0) + jnp.where(z < LINE - 1, 1, 0)
    pl.semaphore_wait(barrier, peers + ends)


def send(source, target, send_sem, recv_sem, device):
    copy = pltpu.make_async_remote_copy(
        src_ref=source,
        dst_ref=target,
        send_sem=send_sem,
        recv_sem=recv_sem,
        device_id=device,
        device_id_type=MESH,
    )
    copy.start()
    return copy


def arrived(ref, sem):
    pltpu.make_async_copy(ref, ref, sem).wait()


def gather_kernel(pieces, count, with_core, *refs):
    ins, outs = refs[:count], refs[count : 2 * count]
    z_send, z_recv, a_send, a_recv, b_send, b_recv, own_sem, c_send, c_recv = refs[2 * count :]
    f, z, y, x, fx, fy, visits = place_of()
    core = lax.axis_index("dp")
    greet(f, z, fx, fy, with_core)

    def at(index, where, rows):
        ref = outs[index].at[where]
        if with_core:
            ref = ref.at[core]
        return ref.at[pl.ds(*rows)]

    own = []
    for i in range(count):
        target = outs[i].at[f, core] if with_core else outs[i].at[f]
        copy = pltpu.make_async_copy(ins[i], target, own_sem.at[i])
        copy.start()
        own.append(copy)
    sent = []

    def spread_z(p, k):
        index, rows, first = pieces[p]
        v = visits[k]
        where = v * 4 + y * 2 + x
        target = at(index, where, rows)
        if k > 0:
            arrived(target, z_recv.at[p, v])
        source = ins[index].at[pl.ds(*rows)] if k == 0 else target

        @pl.when((v <= z) & (z < LINE - 1))
        def _():
            send(source, target, z_send.at[p, k, 0], z_recv.at[p, v], {"fsdp": f + 4})

        @pl.when((v >= z) & (z > 0))
        def _():
            send(source, target, z_send.at[p, k, 1], z_recv.at[p, v], {"fsdp": f - 4})

        fa, fb = (fy, fx) if first == "y" else (fx, fy)
        sent.append(send(source, target, a_send.at[p, k], a_recv.at[p, k], {"fsdp": fa}))
        sent.append(send(source, target, b_send.at[p, k, 0], b_recv.at[p, k, 0], {"fsdp": fb}))

    def spread_a(p, k):
        index, rows, first = pieces[p]
        v = visits[k]
        where = v * 4 + (1 - y) * 2 + x if first == "y" else v * 4 + y * 2 + (1 - x)
        fb = fx if first == "y" else fy
        target = at(index, where, rows)
        arrived(target, a_recv.at[p, k])
        sent.append(send(target, target, b_send.at[p, k, 1], b_recv.at[p, k, 1], {"fsdp": fb}))

    def finish_b(p, k):
        index, rows, first = pieces[p]
        v = visits[k]
        if first == "y":
            spots = v * 4 + y * 2 + (1 - x), v * 4 + (1 - y) * 2 + (1 - x)
        else:
            spots = v * 4 + (1 - y) * 2 + x, v * 4 + (1 - y) * 2 + (1 - x)
        for j in range(2):
            arrived(at(index, spots[j], rows), b_recv.at[p, k, j])

    def swap(k):
        for i in range(count):
            block = outs[i].at[pl.ds(visits[k] * 4, 4), core]
            sent.append(
                send(block, block, c_send.at[i, k], c_recv.at[i, k], {"dp": 1 - core})
            )

    def swapped(k):
        for i in range(count):
            arrived(outs[i].at[pl.ds(visits[k] * 4, 4), 1 - core], c_recv.at[i, k])

    for k in range(LINE + 1):
        if k < LINE:
            for p in range(len(pieces)):
                spread_z(p, k)
        if k > 0:
            for p in range(len(pieces)):
                spread_a(p, k - 1)
    for copy in own:
        copy.wait()
    for k in range(LINE):
        for p in range(len(pieces)):
            finish_b(p, k)
        if with_core:
            swap(k)
    if with_core:
        for k in range(LINE):
            swapped(k)
    for copy in sent:
        copy.wait_send()
    for p in range(len(pieces)):
        index, rows, first = pieces[p]
        for k in range(LINE):
            v = visits[k]
            block = at(index, f, rows)

            @pl.when((v <= z) & (z < LINE - 1))
            def _():
                pltpu.make_async_copy(block, block, z_send.at[p, k, 0]).wait()

            @pl.when((v >= z) & (z > 0))
            def _():
                pltpu.make_async_copy(block, block, z_send.at[p, k, 1]).wait()


def gather_blocks(arrays, splits, with_core, number):
    shards = 4 * LINE
    pieces = []
    for index, parts in enumerate(splits):
        start = 0
        for rows, first in parts:
            pieces.append((index, (start, rows), first))
            start += rows
    lead = (shards, 2) if with_core else (shards,)
    amount = len(pieces)
    dma = pltpu.SemaphoreType.DMA
    outs = pl.pallas_call(
        functools.partial(gather_kernel, pieces, len(arrays), with_core),
        out_shape=[jax.ShapeDtypeStruct(lead + a.shape, a.dtype) for a in arrays],
        in_specs=[pl.BlockSpec(memory_space=pltpu.VMEM)] * len(arrays),
        out_specs=[pl.BlockSpec(memory_space=pl.ANY)] * len(arrays),
        scratch_shapes=[
            dma((amount, LINE, 2)),
            dma((amount, LINE)),
            dma((amount, LINE)),
            dma((amount, LINE)),
            dma((amount, LINE, 2)),
            dma((amount, LINE, 2)),
            dma((len(arrays),)),
            dma((len(arrays), LINE)),
            dma((len(arrays), LINE)),
        ],
        compiler_params=pltpu.CompilerParams(collective_id=number, has_side_effects=True),
        name="gather_blocks_%d" % number,
    )(*arrays)
    return [o.reshape((-1, o.shape[-1])) for o in outs]


def bit_orders(bits):
    rest = list(range(min(bits, 3), bits))
    first = list(range(min(bits, 3)))
    return [first[i % len(first) :] + first[: i % len(first)] + rest for i in range(3)]


def halving_sum(terms, order, place, with_core=False):
    shards = terms.shape[0]
    bits = shards.bit_length() - 1
    current = terms.reshape((2,) * bits + terms.shape[1:])
    left = list(range(bits))[::-1]
    steps = [("fsdp", b) for b in order]
    if with_core:
        steps = [("dp", None)] + steps
    for axis, b in steps:
        if axis == "dp":
            where, mine = bits, lax.axis_index("dp")
            pairs = [(0, 1), (1, 0)]
        else:
            where, mine = left.index(b), (place >> b) & 1
            pairs = [(i, i ^ (1 << b)) for i in range(shards)]
            left.remove(b)
        away = lax.dynamic_index_in_dim(current, 1 - mine, where, keepdims=False)
        keep = lax.dynamic_index_in_dim(current, mine, where, keepdims=False)
        came = lax.ppermute(away, axis, pairs)
        total = keep.astype(jnp.float32) + came.astype(jnp.float32)
        current = total.astype(terms.dtype)
    return total


def scatter_rows(terms, place, shards):
    blocks = terms.reshape(shards, terms.shape[0] // shards, terms.shape[1])
    rows = blocks.shape[1]
    third = (rows * 3 // 8) // 16 * 16
    edges = [0, third, 2 * third, rows]
    orders = bit_orders(shards.bit_length() - 1)
    return jnp.concatenate(
        [halving_sum(blocks[:, edges[i] : edges[i + 1]], orders[i], place) for i in range(3)],
        axis=0,
    )


def scatter_both(big, small, place, core):
    shards, rows, columns = big.shape
    halves = big.reshape(shards, 2, 2, rows // 4, columns)
    streams = [halves[:, 0], halves[:, 1], small.reshape(shards, 2, -1, columns)]
    orders = bit_orders(shards.bit_length() - 1)
    mine = jnp.stack(
        [halving_sum(streams[i], orders[i], place, True).astype(big.dtype) for i in range(2)]
    )
    few = halving_sum(streams[2], orders[2], place, True).astype(big.dtype)
    swap = [(0, 1), (1, 0)]

    def both(own):
        other = lax.ppermute(own, "dp", swap)
        low = jnp.where(core == 0, own, other)
        high = jnp.where(core == 0, other, own)
        return jnp.stack([low, high], axis=-3).astype(jnp.float32)

    return both(mine).reshape(rows, columns), both(few).reshape(-1, columns)


def pack_rows(terms, shards, width):
    count = width // terms.shape[1]
    parts = terms.reshape(shards, count, -1, terms.shape[1])
    return jnp.concatenate([parts[:, i] for i in range(count)], axis=2)


def unpack_rows(terms, columns):
    count = terms.shape[1] // columns
    return jnp.concatenate(
        [terms[:, i * columns : (i + 1) * columns] for i in range(count)], axis=0
    )


def gather_weights(query, output, key_value, shards):
    if shards == 4 * LINE:
        rows = query.shape[0]
        return gather_blocks(
            [query, output, key_value],
            [[(rows, "y")], [(rows, "x")], [(rows // 2, "y"), (rows // 2, "x")]],
            True,
            1,
        )

    def whole(own):
        return lax.all_gather(own, ("fsdp", "dp"), axis=0, tiled=True)

    return whole(query), whole(output), whole(key_value)


def gather_rows(own, shards, number):
    if shards == 4 * LINE:
        half = own.shape[0] // 2
        return gather_blocks([own], [[(half, "y"), (half, "x")]], False, number)[0]
    return lax.all_gather(own, "fsdp", axis=0, tiled=True)


def local(
    tokens,
    segment_ids,
    gain_attn,
    gain_mlp,
    query_matrix,
    key_matrix,
    value_matrix,
    output_matrix,
    gate_matrix,
    upward_matrix,
    down_matrix,
    query_factor_first,
    query_factor_second,
    key_factor_first,
    key_factor_second,
    value_factor_first,
    value_factor_second,
    output_factor_first,
    output_factor_second,
    gate_factor_first,
    gate_factor_second,
    upward_factor_first,
    upward_factor_second,
    down_factor_first,
    down_factor_second,
    cotangent,
):
    bf16 = jnp.bfloat16
    f32 = jnp.float32
    tok_rows = tokens.shape[1]
    width = tokens.shape[2]
    length = segment_ids.shape[1]
    head_size = key_matrix.shape[1]
    heads = query_matrix.shape[1] // head_size
    unit_rows = gate_matrix.shape[0]
    in_rows = query_matrix.shape[0]
    shards = length // tok_rows
    rank = query_factor_first.shape[1]
    place = lax.axis_index("fsdp")
    core = lax.axis_index("dp")
    offset = place * tok_rows
    input_rows = tokens[0].astype(f32)
    seg_all = segment_ids[0]
    seg_own = lax.dynamic_slice_in_dim(seg_all, offset, tok_rows, 0)
    positions = lax.dynamic_slice_in_dim(doc_positions(seg_all), offset, tok_rows, 0)
    half = head_size // 2
    inverse = 10000.0 ** (-(jnp.arange(half, dtype=f32) * 2.0 / head_size))
    angles = positions.astype(f32)[:, None] * inverse[None, :]
    cosines = jnp.cos(angles)
    sines = jnp.sin(angles)

    core_rows = in_rows // 2

    def split_heads(values):
        return values.reshape(tok_rows, heads, head_size).transpose(1, 0, 2)

    def join_heads(values):
        return values.transpose(1, 0, 2).reshape(tok_rows, heads * head_size)

    def merged_rows(matrix, first, second):
        own = lax.dynamic_slice_in_dim(matrix, core * core_rows, core_rows, 0)
        rows = lax.dynamic_slice_in_dim(first, place * in_rows + core * core_rows, core_rows, 0)
        return (own.astype(f32) + matrix_product(rows, second)).astype(bf16)

    query_weight, output_weight, key_value_weight = gather_weights(
        merged_rows(query_matrix, query_factor_first, query_factor_second),
        merged_rows(output_matrix, output_factor_first, output_factor_second),
        jnp.concatenate(
            [
                merged_rows(key_matrix, key_factor_first, key_factor_second),
                merged_rows(value_matrix, value_factor_first, value_factor_second),
            ],
            axis=1,
        ),
        shards,
    )
    cot_own = cotangent[0]

    normed_attn, pull_attn = jax.vjp(rms_norm, input_rows, gain_attn)
    attn_in = normed_attn.astype(bf16)
    key_value_lin = matrix_product(attn_in, key_value_weight)
    key = rotate(key_value_lin[:, :head_size], cosines, sines).astype(bf16)
    value = key_value_lin[:, head_size:].astype(bf16)
    key_value = lax.all_gather(
        jnp.concatenate([key, value], axis=1), "fsdp", axis=0, tiled=True
    )
    query_lin = matrix_product(attn_in, query_weight)
    query = rotate(split_heads(query_lin), cosines[None], sines[None]).astype(bf16)
    keys_all = key_value[:, :head_size]
    values_all = key_value[:, head_size:]
    block = min(512, length)
    scale = head_size ** (-0.5)
    query_index = offset + jnp.arange(tok_rows, dtype=jnp.int32)
    needed = (offset + tok_rows + block - 1) // block
    first_block = (offset - positions[0]) // block

    def scores_of(start):
        key_block = lax.dynamic_slice_in_dim(keys_all, start, block, 0)
        value_block = lax.dynamic_slice_in_dim(values_all, start, block, 0)
        seg_block = lax.dynamic_slice_in_dim(seg_all, start, block, 0)
        key_index = start + jnp.arange(block, dtype=jnp.int32)
        allowed = (seg_own[:, None] == seg_block[None, :]) & (
            key_index[None, :] <= query_index[:, None]
        )
        allowed = allowed[None]
        raw = jnp.einsum("htd,kd->htk", query, key_block, preferred_element_type=f32)
        return (jnp.where(allowed, raw * scale, -1e30), allowed, key_block, value_block)

    def max_step(index, carry):
        top, total = carry
        logits, allowed, key_block, value_block = scores_of(index * block)
        new_top = jnp.maximum(top, jnp.max(logits, axis=-1, keepdims=True))
        weights = jnp.where(allowed, jnp.exp(logits - new_top), 0.0)
        return (new_top, total * jnp.exp(top - new_top) + jnp.sum(weights, axis=-1, keepdims=True))

    start_top = jnp.full((heads, tok_rows, 1), -1e30, f32)
    start_total = jnp.zeros((heads, tok_rows, 1), f32)
    top, total = lax.fori_loop(first_block, needed, max_step, (start_top, start_total))
    log_total = top + jnp.log(total)

    def probs_of(start):
        logits, allowed, key_block, value_block = scores_of(start)
        return (jnp.where(allowed, jnp.exp(logits - log_total), 0.0), key_block, value_block)

    def out_step(index, acc):
        probs, key_block, value_block = probs_of(index * block)
        return acc + jnp.einsum(
            "htk,kd->htd", probs.astype(bf16), value_block, preferred_element_type=f32
        )

    attn_raw = lax.fori_loop(
        first_block, needed, out_step, jnp.zeros((heads, tok_rows, head_size), f32)
    )
    attn = join_heads(attn_raw).astype(bf16)
    resid = input_rows + matrix_product(attn, output_weight)
    normed_mlp, pull_mlp = jax.vjp(rms_norm, resid, gain_mlp)
    mlp_in = normed_mlp.astype(bf16)
    mlp_all = gather_rows(mlp_in, shards, 2)
    cot_all = lax.all_gather(cot_own, "fsdp", axis=0, tiled=True)

    first_unit = place * unit_rows
    gate_second = lax.dynamic_slice_in_dim(gate_factor_second, first_unit, unit_rows, 1)
    up_second = lax.dynamic_slice_in_dim(upward_factor_second, first_unit, unit_rows, 1)
    down_first = lax.dynamic_slice_in_dim(down_factor_first, first_unit, unit_rows, 0)

    def merged_units(matrix, first, second):
        low = lax.dot_general(
            second, first, (((0,), (1,)), ((), ())), preferred_element_type=f32
        )
        return (matrix.astype(f32) + low).astype(bf16)

    gate_weight = merged_units(gate_matrix, gate_factor_first, gate_second)
    up_weight = merged_units(upward_matrix, upward_factor_first, up_second)
    down_weight = (
        down_matrix.astype(f32) + matrix_product(down_first, down_factor_second)
    ).astype(bf16)

    gate = right_product(mlp_all, gate_weight)
    up = right_product(mlp_all, up_weight)
    hidden_full, pull_geglu = jax.vjp(geglu, gate, up)
    hidden = hidden_full.astype(bf16)
    down_sum = scatter_rows(matrix_product(hidden, down_weight).astype(bf16), place, shards)
    grad_hidden = right_product(cot_all, down_weight)
    grad_gate_full, grad_up_full = pull_geglu(grad_hidden)
    grad_gate = grad_gate_full.astype(bf16)
    grad_up = grad_up_full.astype(bf16)
    grad_mlp_in = scatter_rows(
        (matrix_product(grad_gate, gate_weight) + matrix_product(grad_up, up_weight)).astype(bf16),
        place,
        shards,
    )
    gate_rows = left_matrix_product(grad_gate, mlp_all)
    up_rows = left_matrix_product(grad_up, mlp_all)
    down_rows = left_matrix_product(hidden, cot_all)
    gate_rows_low = gate_rows.astype(bf16)
    up_rows_low = up_rows.astype(bf16)
    down_rows_low = down_rows.astype(bf16)
    swap = [(0, 1), (1, 0)]
    g_gate_rows = gate_rows + lax.ppermute(gate_rows_low, "dp", swap).astype(f32)
    g_up_rows = up_rows + lax.ppermute(up_rows_low, "dp", swap).astype(f32)
    g_down_rows = down_rows + lax.ppermute(down_rows_low, "dp", swap).astype(f32)

    def columns_of(first, rows):
        return lax.dot_general(
            first, rows.astype(bf16), (((0,), (1,)), ((), ())), preferred_element_type=f32
        )

    g_gate_out = columns_of(gate_factor_first, g_gate_rows)
    g_up_out = columns_of(upward_factor_first, g_up_rows)
    g_down_in = right_product(g_down_rows.astype(bf16), down_factor_second)
    gate_in_term = lax.dot_general(
        gate_rows_low, gate_second, (((0,), (1,)), ((), ())), preferred_element_type=f32
    )
    up_in_term = lax.dot_general(
        up_rows_low, up_second, (((0,), (1,)), ((), ())), preferred_element_type=f32
    )
    down_out_term = left_matrix_product(down_first, down_rows_low)

    output = (resid + down_sum).astype(bf16)
    grad_resid_norm, gain_mlp_term = pull_mlp(grad_mlp_in)
    grad_resid = cot_own.astype(f32) + grad_resid_norm
    grad_branch = grad_resid.astype(bf16)
    grad_attn = right_product(grad_branch, output_weight).astype(bf16)
    lora_output = matrix_product(attn, output_factor_first).astype(bf16)
    lora_query = matrix_product(attn_in, query_factor_first).astype(bf16)
    lora_key = matrix_product(attn_in, key_factor_first).astype(bf16)
    lora_value = matrix_product(attn_in, value_factor_first).astype(bf16)
    grad_attn_heads = split_heads(grad_attn)
    delta = jnp.sum(
        grad_attn_heads.astype(f32) * attn_raw, axis=-1, keepdims=True
    )

    def grad_step(index, carry):
        grad_query_acc, key_terms = carry
        start = index * block
        probs, key_block, value_block = probs_of(start)
        grad_probs = jnp.einsum(
            "htd,kd->htk", grad_attn_heads, value_block, preferred_element_type=f32
        )
        grad_scores = (scale * probs * (grad_probs - delta)).astype(bf16)
        grad_query_acc = grad_query_acc + jnp.einsum(
            "htk,kd->htd", grad_scores, key_block, preferred_element_type=f32
        )
        key_part = jnp.einsum("htk,htd->kd", grad_scores, query, preferred_element_type=f32)
        value_part = jnp.einsum(
            "htk,htd->kd", probs.astype(bf16), grad_attn_heads, preferred_element_type=f32
        )
        both = jnp.concatenate([key_part, value_part], axis=1).astype(bf16)
        key_terms = lax.dynamic_update_slice_in_dim(key_terms, both, start, 0)
        return (grad_query_acc, key_terms)

    grad_query_rot, key_terms = lax.fori_loop(
        first_block,
        needed,
        grad_step,
        (
            jnp.zeros((heads, tok_rows, head_size), f32),
            jnp.zeros((length, 2 * head_size), bf16),
        ),
    )
    key_sums = scatter_rows(key_terms, place, shards)
    grad_query_lin = join_heads(
        rotate(grad_query_rot, cosines[None], -sines[None]).astype(bf16)
    )
    grad_key_value_lin = jnp.concatenate(
        [rotate(key_sums[:, :head_size], cosines, -sines), key_sums[:, head_size:]], axis=1
    ).astype(bf16)
    grad_attn_in = right_product(grad_query_lin, query_weight) + right_product(
        grad_key_value_lin, key_value_weight
    )
    grad_inputs_norm, gain_attn_term = pull_attn(grad_attn_in)
    grad_inputs = grad_resid + grad_inputs_norm

    def low_term(left, right):
        return left_matrix_product(left, right).astype(bf16)

    per = in_rows
    few = rank // shards
    early = jnp.concatenate(
        [
            low_term(lora_output, grad_branch).reshape(shards, few, width),
            down_out_term.astype(bf16).reshape(shards, few, width),
            pack_rows(
                jnp.concatenate([gate_in_term, up_in_term], axis=1).astype(bf16), shards, width
            ),
        ],
        axis=1,
    )
    g_output_weight, early_sums = scatter_both(
        low_term(attn, grad_branch).reshape(shards, per, width), early, place, core
    )
    g_output_out = early_sums[:few]
    g_down_out = early_sums[few : 2 * few]
    pair = unpack_rows(early_sums[2 * few :], 2 * head_size)
    g_gate_in = pair[:, :head_size]
    g_up_in = pair[:, head_size:]

    tiny = jnp.concatenate(
        [
            low_term(lora_key, grad_key_value_lin[:, :head_size]).reshape(shards, few, head_size),
            low_term(lora_value, grad_key_value_lin[:, head_size:]).reshape(shards, few, head_size),
            gain_attn_term.astype(bf16).reshape(shards, few, -1),
            gain_mlp_term.astype(bf16).reshape(shards, few, -1),
        ],
        axis=2,
    )
    tiny = jnp.pad(tiny, ((0, 0), (0, 0), (0, width - tiny.shape[2])))
    late = jnp.concatenate(
        [
            low_term(lora_query, grad_query_lin).reshape(shards, few, width),
            pack_rows(low_term(attn_in, grad_key_value_lin), shards, width),
            tiny,
        ],
        axis=1,
    )
    g_query_weight, late_sums = scatter_both(
        low_term(attn_in, grad_query_lin).reshape(shards, per, width), late, place, core
    )
    g_query_out = late_sums[:few]
    pair = unpack_rows(late_sums[few : late_sums.shape[0] - few], 2 * head_size)
    g_key_weight = pair[:, :head_size]
    g_value_weight = pair[:, head_size:]
    last = late_sums[late_sums.shape[0] - few :]
    g_key_out = last[:, :head_size]
    g_value_out = last[:, head_size : 2 * head_size]
    each = per // few
    g_gain_attn = last[:, 2 * head_size : 2 * head_size + each].reshape(per)
    g_gain_mlp = last[:, 2 * head_size + each : 2 * head_size + 2 * each].reshape(per)
    g_query_in = right_product(g_query_weight.astype(bf16), query_factor_second)
    g_output_in = right_product(g_output_weight.astype(bf16), output_factor_second)
    g_key_in = right_product(g_key_weight.astype(bf16), key_factor_second)
    g_value_in = right_product(g_value_weight.astype(bf16), value_factor_second)
    return (
        output[None],
        grad_inputs[None],
        g_gain_attn,
        g_gain_mlp,
        g_query_weight,
        g_key_weight,
        g_value_weight,
        g_output_weight,
        g_gate_rows,
        g_up_rows,
        g_down_rows,
        g_query_in,
        g_query_out,
        g_key_in,
        g_key_out,
        g_value_in,
        g_value_out,
        g_output_in,
        g_output_out,
        g_gate_in,
        g_gate_out,
        g_up_in,
        g_up_out,
        g_down_in,
        g_down_out,
    )


def solution(mesh):
    in_specs = (
        P("dp", "fsdp", None),
        P("dp", None),
        P(),
        P(),
        P("fsdp", None),
        P("fsdp", None),
        P("fsdp", None),
        P("fsdp", None),
        P("fsdp", None),
        P("fsdp", None),
        P("fsdp", None),
        P(),
        P(),
        P(),
        P(),
        P(),
        P(),
        P(),
        P(),
        P(),
        P(),
        P(),
        P(),
        P(),
        P(),
        P("dp", "fsdp", None),
    )
    out_specs = (
        P("dp", "fsdp", None),
        P("dp", "fsdp", None),
        P("fsdp"),
        P("fsdp"),
        P("fsdp", None),
        P("fsdp", None),
        P("fsdp", None),
        P("fsdp", None),
        P("fsdp", None),
        P("fsdp", None),
        P("fsdp", None),
        P("fsdp", None),
        P("fsdp", None),
        P("fsdp", None),
        P("fsdp", None),
        P("fsdp", None),
        P("fsdp", None),
        P("fsdp", None),
        P("fsdp", None),
        P("fsdp", None),
        P(None, "fsdp"),
        P("fsdp", None),
        P(None, "fsdp"),
        P("fsdp", None),
        P("fsdp", None),
    )
    return jax.shard_map(local, mesh=mesh, in_specs=in_specs, out_specs=out_specs, check_vma=False)
```

```python
import functools

import jax
import jax.numpy as jnp
from jax import lax
from jax.experimental import pallas as pl
from jax.experimental.pallas import tpu as pltpu
from jax.sharding import PartitionSpec as P

EPS = 1e-06
MESH = pl.DeviceIdType.MESH
LINE = 4


def matrix_product(left, right):
    return jnp.dot(left, right, preferred_element_type=jnp.float32)


def left_matrix_product(left, right):
    return lax.dot_general(
        left, right, (((0,), (0,)), ((), ())), preferred_element_type=jnp.float32
    )


def right_product(left, right):
    return lax.dot_general(
        left, right, (((1,), (1,)), ((), ())), preferred_element_type=jnp.float32
    )


def rms_norm(values, gain):
    factor = lax.rsqrt(jnp.mean(values * values, axis=-1, keepdims=True) + EPS)
    return values * factor * gain


def rotate(values, cosines, sines):
    half = values.shape[-1] // 2
    first = values[..., :half]
    second = values[..., half:]
    return jnp.concatenate(
        [first * cosines - second * sines, second * cosines + first * sines], axis=-1
    )


def doc_positions(segments):
    length = segments.shape[0]
    index = jnp.arange(length, dtype=jnp.int32)
    starts = jnp.concatenate([jnp.ones((1,), dtype=bool), segments[1:] != segments[:-1]])
    first = lax.cummax(jnp.where(starts, index, jnp.zeros_like(index)), axis=0)
    return index - first


def geglu(gate, up):
    return jax.nn.gelu(gate, approximate=True) * up


def place_of():
    f = lax.axis_index("fsdp")
    z, y, x = f // 4, (f // 2) % 2, f % 2
    near_end = z // 2
    inner = (z + near_end) % 2
    visits = []
    for k in range(LINE):
        u = k + inner * (1 if k == 0 else -1 if k == 1 else 0)
        visits.append(u + near_end * (3 - 2 * u))
    return f, z, y, x, f + 1 - 2 * x, f + 2 - 4 * y, visits


def greet(f, z, fx, fy, with_core):
    barrier = pltpu.get_barrier_semaphore()

    def signal(target):
        pl.semaphore_signal(barrier, inc=1, device_id=target, device_id_type=MESH)

    signal({"fsdp": fx})
    signal({"fsdp": fy})
    if with_core:
        signal({"dp": 1 - lax.axis_index("dp")})

    @pl.when(z > 0)
    def _():
        signal({"fsdp": f - 4})

    @pl.when(z < LINE - 1)
    def _():
        signal({"fsdp": f + 4})

    peers = 3 if with_core else 2
    ends = jnp.where(z > 0, 1, 0) + jnp.where(z < LINE - 1, 1, 0)
    pl.semaphore_wait(barrier, peers + ends)


def send(source, target, send_sem, recv_sem, device):
    copy = pltpu.make_async_remote_copy(
        src_ref=source,
        dst_ref=target,
        send_sem=send_sem,
        recv_sem=recv_sem,
        device_id=device,
        device_id_type=MESH,
    )
    copy.start()
    return copy


def arrived(ref, sem):
    pltpu.make_async_copy(ref, ref, sem).wait()


def gather_kernel(pieces, count, with_core, *refs):
    ins, outs = refs[:count], refs[count : 2 * count]
    z_send, z_recv, a_send, a_recv, b_send, b_recv, own_sem, c_send, c_recv = refs[2 * count :]
    f, z, y, x, fx, fy, visits = place_of()
    core = lax.axis_index("dp")
    greet(f, z, fx, fy, with_core)

    def at(index, where, rows):
        ref = outs[index].at[where]
        if with_core:
            ref = ref.at[core]
        return ref.at[pl.ds(*rows)]

    own = []
    for i in range(count):
        target = outs[i].at[f, core] if with_core else outs[i].at[f]
        copy = pltpu.make_async_copy(ins[i], target, own_sem.at[i])
        copy.start()
        own.append(copy)
    sent = []

    def spread_z(p, k):
        index, rows, first = pieces[p]
        v = visits[k]
        where = v * 4 + y * 2 + x
        target = at(index, where, rows)
        if k > 0:
            arrived(target, z_recv.at[p, v])
        source = ins[index].at[pl.ds(*rows)] if k == 0 else target

        @pl.when((v <= z) & (z < LINE - 1))
        def _():
            send(source, target, z_send.at[p, k, 0], z_recv.at[p, v], {"fsdp": f + 4})

        @pl.when((v >= z) & (z > 0))
        def _():
            send(source, target, z_send.at[p, k, 1], z_recv.at[p, v], {"fsdp": f - 4})

        fa, fb = (fy, fx) if first == "y" else (fx, fy)
        sent.append(send(source, target, a_send.at[p, k], a_recv.at[p, k], {"fsdp": fa}))
        sent.append(send(source, target, b_send.at[p, k, 0], b_recv.at[p, k, 0], {"fsdp": fb}))

    def spread_a(p, k):
        index, rows, first = pieces[p]
        v = visits[k]
        where = v * 4 + (1 - y) * 2 + x if first == "y" else v * 4 + y * 2 + (1 - x)
        fb = fx if first == "y" else fy
        target = at(index, where, rows)
        arrived(target, a_recv.at[p, k])
        sent.append(send(target, target, b_send.at[p, k, 1], b_recv.at[p, k, 1], {"fsdp": fb}))

    def finish_b(p, k):
        index, rows, first = pieces[p]
        v = visits[k]
        if first == "y":
            spots = v * 4 + y * 2 + (1 - x), v * 4 + (1 - y) * 2 + (1 - x)
        else:
            spots = v * 4 + (1 - y) * 2 + x, v * 4 + (1 - y) * 2 + (1 - x)
        for j in range(2):
            arrived(at(index, spots[j], rows), b_recv.at[p, k, j])

    def swap(k):
        for i in range(count):
            block = outs[i].at[pl.ds(visits[k] * 4, 4), core]
            sent.append(
                send(block, block, c_send.at[i, k], c_recv.at[i, k], {"dp": 1 - core})
            )

    def swapped(k):
        for i in range(count):
            arrived(outs[i].at[pl.ds(visits[k] * 4, 4), 1 - core], c_recv.at[i, k])

    for k in range(LINE + 1):
        if k < LINE:
            for p in range(len(pieces)):
                spread_z(p, k)
        if k > 0:
            for p in range(len(pieces)):
                spread_a(p, k - 1)
    for copy in own:
        copy.wait()
    for k in range(LINE):
        for p in range(len(pieces)):
            finish_b(p, k)
        if with_core:
            swap(k)
    if with_core:
        for k in range(LINE):
            swapped(k)
    for copy in sent:
        copy.wait_send()
    for p in range(len(pieces)):
        index, rows, first = pieces[p]
        for k in range(LINE):
            v = visits[k]
            block = at(index, f, rows)

            @pl.when((v <= z) & (z < LINE - 1))
            def _():
                pltpu.make_async_copy(block, block, z_send.at[p, k, 0]).wait()

            @pl.when((v >= z) & (z > 0))
            def _():
                pltpu.make_async_copy(block, block, z_send.at[p, k, 1]).wait()


def gather_blocks(arrays, splits, with_core, number):
    shards = 4 * LINE
    pieces = []
    for index, parts in enumerate(splits):
        start = 0
        for rows, first in parts:
            pieces.append((index, (start, rows), first))
            start += rows
    lead = (shards, 2) if with_core else (shards,)
    amount = len(pieces)
    dma = pltpu.SemaphoreType.DMA
    outs = pl.pallas_call(
        functools.partial(gather_kernel, pieces, len(arrays), with_core),
        out_shape=[jax.ShapeDtypeStruct(lead + a.shape, a.dtype) for a in arrays],
        in_specs=[pl.BlockSpec(memory_space=pltpu.VMEM)] * len(arrays),
        out_specs=[pl.BlockSpec(memory_space=pl.ANY)] * len(arrays),
        scratch_shapes=[
            dma((amount, LINE, 2)),
            dma((amount, LINE)),
            dma((amount, LINE)),
            dma((amount, LINE)),
            dma((amount, LINE, 2)),
            dma((amount, LINE, 2)),
            dma((len(arrays),)),
            dma((len(arrays), LINE)),
            dma((len(arrays), LINE)),
        ],
        compiler_params=pltpu.CompilerParams(collective_id=number, has_side_effects=True),
        name="gather_blocks_%d" % number,
    )(*arrays)
    return [o.reshape((-1, o.shape[-1])) for o in outs]


def bit_orders(bits):
    rest = list(range(min(bits, 3), bits))
    first = list(range(min(bits, 3)))
    return [first[i % len(first) :] + first[: i % len(first)] + rest for i in range(3)]


def add_rows(target, other):
    rows = target.shape[0]
    step = 16

    @pl.loop(0, rows // step)
    def _(i):
        part = pl.ds(pl.multiple_of(i * step, step), step)
        total = target[part].astype(jnp.float32) + other[part].astype(jnp.float32)
        target[part] = total.astype(target.dtype)


def scatter_kernel(terms_ref, out_ref, *refs):
    held, c_buf, a_buf, b_buf, z_buf = refs[:5]
    h_sem, c_send, c_recv, a_send, a_recv, b_send, b_recv, z_send, z_recv, o_send, o_recv = refs[5:]
    f, z, y, x, fx, fy, visits = place_of()
    core = lax.axis_index("dp")
    visits = visits[::-1]
    rows = out_ref.shape[0] // 2
    base = pl.multiple_of(core * rows, 16)
    away = pl.multiple_of((1 - core) * rows, 16)
    part = rows // 2
    loads = []
    for k in range(LINE):
        four = pl.ds(visits[k] * 4, 4)
        copy = pltpu.make_async_copy(
            terms_ref.at[four, pl.ds(base, rows)], held.at[four], h_sem.at[k]
        )
        copy.start()
        loads.append(copy)
    greet(f, z, fx, fy, True)

    def spots(p, v):
        piece = pl.ds(p * part, part)
        both = held.at[v * 4 + (1 - y) * 2 + (1 - x), piece]
        only_x = held.at[v * 4 + y * 2 + (1 - x), piece]
        only_y = held.at[v * 4 + (1 - y) * 2 + x, piece]
        own = held.at[v * 4 + y * 2 + x, piece]
        return (both, only_x, only_y, own) if p == 0 else (both, only_y, only_x, own)

    sent = []
    near = ((fx, fy), (fy, fx))
    for k in range(LINE):
        source = terms_ref.at[pl.ds(visits[k] * 4, 4), pl.ds(away, rows)]
        sent.append(send(source, c_buf.at[k], c_send.at[k], c_recv.at[k], {"dp": 1 - core}))

    def start_a(k):
        loads[k].wait()
        arrived(c_buf.at[k], c_recv.at[k])
        for j in range(4):
            add_rows(held.at[visits[k] * 4 + j], c_buf.at[k, j])
        for j in range(2):
            for p in range(2):
                sent.append(
                    send(
                        spots(p, visits[k])[j],
                        a_buf.at[p, k, j],
                        a_send.at[p, k, j],
                        a_recv.at[p, k, j],
                        {"fsdp": near[p][0]},
                    )
                )

    def start_b(p, k):
        flipped = spots(p, visits[k])[2]
        arrived(a_buf.at[p, k, 0], a_recv.at[p, k, 0])
        add_rows(flipped, a_buf.at[p, k, 0])
        sent.append(
            send(flipped, b_buf.at[p, k], b_send.at[p, k], b_recv.at[p, k], {"fsdp": near[p][1]})
        )
        arrived(a_buf.at[p, k, 1], a_recv.at[p, k, 1])
        add_rows(spots(p, visits[k])[3], a_buf.at[p, k, 1])

    def take(p, own, slot):
        arrived(z_buf.at[p, slot], z_recv.at[p, slot])
        add_rows(own, z_buf.at[p, slot])

    def start_z(p, k):
        v = visits[k]
        own = spots(p, v)[3]
        arrived(b_buf.at[p, k], b_recv.at[p, k])
        add_rows(own, b_buf.at[p, k])
        if k == LINE - 1:

            @pl.when(z > 0)
            def _():
                take(p, own, z)

            @pl.when(z < LINE - 1)
            def _():
                take(p, own, LINE)

            return

        @pl.when(v > z)
        def _():
            @pl.when(z > 0)
            def _():
                take(p, own, v)

            send(own, z_buf.at[p, v], z_send.at[p, k], z_recv.at[p, v], {"fsdp": f + 4})

        @pl.when(v < z)
        def _():
            @pl.when(z < LINE - 1)
            def _():
                take(p, own, v)

            @pl.when(v == z - 1)
            def _():
                send(own, z_buf.at[p, LINE], z_send.at[p, k], z_recv.at[p, LINE], {"fsdp": f - 4})

            @pl.when(v < z - 1)
            def _():
                send(own, z_buf.at[p, v], z_send.at[p, k], z_recv.at[p, v], {"fsdp": f - 4})

    start_a(0)
    start_a(1)
    for k in range(LINE + 1):
        if k + 2 < LINE:
            start_a(k + 2)
        if k < LINE:
            for p in range(2):
                start_b(p, k)
        if k > 0:
            for p in range(2):
                start_z(p, k - 1)
    step = 16

    @pl.loop(0, rows // step)
    def _(i):
        offset = pl.multiple_of(i * step, step)
        out_ref[pl.ds(pl.multiple_of(base + offset, step), step)] = held[f, pl.ds(offset, step)]

    final = out_ref.at[pl.ds(base, rows)]
    sent.append(send(final, final, o_send.at[0], o_recv.at[0], {"dp": 1 - core}))
    arrived(out_ref.at[pl.ds(away, rows)], o_recv.at[0])
    for copy in sent:
        copy.wait_send()
    for p in range(2):
        for k in range(LINE - 1):
            pltpu.make_async_copy(b_buf.at[p, k], b_buf.at[p, k], z_send.at[p, k]).wait()


def scatter_blocks(terms, number):
    shards, rows, columns = terms.shape
    dma = pltpu.SemaphoreType.DMA
    own = rows // 2
    part = own // 2
    return pl.pallas_call(
        scatter_kernel,
        out_shape=jax.ShapeDtypeStruct((rows, columns), terms.dtype),
        in_specs=[pl.BlockSpec(memory_space=pl.ANY)],
        out_specs=pl.BlockSpec(memory_space=pltpu.VMEM),
        scratch_shapes=[
            pltpu.VMEM((shards, own, columns), terms.dtype),
            pltpu.VMEM((LINE, 4, own, columns), terms.dtype),
            pltpu.VMEM((2, LINE, 2, part, columns), terms.dtype),
            pltpu.VMEM((2, LINE, part, columns), terms.dtype),
            pltpu.VMEM((2, LINE + 1, part, columns), terms.dtype),
            dma((LINE,)),
            dma((LINE,)),
            dma((LINE,)),
            dma((2, LINE, 2)),
            dma((2, LINE, 2)),
            dma((2, LINE)),
            dma((2, LINE)),
            dma((2, LINE)),
            dma((2, LINE + 1)),
            dma((1,)),
            dma((1,)),
        ],
        compiler_params=pltpu.CompilerParams(
            collective_id=number, has_side_effects=True, vmem_limit_bytes=40 * 1024 * 1024
        ),
        name="scatter_blocks_%d" % number,
    )(terms)


class HalvingSum:
    def __init__(self, terms, place, shards, edges):
        blocks = terms.reshape(shards, terms.shape[0] // shards, terms.shape[1])
        self.place, self.shards, self.kind = place, shards, terms.dtype
        self.bits = shards.bit_length() - 1
        self.orders = bit_orders(self.bits)
        self.held = [
            blocks[:, low:high].reshape((2,) * self.bits + (high - low, terms.shape[1]))
            for low, high in zip(edges[:-1], edges[1:])
        ]
        self.left = [list(range(self.bits))[::-1] for _ in self.held]
        self.step = 0
        self.came = []

    def start(self):
        self.keep, self.came = [], []
        for i, current in enumerate(self.held):
            b = self.orders[i][self.step]
            where, mine = self.left[i].index(b), (self.place >> b) & 1
            self.left[i].remove(b)
            away = lax.dynamic_index_in_dim(current, 1 - mine, where, keepdims=False)
            self.keep.append(lax.dynamic_index_in_dim(current, mine, where, keepdims=False))
            pairs = [(j, j ^ (1 << b)) for j in range(self.shards)]
            self.came.append(lax.ppermute(away, "fsdp", pairs))
        self.step += 1

    def finish(self, came):
        totals = [k.astype(jnp.float32) + c.astype(jnp.float32) for k, c in zip(self.keep, came)]
        if self.step == self.bits:
            self.sum = jnp.concatenate(totals, axis=0)
        else:
            self.held = [t.astype(self.kind) for t in totals]

    def rest(self):
        while self.step < self.bits:
            self.start()
            self.finish(self.came)
        return self.sum


def together(sums, work):
    came, work = lax.optimization_barrier(([s.came for s in sums], work))
    for one, own in zip(sums, came):
        one.finish(own)
    return work


def row_edges(rows):
    third = (rows * 3 // 8) // 16 * 16
    return [0, third, 2 * third, rows]


def scatter_shared(terms, core):
    half = terms.shape[2] // 2
    swap = [(0, 1), (1, 0)]
    own = lax.dynamic_slice_in_dim(terms, core * half, half, 2)
    away = lax.dynamic_slice_in_dim(terms, (1 - core) * half, half, 2)
    both = own + lax.ppermute(away, "dp", swap)
    mine = lax.psum_scatter(both, "fsdp", scatter_dimension=0, tiled=False)
    theirs = lax.ppermute(mine, "dp", swap)
    return jnp.where(
        core == 0,
        jnp.concatenate([mine, theirs], axis=1),
        jnp.concatenate([theirs, mine], axis=1),
    )


def pack_rows(terms, shards, width):
    count = width // terms.shape[1]
    parts = terms.reshape(shards, count, -1, terms.shape[1])
    return jnp.concatenate([parts[:, i] for i in range(count)], axis=2)


def unpack_rows(terms, columns):
    count = terms.shape[1] // columns
    return jnp.concatenate(
        [terms[:, i * columns : (i + 1) * columns] for i in range(count)], axis=0
    )


def gather_weights(query, output, key_value, shards):
    if shards == 4 * LINE:
        rows = query.shape[0]
        return gather_blocks(
            [query, output, key_value],
            [[(rows, "y")], [(rows, "x")], [(rows // 2, "y"), (rows // 2, "x")]],
            True,
            1,
        )

    def whole(own):
        return lax.all_gather(own, ("fsdp", "dp"), axis=0, tiled=True)

    return whole(query), whole(output), whole(key_value)


def gather_rows(own, shards, number):
    if shards == 4 * LINE:
        half = own.shape[0] // 2
        return gather_blocks([own], [[(half, "y"), (half, "x")]], False, number)[0]
    return lax.all_gather(own, "fsdp", axis=0, tiled=True)


def local(
    tokens,
    segment_ids,
    gain_attn,
    gain_mlp,
    query_matrix,
    key_matrix,
    value_matrix,
    output_matrix,
    gate_matrix,
    upward_matrix,
    down_matrix,
    query_factor_first,
    query_factor_second,
    key_factor_first,
    key_factor_second,
    value_factor_first,
    value_factor_second,
    output_factor_first,
    output_factor_second,
    gate_factor_first,
    gate_factor_second,
    upward_factor_first,
    upward_factor_second,
    down_factor_first,
    down_factor_second,
    cotangent,
):
    bf16 = jnp.bfloat16
    f32 = jnp.float32
    tok_rows = tokens.shape[1]
    width = tokens.shape[2]
    length = segment_ids.shape[1]
    head_size = key_matrix.shape[1]
    heads = query_matrix.shape[1] // head_size
    unit_rows = gate_matrix.shape[0]
    in_rows = query_matrix.shape[0]
    shards = length // tok_rows
    rank = query_factor_first.shape[1]
    place = lax.axis_index("fsdp")
    core = lax.axis_index("dp")
    offset = place * tok_rows
    input_rows = tokens[0].astype(f32)
    seg_all = segment_ids[0]
    seg_own = lax.dynamic_slice_in_dim(seg_all, offset, tok_rows, 0)
    positions = lax.dynamic_slice_in_dim(doc_positions(seg_all), offset, tok_rows, 0)
    half = head_size // 2
    inverse = 10000.0 ** (-(jnp.arange(half, dtype=f32) * 2.0 / head_size))
    angles = positions.astype(f32)[:, None] * inverse[None, :]
    cosines = jnp.cos(angles)
    sines = jnp.sin(angles)

    core_rows = in_rows // 2

    def split_heads(values):
        return jnp.stack(
            [values[:, h * head_size : (h + 1) * head_size] for h in range(heads)]
        )

    def join_heads(values):
        return jnp.concatenate([values[h] for h in range(heads)], axis=1)

    def merged_rows(matrix, first, second):
        own = lax.dynamic_slice_in_dim(matrix, core * core_rows, core_rows, 0)
        rows = lax.dynamic_slice_in_dim(first, place * in_rows + core * core_rows, core_rows, 0)
        return (own.astype(f32) + matrix_product(rows, second)).astype(bf16)

    query_weight, output_weight, key_value_weight = gather_weights(
        merged_rows(query_matrix, query_factor_first, query_factor_second),
        merged_rows(output_matrix, output_factor_first, output_factor_second),
        jnp.concatenate(
            [
                merged_rows(key_matrix, key_factor_first, key_factor_second),
                merged_rows(value_matrix, value_factor_first, value_factor_second),
            ],
            axis=1,
        ),
        shards,
    )
    cot_own, key_value_weight = lax.optimization_barrier((cotangent[0], key_value_weight))
    cot_all = lax.all_gather(cot_own, "fsdp", axis=0, tiled=True)

    normed_attn, pull_attn = jax.vjp(rms_norm, input_rows, gain_attn)
    attn_in = normed_attn.astype(bf16)
    key_value_lin = matrix_product(attn_in, key_value_weight)
    key = rotate(key_value_lin[:, :head_size], cosines, sines).astype(bf16)
    value = key_value_lin[:, head_size:].astype(bf16)
    key_value = gather_rows(jnp.concatenate([key, value], axis=1), shards, 3)
    query_lin = matrix_product(attn_in, query_weight)
    query = rotate(split_heads(query_lin), cosines[None], sines[None]).astype(bf16)
    keys_all = key_value[:, :head_size]
    values_all = key_value[:, head_size:]
    block = min(512, length)
    scale = head_size ** (-0.5)
    query_index = offset + jnp.arange(tok_rows, dtype=jnp.int32)
    needed = (offset + tok_rows + block - 1) // block
    first_block = (offset - positions[0]) // block

    def scores_of(start):
        key_block = lax.dynamic_slice_in_dim(keys_all, start, block, 0)
        value_block = lax.dynamic_slice_in_dim(values_all, start, block, 0)
        seg_block = lax.dynamic_slice_in_dim(seg_all, start, block, 0)
        key_index = start + jnp.arange(block, dtype=jnp.int32)
        allowed = (seg_own[:, None] == seg_block[None, :]) & (
            key_index[None, :] <= query_index[:, None]
        )
        allowed = allowed[None]
        raw = jnp.einsum("htd,kd->htk", query, key_block, preferred_element_type=f32)
        return (jnp.where(allowed, raw * scale, -1e30), allowed, key_block, value_block)

    def max_step(index, carry):
        top, total = carry
        logits, allowed, key_block, value_block = scores_of(index * block)
        new_top = jnp.maximum(top, jnp.max(logits, axis=-1, keepdims=True))
        weights = jnp.where(allowed, jnp.exp(logits - new_top), 0.0)
        return (new_top, total * jnp.exp(top - new_top) + jnp.sum(weights, axis=-1, keepdims=True))

    start_top = jnp.full((heads, tok_rows, 1), -1e30, f32)
    start_total = jnp.zeros((heads, tok_rows, 1), f32)
    top, total = lax.fori_loop(first_block, needed, max_step, (start_top, start_total))
    log_total = top + jnp.log(total)

    def probs_of(start):
        logits, allowed, key_block, value_block = scores_of(start)
        return (jnp.where(allowed, jnp.exp(logits - log_total), 0.0), key_block, value_block)

    def out_step(index, acc):
        probs, key_block, value_block = probs_of(index * block)
        return acc + jnp.einsum(
            "htk,kd->htd", probs.astype(bf16), value_block, preferred_element_type=f32
        )

    attn_raw = lax.fori_loop(
        first_block, needed, out_step, jnp.zeros((heads, tok_rows, head_size), f32)
    )
    attn = join_heads(attn_raw).astype(bf16)
    resid = input_rows + matrix_product(attn, output_weight)
    normed_mlp, pull_mlp = jax.vjp(rms_norm, resid, gain_mlp)
    mlp_in = normed_mlp.astype(bf16)
    mlp_all = gather_rows(mlp_in, shards, 2)

    first_unit = place * unit_rows
    gate_second = lax.dynamic_slice_in_dim(gate_factor_second, first_unit, unit_rows, 1)
    up_second = lax.dynamic_slice_in_dim(upward_factor_second, first_unit, unit_rows, 1)
    down_first = lax.dynamic_slice_in_dim(down_factor_first, first_unit, unit_rows, 0)

    def merged_units(matrix, first, second):
        low = lax.dot_general(
            second, first, (((0,), (1,)), ((), ())), preferred_element_type=f32
        )
        return (matrix.astype(f32) + low).astype(bf16)

    gate_weight = merged_units(gate_matrix, gate_factor_first, gate_second)
    up_weight = merged_units(upward_matrix, upward_factor_first, up_second)
    down_weight = (
        down_matrix.astype(f32) + matrix_product(down_first, down_factor_second)
    ).astype(bf16)

    gate = right_product(mlp_all, gate_weight)
    up = right_product(mlp_all, up_weight)
    hidden_full, pull_geglu = jax.vjp(geglu, gate, up)
    hidden = hidden_full.astype(bf16)
    edges = row_edges(tok_rows)
    down_terms = HalvingSum(
        matrix_product(hidden, down_weight).astype(bf16), place, shards, edges
    )
    down_terms.start()
    grad_hidden = right_product(cot_all, down_weight)
    grad_gate_full, grad_up_full = pull_geglu(grad_hidden)
    grad_gate, grad_up = together(
        [down_terms], (grad_gate_full.astype(bf16), grad_up_full.astype(bf16))
    )
    down_terms.start()
    in_terms = matrix_product(grad_gate, gate_weight)
    in_terms, grad_gate, grad_up = together([down_terms], (in_terms, grad_gate, grad_up))
    down_terms.start()
    in_terms = (in_terms + matrix_product(grad_up, up_weight)).astype(bf16)
    in_terms, grad_gate, grad_up = together([down_terms], (in_terms, grad_gate, grad_up))
    mlp_terms = HalvingSum(in_terms, place, shards, edges)
    down_terms.start()
    mlp_terms.start()
    gate_rows = left_matrix_product(grad_gate, mlp_all)
    up_rows = left_matrix_product(grad_up, mlp_all)
    gate_rows, up_rows, hidden = together([down_terms, mlp_terms], (gate_rows, up_rows, hidden))
    mlp_terms.start()
    down_rows = left_matrix_product(hidden, cot_all)
    gate_rows_low = gate_rows.astype(bf16)
    down_rows, gate_rows_low = together([mlp_terms], (down_rows, gate_rows_low))
    mlp_terms.start()
    gate_in_term = lax.dot_general(
        gate_rows_low, gate_second, (((0,), (1,)), ((), ())), preferred_element_type=f32
    )
    up_rows_low = up_rows.astype(bf16)
    down_rows_low = down_rows.astype(bf16)
    gate_in_term, up_rows_low, down_rows_low = together(
        [mlp_terms], (gate_in_term, up_rows_low, down_rows_low)
    )
    mlp_terms.start()
    up_in_term = lax.dot_general(
        up_rows_low, up_second, (((0,), (1,)), ((), ())), preferred_element_type=f32
    )
    down_out_term = left_matrix_product(down_first, down_rows_low)
    up_in_term, down_out_term = together([mlp_terms], (up_in_term, down_out_term))
    grad_mlp_in = mlp_terms.rest()
    down_sum = down_terms.rest()
    swap = [(0, 1), (1, 0)]

    def over_cores(rows, low):
        return rows + lax.ppermute(low, "dp", swap).astype(f32)

    def columns_of(first, rows):
        return lax.dot_general(
            first, rows.astype(bf16), (((0,), (1,)), ((), ())), preferred_element_type=f32
        )

    output = (resid + down_sum).astype(bf16)
    grad_resid_norm, gain_mlp_term = pull_mlp(grad_mlp_in)
    grad_resid = cot_own.astype(f32) + grad_resid_norm
    grad_branch = grad_resid.astype(bf16)
    def low_term(left, right):
        return left_matrix_product(left, right).astype(bf16)

    per = in_rows
    few = rank // shards
    grad_attn = right_product(grad_branch, output_weight).astype(bf16)
    lora_output = matrix_product(attn, output_factor_first).astype(bf16)
    lora_query = matrix_product(attn_in, query_factor_first).astype(bf16)
    lora_key = matrix_product(attn_in, key_factor_first).astype(bf16)
    lora_value = matrix_product(attn_in, value_factor_first).astype(bf16)
    early = jnp.concatenate(
        [
            low_term(lora_output, grad_branch).reshape(shards, few, width),
            down_out_term.astype(bf16).reshape(shards, few, width),
            pack_rows(
                jnp.concatenate([gate_in_term, up_in_term], axis=1).astype(bf16), shards, width
            ),
        ],
        axis=1,
    )
    early_sums = scatter_shared(
        jnp.concatenate(
            [low_term(attn, grad_branch).reshape(shards, per, width), early], axis=1
        ),
        core,
    ).astype(f32)
    g_output_weight = early_sums[:per]
    early_sums = early_sums[per:]
    g_output_out = early_sums[:few]
    g_down_out = early_sums[few : 2 * few]
    pair = unpack_rows(early_sums[2 * few :], 2 * head_size)
    g_gate_in = pair[:, :head_size]
    g_up_in = pair[:, head_size:]

    grad_attn_heads = split_heads(grad_attn)
    delta = jnp.sum(
        grad_attn_heads.astype(f32) * attn_raw, axis=-1, keepdims=True
    )

    def grad_step(index, carry):
        grad_query_acc, key_terms = carry
        start = index * block
        probs, key_block, value_block = probs_of(start)
        grad_probs = jnp.einsum(
            "htd,kd->htk", grad_attn_heads, value_block, preferred_element_type=f32
        )
        grad_scores = (scale * probs * (grad_probs - delta)).astype(bf16)
        grad_query_acc = grad_query_acc + jnp.einsum(
            "htk,kd->htd", grad_scores, key_block, preferred_element_type=f32
        )
        key_part = jnp.einsum("htk,htd->kd", grad_scores, query, preferred_element_type=f32)
        value_part = jnp.einsum(
            "htk,htd->kd", probs.astype(bf16), grad_attn_heads, preferred_element_type=f32
        )
        both = jnp.concatenate([key_part, value_part], axis=1).astype(bf16)
        key_terms = lax.dynamic_update_slice_in_dim(key_terms, both, start, 0)
        return (grad_query_acc, key_terms)

    grad_query_rot, key_terms = lax.fori_loop(
        first_block,
        needed,
        grad_step,
        (
            jnp.zeros((heads, tok_rows, head_size), f32),
            jnp.zeros((length, 2 * head_size), bf16),
        ),
    )
    grad_query_lin = join_heads(
        rotate(grad_query_rot, cosines[None], -sines[None]).astype(bf16)
    )
    key_halves = HalvingSum(key_terms, place, shards, [0, tok_rows // 2, tok_rows])
    key_halves.start()
    g_gate_rows = over_cores(gate_rows, gate_rows_low)
    g_gate_rows, up_rows, up_rows_low = together(
        [key_halves], (g_gate_rows, up_rows, up_rows_low)
    )
    key_halves.start()
    g_up_rows = over_cores(up_rows, up_rows_low)
    g_up_rows, down_rows, down_rows_low = together(
        [key_halves], (g_up_rows, down_rows, down_rows_low)
    )
    key_halves.start()
    g_down_rows = over_cores(down_rows, down_rows_low)
    g_gate_out = columns_of(gate_factor_first, g_gate_rows)
    g_down_rows, g_gate_out, g_up_rows, grad_query_lin = together(
        [key_halves], (g_down_rows, g_gate_out, g_up_rows, grad_query_lin)
    )
    key_halves.start()
    g_up_out = columns_of(upward_factor_first, g_up_rows)
    g_down_in = right_product(g_down_rows.astype(bf16), down_factor_second)
    query_terms = low_term(attn_in, grad_query_lin)
    query_grad = right_product(grad_query_lin, query_weight)
    g_up_out, g_down_in, query_terms, query_grad = together(
        [key_halves], (g_up_out, g_down_in, query_terms, query_grad)
    )
    key_sums = key_halves.rest()
    grad_key_value_lin = jnp.concatenate(
        [rotate(key_sums[:, :head_size], cosines, -sines), key_sums[:, head_size:]], axis=1
    ).astype(bf16)
    grad_attn_in = query_grad + right_product(grad_key_value_lin, key_value_weight)
    grad_inputs_norm, gain_attn_term = pull_attn(grad_attn_in)
    grad_inputs = grad_resid + grad_inputs_norm

    tiny = jnp.concatenate(
        [
            low_term(lora_key, grad_key_value_lin[:, :head_size]).reshape(shards, few, head_size),
            low_term(lora_value, grad_key_value_lin[:, head_size:]).reshape(shards, few, head_size),
            gain_attn_term.astype(bf16).reshape(shards, few, -1),
            gain_mlp_term.astype(bf16).reshape(shards, few, -1),
        ],
        axis=2,
    )
    tiny = jnp.pad(tiny, ((0, 0), (0, 0), (0, width - tiny.shape[2])))
    late = jnp.concatenate(
        [
            low_term(lora_query, grad_query_lin).reshape(shards, few, width),
            pack_rows(low_term(attn_in, grad_key_value_lin), shards, width),
            tiny,
        ],
        axis=1,
    )
    late = jnp.concatenate([query_terms.reshape(shards, per, width), late], axis=1)
    if shards == 4 * LINE:
        late_sums = scatter_blocks(late, 4).astype(f32)
    else:
        late_sums = scatter_shared(late, core).astype(f32)
    g_query_weight = late_sums[:per]
    late_sums = late_sums[per:]
    g_query_out = late_sums[:few]
    pair = unpack_rows(late_sums[few : late_sums.shape[0] - few], 2 * head_size)
    g_key_weight = pair[:, :head_size]
    g_value_weight = pair[:, head_size:]
    last = late_sums[late_sums.shape[0] - few :]
    g_key_out = last[:, :head_size]
    g_value_out = last[:, head_size : 2 * head_size]
    each = per // few
    g_gain_attn = last[:, 2 * head_size : 2 * head_size + each].reshape(per)
    g_gain_mlp = last[:, 2 * head_size + each : 2 * head_size + 2 * each].reshape(per)
    g_query_in = right_product(g_query_weight.astype(bf16), query_factor_second)
    g_output_in = right_product(g_output_weight.astype(bf16), output_factor_second)
    g_key_in = right_product(g_key_weight.astype(bf16), key_factor_second)
    g_value_in = right_product(g_value_weight.astype(bf16), value_factor_second)
    return (
        output[None],
        grad_inputs[None],
        g_gain_attn,
        g_gain_mlp,
        g_query_weight,
        g_key_weight,
        g_value_weight,
        g_output_weight,
        g_gate_rows,
        g_up_rows,
        g_down_rows,
        g_query_in,
        g_query_out,
        g_key_in,
        g_key_out,
        g_value_in,
        g_value_out,
        g_output_in,
        g_output_out,
        g_gate_in,
        g_gate_out,
        g_up_in,
        g_up_out,
        g_down_in,
        g_down_out,
    )


def solution(mesh):
    in_specs = (
        P("dp", "fsdp", None),
        P("dp", None),
        P(),
        P(),
        P("fsdp", None),
        P("fsdp", None),
        P("fsdp", None),
        P("fsdp", None),
        P("fsdp", None),
        P("fsdp", None),
        P("fsdp", None),
        P(),
        P(),
        P(),
        P(),
        P(),
        P(),
        P(),
        P(),
        P(),
        P(),
        P(),
        P(),
        P(),
        P(),
        P("dp", "fsdp", None),
    )
    out_specs = (
        P("dp", "fsdp", None),
        P("dp", "fsdp", None),
        P("fsdp"),
        P("fsdp"),
        P("fsdp", None),
        P("fsdp", None),
        P("fsdp", None),
        P("fsdp", None),
        P("fsdp", None),
        P("fsdp", None),
        P("fsdp", None),
        P("fsdp", None),
        P("fsdp", None),
        P("fsdp", None),
        P("fsdp", None),
        P("fsdp", None),
        P("fsdp", None),
        P("fsdp", None),
        P("fsdp", None),
        P("fsdp", None),
        P(None, "fsdp"),
        P("fsdp", None),
        P(None, "fsdp"),
        P("fsdp", None),
        P("fsdp", None),
    )
    return jax.shard_map(local, mesh=mesh, in_specs=in_specs, out_specs=out_specs, check_vma=False)
```

```python
import functools

import jax
import jax.numpy as jnp
from jax import lax
from jax.experimental import pallas as pl
from jax.experimental.pallas import tpu as pltpu
from jax.sharding import PartitionSpec as P

EPS = 1e-06
MESH = pl.DeviceIdType.MESH
LINE = 4


def matrix_product(left, right):
    return jnp.dot(left, right, preferred_element_type=jnp.float32)


def left_matrix_product(left, right):
    return lax.dot_general(
        left, right, (((0,), (0,)), ((), ())), preferred_element_type=jnp.float32
    )


def right_product(left, right):
    return lax.dot_general(
        left, right, (((1,), (1,)), ((), ())), preferred_element_type=jnp.float32
    )


def rms_norm(values, gain):
    factor = lax.rsqrt(jnp.mean(values * values, axis=-1, keepdims=True) + EPS)
    return values * factor * gain


def rotate(values, cosines, sines):
    half = values.shape[-1] // 2
    first = values[..., :half]
    second = values[..., half:]
    return jnp.concatenate(
        [first * cosines - second * sines, second * cosines + first * sines], axis=-1
    )


def doc_positions(segments):
    length = segments.shape[0]
    index = jnp.arange(length, dtype=jnp.int32)
    starts = jnp.concatenate([jnp.ones((1,), dtype=bool), segments[1:] != segments[:-1]])
    first = lax.cummax(jnp.where(starts, index, jnp.zeros_like(index)), axis=0)
    return index - first


def geglu(gate, up):
    return jax.nn.gelu(gate, approximate=True) * up


def place_of():
    f = lax.axis_index("fsdp")
    z, y, x = f // 4, (f // 2) % 2, f % 2
    near_end = z // 2
    inner = (z + near_end) % 2
    visits = []
    for k in range(LINE):
        u = k + inner * (1 if k == 0 else -1 if k == 1 else 0)
        visits.append(u + near_end * (3 - 2 * u))
    return f, z, y, x, f + 1 - 2 * x, f + 2 - 4 * y, visits


def greet(f, z, fx, fy, with_core):
    barrier = pltpu.get_barrier_semaphore()

    def signal(target):
        pl.semaphore_signal(barrier, inc=1, device_id=target, device_id_type=MESH)

    signal({"fsdp": fx})
    signal({"fsdp": fy})
    if with_core:
        signal({"dp": 1 - lax.axis_index("dp")})

    @pl.when(z > 0)
    def _():
        signal({"fsdp": f - 4})

    @pl.when(z < LINE - 1)
    def _():
        signal({"fsdp": f + 4})

    peers = 3 if with_core else 2
    ends = jnp.where(z > 0, 1, 0) + jnp.where(z < LINE - 1, 1, 0)
    pl.semaphore_wait(barrier, peers + ends)


def send(source, target, send_sem, recv_sem, device):
    copy = pltpu.make_async_remote_copy(
        src_ref=source,
        dst_ref=target,
        send_sem=send_sem,
        recv_sem=recv_sem,
        device_id=device,
        device_id_type=MESH,
    )
    copy.start()
    return copy


def arrived(ref, sem):
    pltpu.make_async_copy(ref, ref, sem).wait()


def gather_kernel(pieces, count, with_core, *refs):
    ins, outs = refs[:count], refs[count : 2 * count]
    z_send, z_recv, a_send, a_recv, b_send, b_recv, own_sem, c_send, c_recv = refs[2 * count :]
    f, z, y, x, fx, fy, visits = place_of()
    core = lax.axis_index("dp")
    greet(f, z, fx, fy, with_core)

    def at(index, where, rows):
        ref = outs[index].at[where]
        if with_core:
            ref = ref.at[core]
        return ref.at[pl.ds(*rows)]

    own = []
    for i in range(count):
        target = outs[i].at[f, core] if with_core else outs[i].at[f]
        copy = pltpu.make_async_copy(ins[i], target, own_sem.at[i])
        copy.start()
        own.append(copy)
    sent = []

    def spread_z(p, k):
        index, rows, first = pieces[p]
        v = visits[k]
        where = v * 4 + y * 2 + x
        target = at(index, where, rows)
        if k > 0:
            arrived(target, z_recv.at[p, v])
        source = ins[index].at[pl.ds(*rows)] if k == 0 else target

        @pl.when((v <= z) & (z < LINE - 1))
        def _():
            send(source, target, z_send.at[p, k, 0], z_recv.at[p, v], {"fsdp": f + 4})

        @pl.when((v >= z) & (z > 0))
        def _():
            send(source, target, z_send.at[p, k, 1], z_recv.at[p, v], {"fsdp": f - 4})

        fa, fb = (fy, fx) if first == "y" else (fx, fy)
        sent.append(send(source, target, a_send.at[p, k], a_recv.at[p, k], {"fsdp": fa}))
        sent.append(send(source, target, b_send.at[p, k, 0], b_recv.at[p, k, 0], {"fsdp": fb}))

    def spread_a(p, k):
        index, rows, first = pieces[p]
        v = visits[k]
        where = v * 4 + (1 - y) * 2 + x if first == "y" else v * 4 + y * 2 + (1 - x)
        fb = fx if first == "y" else fy
        target = at(index, where, rows)
        arrived(target, a_recv.at[p, k])
        sent.append(send(target, target, b_send.at[p, k, 1], b_recv.at[p, k, 1], {"fsdp": fb}))

    def finish_b(p, k):
        index, rows, first = pieces[p]
        v = visits[k]
        if first == "y":
            spots = v * 4 + y * 2 + (1 - x), v * 4 + (1 - y) * 2 + (1 - x)
        else:
            spots = v * 4 + (1 - y) * 2 + x, v * 4 + (1 - y) * 2 + (1 - x)
        for j in range(2):
            arrived(at(index, spots[j], rows), b_recv.at[p, k, j])

    def swap(k):
        for i in range(count):
            block = outs[i].at[pl.ds(visits[k] * 4, 4), core]
            sent.append(
                send(block, block, c_send.at[i, k], c_recv.at[i, k], {"dp": 1 - core})
            )

    def swapped(k):
        for i in range(count):
            arrived(outs[i].at[pl.ds(visits[k] * 4, 4), 1 - core], c_recv.at[i, k])

    for k in range(LINE + 1):
        if k < LINE:
            for p in range(len(pieces)):
                spread_z(p, k)
        if k > 0:
            for p in range(len(pieces)):
                spread_a(p, k - 1)
    for copy in own:
        copy.wait()
    for k in range(LINE):
        for p in range(len(pieces)):
            finish_b(p, k)
        if with_core:
            swap(k)
    if with_core:
        for k in range(LINE):
            swapped(k)
    for copy in sent:
        copy.wait_send()
    for p in range(len(pieces)):
        index, rows, first = pieces[p]
        for k in range(LINE):
            v = visits[k]
            block = at(index, f, rows)

            @pl.when((v <= z) & (z < LINE - 1))
            def _():
                pltpu.make_async_copy(block, block, z_send.at[p, k, 0]).wait()

            @pl.when((v >= z) & (z > 0))
            def _():
                pltpu.make_async_copy(block, block, z_send.at[p, k, 1]).wait()


def gather_blocks(arrays, splits, with_core, number):
    shards = 4 * LINE
    pieces = []
    for index, parts in enumerate(splits):
        start = 0
        for rows, first in parts:
            pieces.append((index, (start, rows), first))
            start += rows
    lead = (shards, 2) if with_core else (shards,)
    amount = len(pieces)
    dma = pltpu.SemaphoreType.DMA
    outs = pl.pallas_call(
        functools.partial(gather_kernel, pieces, len(arrays), with_core),
        out_shape=[jax.ShapeDtypeStruct(lead + a.shape, a.dtype) for a in arrays],
        in_specs=[pl.BlockSpec(memory_space=pltpu.VMEM)] * len(arrays),
        out_specs=[pl.BlockSpec(memory_space=pl.ANY)] * len(arrays),
        scratch_shapes=[
            dma((amount, LINE, 2)),
            dma((amount, LINE)),
            dma((amount, LINE)),
            dma((amount, LINE)),
            dma((amount, LINE, 2)),
            dma((amount, LINE, 2)),
            dma((len(arrays),)),
            dma((len(arrays), LINE)),
            dma((len(arrays), LINE)),
        ],
        compiler_params=pltpu.CompilerParams(collective_id=number, has_side_effects=True),
        name="gather_blocks_%d" % number,
    )(*arrays)
    return [o.reshape((-1, o.shape[-1])) for o in outs]


def bit_orders(bits):
    rest = list(range(min(bits, 3), bits))
    first = list(range(min(bits, 3)))
    return [first[i % len(first) :] + first[: i % len(first)] + rest for i in range(3)]


def add_rows(target, other):
    rows = target.shape[0]
    step = 16

    @pl.loop(0, rows // step)
    def _(i):
        part = pl.ds(pl.multiple_of(i * step, step), step)
        total = target[part].astype(jnp.float32) + other[part].astype(jnp.float32)
        target[part] = total.astype(target.dtype)


def scatter_kernel(terms_ref, out_ref, *refs):
    held, c_buf, a_buf, b_buf, z_buf = refs[:5]
    h_sem, c_send, c_recv, a_send, a_recv, b_send, b_recv, z_send, z_recv, o_send, o_recv = refs[5:]
    f, z, y, x, fx, fy, visits = place_of()
    core = lax.axis_index("dp")
    visits = visits[::-1]
    rows = out_ref.shape[0] // 2
    base = pl.multiple_of(core * rows, 16)
    away = pl.multiple_of((1 - core) * rows, 16)
    part = rows // 2
    loads = []
    for k in range(LINE):
        four = pl.ds(visits[k] * 4, 4)
        copy = pltpu.make_async_copy(
            terms_ref.at[four, pl.ds(base, rows)], held.at[four], h_sem.at[k]
        )
        copy.start()
        loads.append(copy)
    greet(f, z, fx, fy, True)

    def spots(p, v):
        piece = pl.ds(p * part, part)
        both = held.at[v * 4 + (1 - y) * 2 + (1 - x), piece]
        only_x = held.at[v * 4 + y * 2 + (1 - x), piece]
        only_y = held.at[v * 4 + (1 - y) * 2 + x, piece]
        own = held.at[v * 4 + y * 2 + x, piece]
        return (both, only_x, only_y, own) if p == 0 else (both, only_y, only_x, own)

    sent = []
    near = ((fx, fy), (fy, fx))
    for k in range(LINE):
        source = terms_ref.at[pl.ds(visits[k] * 4, 4), pl.ds(away, rows)]
        sent.append(send(source, c_buf.at[k], c_send.at[k], c_recv.at[k], {"dp": 1 - core}))

    def start_a(k):
        loads[k].wait()
        arrived(c_buf.at[k], c_recv.at[k])
        for j in range(4):
            add_rows(held.at[visits[k] * 4 + j], c_buf.at[k, j])
        for j in range(2):
            for p in range(2):
                sent.append(
                    send(
                        spots(p, visits[k])[j],
                        a_buf.at[p, k, j],
                        a_send.at[p, k, j],
                        a_recv.at[p, k, j],
                        {"fsdp": near[p][0]},
                    )
                )

    def start_b(p, k):
        flipped = spots(p, visits[k])[2]
        arrived(a_buf.at[p, k, 0], a_recv.at[p, k, 0])
        add_rows(flipped, a_buf.at[p, k, 0])
        sent.append(
            send(flipped, b_buf.at[p, k], b_send.at[p, k], b_recv.at[p, k], {"fsdp": near[p][1]})
        )
        arrived(a_buf.at[p, k, 1], a_recv.at[p, k, 1])
        add_rows(spots(p, visits[k])[3], a_buf.at[p, k, 1])

    def take(p, own, slot):
        arrived(z_buf.at[p, slot], z_recv.at[p, slot])
        add_rows(own, z_buf.at[p, slot])

    def start_z(p, k):
        v = visits[k]
        own = spots(p, v)[3]
        arrived(b_buf.at[p, k], b_recv.at[p, k])
        add_rows(own, b_buf.at[p, k])
        if k == LINE - 1:

            @pl.when(z > 0)
            def _():
                take(p, own, z)

            @pl.when(z < LINE - 1)
            def _():
                take(p, own, LINE)

            return

        @pl.when(v > z)
        def _():
            @pl.when(z > 0)
            def _():
                take(p, own, v)

            send(own, z_buf.at[p, v], z_send.at[p, k], z_recv.at[p, v], {"fsdp": f + 4})

        @pl.when(v < z)
        def _():
            @pl.when(z < LINE - 1)
            def _():
                take(p, own, v)

            @pl.when(v == z - 1)
            def _():
                send(own, z_buf.at[p, LINE], z_send.at[p, k], z_recv.at[p, LINE], {"fsdp": f - 4})

            @pl.when(v < z - 1)
            def _():
                send(own, z_buf.at[p, v], z_send.at[p, k], z_recv.at[p, v], {"fsdp": f - 4})

    start_a(0)
    start_a(1)
    for k in range(LINE + 1):
        if k + 2 < LINE:
            start_a(k + 2)
        if k < LINE:
            for p in range(2):
                start_b(p, k)
        if k > 0:
            for p in range(2):
                start_z(p, k - 1)
    step = 16

    @pl.loop(0, rows // step)
    def _(i):
        offset = pl.multiple_of(i * step, step)
        out_ref[pl.ds(pl.multiple_of(base + offset, step), step)] = held[f, pl.ds(offset, step)]

    final = out_ref.at[pl.ds(base, rows)]
    sent.append(send(final, final, o_send.at[0], o_recv.at[0], {"dp": 1 - core}))
    arrived(out_ref.at[pl.ds(away, rows)], o_recv.at[0])
    for copy in sent:
        copy.wait_send()
    for p in range(2):
        for k in range(LINE - 1):
            pltpu.make_async_copy(b_buf.at[p, k], b_buf.at[p, k], z_send.at[p, k]).wait()


def scatter_blocks(terms, number):
    shards, rows, columns = terms.shape
    dma = pltpu.SemaphoreType.DMA
    own = rows // 2
    part = own // 2
    return pl.pallas_call(
        scatter_kernel,
        out_shape=jax.ShapeDtypeStruct((rows, columns), terms.dtype),
        in_specs=[pl.BlockSpec(memory_space=pl.ANY)],
        out_specs=pl.BlockSpec(memory_space=pltpu.VMEM),
        scratch_shapes=[
            pltpu.VMEM((shards, own, columns), terms.dtype),
            pltpu.VMEM((LINE, 4, own, columns), terms.dtype),
            pltpu.VMEM((2, LINE, 2, part, columns), terms.dtype),
            pltpu.VMEM((2, LINE, part, columns), terms.dtype),
            pltpu.VMEM((2, LINE + 1, part, columns), terms.dtype),
            dma((LINE,)),
            dma((LINE,)),
            dma((LINE,)),
            dma((2, LINE, 2)),
            dma((2, LINE, 2)),
            dma((2, LINE)),
            dma((2, LINE)),
            dma((2, LINE)),
            dma((2, LINE + 1)),
            dma((1,)),
            dma((1,)),
        ],
        compiler_params=pltpu.CompilerParams(
            collective_id=number, has_side_effects=True, vmem_limit_bytes=40 * 1024 * 1024
        ),
        name="scatter_blocks_%d" % number,
    )(terms)


class HalvingSum:
    def __init__(self, terms, place, shards, edges):
        blocks = terms.reshape(shards, terms.shape[0] // shards, terms.shape[1])
        self.place, self.shards, self.kind = place, shards, terms.dtype
        self.bits = shards.bit_length() - 1
        self.orders = bit_orders(self.bits)
        self.held = [
            blocks[:, low:high].reshape((2,) * self.bits + (high - low, terms.shape[1]))
            for low, high in zip(edges[:-1], edges[1:])
        ]
        self.left = [list(range(self.bits))[::-1] for _ in self.held]
        self.step = 0
        self.came = []

    def start(self):
        self.keep, self.came = [], []
        for i, current in enumerate(self.held):
            b = self.orders[i][self.step]
            where, mine = self.left[i].index(b), (self.place >> b) & 1
            self.left[i].remove(b)
            away = lax.dynamic_index_in_dim(current, 1 - mine, where, keepdims=False)
            self.keep.append(lax.dynamic_index_in_dim(current, mine, where, keepdims=False))
            pairs = [(j, j ^ (1 << b)) for j in range(self.shards)]
            self.came.append(lax.ppermute(away, "fsdp", pairs))
        self.step += 1

    def finish(self, came):
        totals = [k.astype(jnp.float32) + c.astype(jnp.float32) for k, c in zip(self.keep, came)]
        if self.step == self.bits:
            self.sum = jnp.concatenate(totals, axis=0)
        else:
            self.held = [t.astype(self.kind) for t in totals]

    def rest(self):
        while self.step < self.bits:
            self.start()
            self.finish(self.came)
        return self.sum


def together(sums, work):
    came, work = lax.optimization_barrier(([s.came for s in sums], work))
    for one, own in zip(sums, came):
        one.finish(own)
    return work


def row_edges(rows):
    third = (rows * 3 // 8) // 16 * 16
    return [0, third, 2 * third, rows]


def scatter_shared(terms, core):
    half = terms.shape[2] // 2
    swap = [(0, 1), (1, 0)]
    own = lax.dynamic_slice_in_dim(terms, core * half, half, 2)
    away = lax.dynamic_slice_in_dim(terms, (1 - core) * half, half, 2)
    return scatter_half(own + lax.ppermute(away, "dp", swap), core)


def scatter_half(both, core):
    swap = [(0, 1), (1, 0)]
    mine = lax.psum_scatter(both, "fsdp", scatter_dimension=0, tiled=False)
    theirs = lax.ppermute(mine, "dp", swap)
    return jnp.where(
        core == 0,
        jnp.concatenate([mine, theirs], axis=1),
        jnp.concatenate([theirs, mine], axis=1),
    )


def pack_rows(terms, shards, width):
    count = width // terms.shape[1]
    parts = terms.reshape(shards, count, -1, terms.shape[1])
    return jnp.concatenate([parts[:, i] for i in range(count)], axis=2)


def unpack_rows(terms, columns):
    count = terms.shape[1] // columns
    return jnp.concatenate(
        [terms[:, i * columns : (i + 1) * columns] for i in range(count)], axis=0
    )


def gather_weights(query, output, key_value, shards):
    if shards == 4 * LINE:
        rows = query.shape[0]
        return gather_blocks(
            [query, output, key_value],
            [[(rows, "y")], [(rows, "x")], [(rows // 2, "y"), (rows // 2, "x")]],
            True,
            1,
        )

    def whole(own):
        return lax.all_gather(own, ("fsdp", "dp"), axis=0, tiled=True)

    return whole(query), whole(output), whole(key_value)


def gather_rows(own, shards, number):
    if shards == 4 * LINE:
        half = own.shape[0] // 2
        return gather_blocks([own], [[(half, "y"), (half, "x")]], False, number)[0]
    return lax.all_gather(own, "fsdp", axis=0, tiled=True)


def local(
    tokens,
    segment_ids,
    gain_attn,
    gain_mlp,
    query_matrix,
    key_matrix,
    value_matrix,
    output_matrix,
    gate_matrix,
    upward_matrix,
    down_matrix,
    query_factor_first,
    query_factor_second,
    key_factor_first,
    key_factor_second,
    value_factor_first,
    value_factor_second,
    output_factor_first,
    output_factor_second,
    gate_factor_first,
    gate_factor_second,
    upward_factor_first,
    upward_factor_second,
    down_factor_first,
    down_factor_second,
    cotangent,
):
    bf16 = jnp.bfloat16
    f32 = jnp.float32
    tok_rows = tokens.shape[1]
    width = tokens.shape[2]
    length = segment_ids.shape[1]
    head_size = key_matrix.shape[1]
    heads = query_matrix.shape[1] // head_size
    unit_rows = gate_matrix.shape[0]
    in_rows = query_matrix.shape[0]
    shards = length // tok_rows
    rank = query_factor_first.shape[1]
    place = lax.axis_index("fsdp")
    core = lax.axis_index("dp")
    offset = place * tok_rows
    input_rows = tokens[0].astype(f32)
    seg_all = segment_ids[0]
    seg_own = lax.dynamic_slice_in_dim(seg_all, offset, tok_rows, 0)
    positions = lax.dynamic_slice_in_dim(doc_positions(seg_all), offset, tok_rows, 0)
    half = head_size // 2
    inverse = 10000.0 ** (-(jnp.arange(half, dtype=f32) * 2.0 / head_size))
    angles = positions.astype(f32)[:, None] * inverse[None, :]
    cosines = jnp.cos(angles)
    sines = jnp.sin(angles)

    core_rows = in_rows // 2

    def split_heads(values):
        return jnp.stack(
            [values[:, h * head_size : (h + 1) * head_size] for h in range(heads)]
        )

    def join_heads(values):
        return jnp.concatenate([values[h] for h in range(heads)], axis=1)

    def merged_rows(matrix, first, second):
        own = lax.dynamic_slice_in_dim(matrix, core * core_rows, core_rows, 0)
        rows = lax.dynamic_slice_in_dim(first, place * in_rows + core * core_rows, core_rows, 0)
        return (own.astype(f32) + matrix_product(rows, second)).astype(bf16)

    query_weight, output_weight, key_value_weight = gather_weights(
        merged_rows(query_matrix, query_factor_first, query_factor_second),
        merged_rows(output_matrix, output_factor_first, output_factor_second),
        jnp.concatenate(
            [
                merged_rows(key_matrix, key_factor_first, key_factor_second),
                merged_rows(value_matrix, value_factor_first, value_factor_second),
            ],
            axis=1,
        ),
        shards,
    )
    cot_own, key_value_weight = lax.optimization_barrier((cotangent[0], key_value_weight))
    cot_all = lax.all_gather(cot_own, "fsdp", axis=0, tiled=True)

    normed_attn, pull_attn = jax.vjp(rms_norm, input_rows, gain_attn)
    attn_in = normed_attn.astype(bf16)
    key_value_lin = matrix_product(attn_in, key_value_weight)
    key = rotate(key_value_lin[:, :head_size], cosines, sines).astype(bf16)
    value = key_value_lin[:, head_size:].astype(bf16)
    key_value = gather_rows(jnp.concatenate([key, value], axis=1), shards, 3)
    query_lin = matrix_product(attn_in, query_weight)
    query = rotate(split_heads(query_lin), cosines[None], sines[None]).astype(bf16)
    keys_all = key_value[:, :head_size]
    values_all = key_value[:, head_size:]
    block = min(512, length)
    scale = head_size ** (-0.5)
    query_index = offset + jnp.arange(tok_rows, dtype=jnp.int32)
    needed = (offset + tok_rows + block - 1) // block
    first_block = (offset - positions[0]) // block

    def scores_of(start):
        key_block = lax.dynamic_slice_in_dim(keys_all, start, block, 0)
        value_block = lax.dynamic_slice_in_dim(values_all, start, block, 0)
        seg_block = lax.dynamic_slice_in_dim(seg_all, start, block, 0)
        key_index = start + jnp.arange(block, dtype=jnp.int32)
        allowed = (seg_own[:, None] == seg_block[None, :]) & (
            key_index[None, :] <= query_index[:, None]
        )
        allowed = allowed[None]
        raw = jnp.einsum("htd,kd->htk", query, key_block, preferred_element_type=f32)
        return (jnp.where(allowed, raw * scale, -1e30), allowed, key_block, value_block)

    def max_step(index, carry):
        top, total = carry
        logits, allowed, key_block, value_block = scores_of(index * block)
        new_top = jnp.maximum(top, jnp.max(logits, axis=-1, keepdims=True))
        weights = jnp.where(allowed, jnp.exp(logits - new_top), 0.0)
        return (new_top, total * jnp.exp(top - new_top) + jnp.sum(weights, axis=-1, keepdims=True))

    start_top = jnp.full((heads, tok_rows, 1), -1e30, f32)
    start_total = jnp.zeros((heads, tok_rows, 1), f32)
    top, total = lax.fori_loop(first_block, needed, max_step, (start_top, start_total))
    log_total = top + jnp.log(total)

    def probs_of(start):
        logits, allowed, key_block, value_block = scores_of(start)
        return (jnp.where(allowed, jnp.exp(logits - log_total), 0.0), key_block, value_block)

    def out_step(index, acc):
        probs, key_block, value_block = probs_of(index * block)
        return acc + jnp.einsum(
            "htk,kd->htd", probs.astype(bf16), value_block, preferred_element_type=f32
        )

    attn_raw = lax.fori_loop(
        first_block, needed, out_step, jnp.zeros((heads, tok_rows, head_size), f32)
    )
    attn = join_heads(attn_raw).astype(bf16)
    resid = input_rows + matrix_product(attn, output_weight)
    normed_mlp, pull_mlp = jax.vjp(rms_norm, resid, gain_mlp)
    mlp_in = normed_mlp.astype(bf16)
    mlp_all = gather_rows(mlp_in, shards, 2)

    first_unit = place * unit_rows
    gate_second = lax.dynamic_slice_in_dim(gate_factor_second, first_unit, unit_rows, 1)
    up_second = lax.dynamic_slice_in_dim(upward_factor_second, first_unit, unit_rows, 1)
    down_first = lax.dynamic_slice_in_dim(down_factor_first, first_unit, unit_rows, 0)

    def merged_units(matrix, first, second):
        low = lax.dot_general(
            second, first, (((0,), (1,)), ((), ())), preferred_element_type=f32
        )
        return (matrix.astype(f32) + low).astype(bf16)

    gate_weight = merged_units(gate_matrix, gate_factor_first, gate_second)
    up_weight = merged_units(upward_matrix, upward_factor_first, up_second)
    down_weight = (
        down_matrix.astype(f32) + matrix_product(down_first, down_factor_second)
    ).astype(bf16)

    gate = right_product(mlp_all, gate_weight)
    up = right_product(mlp_all, up_weight)
    hidden_full, pull_geglu = jax.vjp(geglu, gate, up)
    hidden = hidden_full.astype(bf16)
    edges = row_edges(tok_rows)
    down_product, hidden, cot_late = lax.optimization_barrier(
        (matrix_product(hidden, down_weight).astype(bf16), hidden, cot_all)
    )
    down_terms = HalvingSum(down_product, place, shards, edges)
    down_terms.start()
    grad_hidden = right_product(cot_late, down_weight)
    grad_gate_full, grad_up_full = pull_geglu(grad_hidden)
    grad_gate, grad_up = together(
        [down_terms], (grad_gate_full.astype(bf16), grad_up_full.astype(bf16))
    )
    down_terms.start()
    in_terms = matrix_product(grad_gate, gate_weight)
    in_terms, grad_gate, grad_up = together([down_terms], (in_terms, grad_gate, grad_up))
    down_terms.start()
    in_terms = (in_terms + matrix_product(grad_up, up_weight)).astype(bf16)
    in_terms, grad_gate, grad_up = together([down_terms], (in_terms, grad_gate, grad_up))
    mlp_terms = HalvingSum(in_terms, place, shards, edges)
    down_terms.start()
    mlp_terms.start()
    gate_rows = left_matrix_product(grad_gate, mlp_all).astype(bf16)
    up_rows = left_matrix_product(grad_up, mlp_all).astype(bf16)
    gate_rows, up_rows, hidden = together([down_terms, mlp_terms], (gate_rows, up_rows, hidden))
    mlp_terms.start()
    down_rows = left_matrix_product(hidden, cot_all).astype(bf16)
    down_rows, gate_rows = together([mlp_terms], (down_rows, gate_rows))
    mlp_terms.start()
    gate_in_term = lax.dot_general(
        gate_rows, gate_second, (((0,), (1,)), ((), ())), preferred_element_type=f32
    ).astype(bf16)
    gate_in_term, up_rows, down_rows = together([mlp_terms], (gate_in_term, up_rows, down_rows))
    mlp_terms.start()
    up_in_term = lax.dot_general(
        up_rows, up_second, (((0,), (1,)), ((), ())), preferred_element_type=f32
    ).astype(bf16)
    few = rank // shards
    early = jnp.concatenate(
        [
            left_matrix_product(down_first, down_rows).astype(bf16).reshape(shards, few, width),
            pack_rows(jnp.concatenate([gate_in_term, up_in_term], axis=1), shards, width),
        ],
        axis=1,
    )
    early = together([mlp_terms], early)
    grad_mlp_in = mlp_terms.rest()
    down_sum = down_terms.rest()
    swap = [(0, 1), (1, 0)]

    def over_cores(rows):
        return rows.astype(f32) + lax.ppermute(rows, "dp", swap).astype(f32)

    def columns_of(first, rows):
        return lax.dot_general(
            first, rows.astype(bf16), (((0,), (1,)), ((), ())), preferred_element_type=f32
        )

    output = (resid + down_sum).astype(bf16)
    grad_resid_norm, gain_mlp_term = pull_mlp(grad_mlp_in)
    grad_resid = cot_own.astype(f32) + grad_resid_norm
    grad_branch = grad_resid.astype(bf16)
    def low_term(left, right):
        return left_matrix_product(left, right).astype(bf16)

    per = in_rows
    grad_attn = right_product(grad_branch, output_weight).astype(bf16)
    lora_output = matrix_product(attn, output_factor_first).astype(bf16)
    lora_query = matrix_product(attn_in, query_factor_first).astype(bf16)
    lora_key = matrix_product(attn_in, key_factor_first).astype(bf16)
    lora_value = matrix_product(attn_in, value_factor_first).astype(bf16)
    columns = width // 2

    def half_of(values, which):
        return lax.dynamic_slice_in_dim(values, which * columns, columns, values.ndim - 1)

    def early_parts(which):
        branch = half_of(grad_branch, which)
        return [
            low_term(attn, branch).reshape(shards, per, columns),
            low_term(lora_output, branch).reshape(shards, few, columns),
            half_of(early, which),
        ]

    early_half = jnp.concatenate(
        [
            own + lax.ppermute(away, "dp", swap)
            for own, away in zip(early_parts(core), early_parts(1 - core))
        ],
        axis=1,
    )
    early_half, grad_attn = lax.optimization_barrier((early_half, grad_attn))
    early_sums = scatter_half(early_half, core).astype(f32)
    g_output_weight = early_sums[:per]
    early_sums = early_sums[per:]
    g_output_out = early_sums[:few]
    g_down_out = early_sums[few : 2 * few]
    pair = unpack_rows(early_sums[2 * few :], 2 * head_size)
    g_gate_in = pair[:, :head_size]
    g_up_in = pair[:, head_size:]

    grad_attn_heads = split_heads(grad_attn)
    delta = jnp.sum(
        grad_attn_heads.astype(f32) * attn_raw, axis=-1, keepdims=True
    )

    def grad_step(index, carry):
        grad_query_acc, key_terms = carry
        start = index * block
        probs, key_block, value_block = probs_of(start)
        grad_probs = jnp.einsum(
            "htd,kd->htk", grad_attn_heads, value_block, preferred_element_type=f32
        )
        grad_scores = (scale * probs * (grad_probs - delta)).astype(bf16)
        grad_query_acc = grad_query_acc + jnp.einsum(
            "htk,kd->htd", grad_scores, key_block, preferred_element_type=f32
        )
        key_part = jnp.einsum("htk,htd->kd", grad_scores, query, preferred_element_type=f32)
        value_part = jnp.einsum(
            "htk,htd->kd", probs.astype(bf16), grad_attn_heads, preferred_element_type=f32
        )
        both = jnp.concatenate([key_part, value_part], axis=1).astype(bf16)
        key_terms = lax.dynamic_update_slice_in_dim(key_terms, both, start, 0)
        return (grad_query_acc, key_terms)

    grad_query_rot, key_terms = lax.fori_loop(
        first_block,
        needed,
        grad_step,
        (
            jnp.zeros((heads, tok_rows, head_size), f32),
            jnp.zeros((length, 2 * head_size), bf16),
        ),
    )
    grad_query_lin = join_heads(
        rotate(grad_query_rot, cosines[None], -sines[None]).astype(bf16)
    )
    key_halves = HalvingSum(key_terms, place, shards, [0, tok_rows // 2, tok_rows])
    key_halves.start()
    g_gate_rows = over_cores(gate_rows)
    g_gate_rows, up_rows = together([key_halves], (g_gate_rows, up_rows))
    key_halves.start()
    g_up_rows = over_cores(up_rows)
    g_up_rows, down_rows = together([key_halves], (g_up_rows, down_rows))
    key_halves.start()
    g_down_rows = over_cores(down_rows)
    g_gate_out = columns_of(gate_factor_first, g_gate_rows)
    g_down_rows, g_gate_out, g_up_rows, grad_query_lin = together(
        [key_halves], (g_down_rows, g_gate_out, g_up_rows, grad_query_lin)
    )
    key_halves.start()
    g_up_out = columns_of(upward_factor_first, g_up_rows)
    g_down_in = right_product(g_down_rows.astype(bf16), down_factor_second)
    query_terms = low_term(attn_in, grad_query_lin)
    query_grad = right_product(grad_query_lin, query_weight)
    g_up_out, g_down_in, query_terms, query_grad = together(
        [key_halves], (g_up_out, g_down_in, query_terms, query_grad)
    )
    key_sums = key_halves.rest()
    grad_key_value_lin = jnp.concatenate(
        [rotate(key_sums[:, :head_size], cosines, -sines), key_sums[:, head_size:]], axis=1
    ).astype(bf16)
    grad_attn_in = query_grad + right_product(grad_key_value_lin, key_value_weight)
    grad_inputs_norm, gain_attn_term = pull_attn(grad_attn_in)
    grad_inputs = grad_resid + grad_inputs_norm

    tiny = jnp.concatenate(
        [
            low_term(lora_key, grad_key_value_lin[:, :head_size]).reshape(shards, few, head_size),
            low_term(lora_value, grad_key_value_lin[:, head_size:]).reshape(shards, few, head_size),
            gain_attn_term.astype(bf16).reshape(shards, few, -1),
            gain_mlp_term.astype(bf16).reshape(shards, few, -1),
        ],
        axis=2,
    )
    tiny = jnp.pad(tiny, ((0, 0), (0, 0), (0, width - tiny.shape[2])))
    late = jnp.concatenate(
        [
            low_term(lora_query, grad_query_lin).reshape(shards, few, width),
            pack_rows(low_term(attn_in, grad_key_value_lin), shards, width),
            tiny,
        ],
        axis=1,
    )
    late = jnp.concatenate([query_terms.reshape(shards, per, width), late], axis=1)
    if shards == 4 * LINE:
        late_sums = scatter_blocks(late, 4).astype(f32)
    else:
        late_sums = scatter_shared(late, core).astype(f32)
    g_query_weight = late_sums[:per]
    late_sums = late_sums[per:]
    g_query_out = late_sums[:few]
    pair = unpack_rows(late_sums[few : late_sums.shape[0] - few], 2 * head_size)
    g_key_weight = pair[:, :head_size]
    g_value_weight = pair[:, head_size:]
    last = late_sums[late_sums.shape[0] - few :]
    g_key_out = last[:, :head_size]
    g_value_out = last[:, head_size : 2 * head_size]
    each = per // few
    g_gain_attn = last[:, 2 * head_size : 2 * head_size + each].reshape(per)
    g_gain_mlp = last[:, 2 * head_size + each : 2 * head_size + 2 * each].reshape(per)
    g_query_in = right_product(g_query_weight.astype(bf16), query_factor_second)
    g_output_in = right_product(g_output_weight.astype(bf16), output_factor_second)
    g_key_in = right_product(g_key_weight.astype(bf16), key_factor_second)
    g_value_in = right_product(g_value_weight.astype(bf16), value_factor_second)
    return (
        output[None],
        grad_inputs[None],
        g_gain_attn,
        g_gain_mlp,
        g_query_weight,
        g_key_weight,
        g_value_weight,
        g_output_weight,
        g_gate_rows,
        g_up_rows,
        g_down_rows,
        g_query_in,
        g_query_out,
        g_key_in,
        g_key_out,
        g_value_in,
        g_value_out,
        g_output_in,
        g_output_out,
        g_gate_in,
        g_gate_out,
        g_up_in,
        g_up_out,
        g_down_in,
        g_down_out,
    )


def solution(mesh):
    in_specs = (
        P("dp", "fsdp", None),
        P("dp", None),
        P(),
        P(),
        P("fsdp", None),
        P("fsdp", None),
        P("fsdp", None),
        P("fsdp", None),
        P("fsdp", None),
        P("fsdp", None),
        P("fsdp", None),
        P(),
        P(),
        P(),
        P(),
        P(),
        P(),
        P(),
        P(),
        P(),
        P(),
        P(),
        P(),
        P(),
        P(),
        P("dp", "fsdp", None),
    )
    out_specs = (
        P("dp", "fsdp", None),
        P("dp", "fsdp", None),
        P("fsdp"),
        P("fsdp"),
        P("fsdp", None),
        P("fsdp", None),
        P("fsdp", None),
        P("fsdp", None),
        P("fsdp", None),
        P("fsdp", None),
        P("fsdp", None),
        P("fsdp", None),
        P("fsdp", None),
        P("fsdp", None),
        P("fsdp", None),
        P("fsdp", None),
        P("fsdp", None),
        P("fsdp", None),
        P("fsdp", None),
        P("fsdp", None),
        P(None, "fsdp"),
        P("fsdp", None),
        P(None, "fsdp"),
        P("fsdp", None),
        P("fsdp", None),
    )
    return jax.shard_map(local, mesh=mesh, in_specs=in_specs, out_specs=out_specs, check_vma=False)
```

```python
import functools

import jax
import jax.numpy as jnp
from jax import lax
from jax.experimental import pallas as pl
from jax.experimental.pallas import tpu as pltpu
from jax.sharding import PartitionSpec as P

EPS = 1e-06
MESH = pl.DeviceIdType.MESH
LINE = 4


def matrix_product(left, right):
    return jnp.dot(left, right, preferred_element_type=jnp.float32)


def left_matrix_product(left, right):
    return lax.dot_general(
        left, right, (((0,), (0,)), ((), ())), preferred_element_type=jnp.float32
    )


def right_product(left, right):
    return lax.dot_general(
        left, right, (((1,), (1,)), ((), ())), preferred_element_type=jnp.float32
    )


def rms_norm(values, gain):
    factor = lax.rsqrt(jnp.mean(values * values, axis=-1, keepdims=True) + EPS)
    return values * factor * gain


def rotate(values, cosines, sines):
    half = values.shape[-1] // 2
    first = values[..., :half]
    second = values[..., half:]
    return jnp.concatenate(
        [first * cosines - second * sines, second * cosines + first * sines], axis=-1
    )


def doc_positions(segments):
    length = segments.shape[0]
    index = jnp.arange(length, dtype=jnp.int32)
    starts = jnp.concatenate([jnp.ones((1,), dtype=bool), segments[1:] != segments[:-1]])
    first = lax.cummax(jnp.where(starts, index, jnp.zeros_like(index)), axis=0)
    return index - first


def geglu(gate, up):
    return jax.nn.gelu(gate, approximate=True) * up


def place_of():
    f = lax.axis_index("fsdp")
    z, y, x = f // 4, (f // 2) % 2, f % 2
    near_end = z // 2
    inner = (z + near_end) % 2
    visits = []
    for k in range(LINE):
        u = k + inner * (1 if k == 0 else -1 if k == 1 else 0)
        visits.append(u + near_end * (3 - 2 * u))
    return f, z, y, x, f + 1 - 2 * x, f + 2 - 4 * y, visits


def greet(f, z, fx, fy, with_core):
    barrier = pltpu.get_barrier_semaphore()

    def signal(target):
        pl.semaphore_signal(barrier, inc=1, device_id=target, device_id_type=MESH)

    signal({"fsdp": fx})
    signal({"fsdp": fy})
    if with_core:
        signal({"dp": 1 - lax.axis_index("dp")})

    @pl.when(z > 0)
    def _():
        signal({"fsdp": f - 4})

    @pl.when(z < LINE - 1)
    def _():
        signal({"fsdp": f + 4})

    peers = 3 if with_core else 2
    ends = jnp.where(z > 0, 1, 0) + jnp.where(z < LINE - 1, 1, 0)
    pl.semaphore_wait(barrier, peers + ends)


def send(source, target, send_sem, recv_sem, device):
    copy = pltpu.make_async_remote_copy(
        src_ref=source,
        dst_ref=target,
        send_sem=send_sem,
        recv_sem=recv_sem,
        device_id=device,
        device_id_type=MESH,
    )
    copy.start()
    return copy


def arrived(ref, sem):
    pltpu.make_async_copy(ref, ref, sem).wait()


def gather_kernel(pieces, count, with_core, *refs):
    ins, outs = refs[:count], refs[count : 2 * count]
    z_send, z_recv, a_send, a_recv, b_send, b_recv, own_sem, c_send, c_recv = refs[2 * count :]
    f, z, y, x, fx, fy, visits = place_of()
    core = lax.axis_index("dp")
    greet(f, z, fx, fy, with_core)

    def at(index, where, rows):
        ref = outs[index].at[where]
        if with_core:
            ref = ref.at[core]
        return ref.at[pl.ds(*rows)]

    own = []
    for i in range(count):
        target = outs[i].at[f, core] if with_core else outs[i].at[f]
        copy = pltpu.make_async_copy(ins[i], target, own_sem.at[i])
        copy.start()
        own.append(copy)
    sent = []

    def spread_z(p, k):
        index, rows, first = pieces[p]
        v = visits[k]
        where = v * 4 + y * 2 + x
        target = at(index, where, rows)
        if k > 0:
            arrived(target, z_recv.at[p, v])
        source = ins[index].at[pl.ds(*rows)] if k == 0 else target

        @pl.when((v <= z) & (z < LINE - 1))
        def _():
            send(source, target, z_send.at[p, k, 0], z_recv.at[p, v], {"fsdp": f + 4})

        @pl.when((v >= z) & (z > 0))
        def _():
            send(source, target, z_send.at[p, k, 1], z_recv.at[p, v], {"fsdp": f - 4})

        fa, fb = (fy, fx) if first == "y" else (fx, fy)
        sent.append(send(source, target, a_send.at[p, k], a_recv.at[p, k], {"fsdp": fa}))
        sent.append(send(source, target, b_send.at[p, k, 0], b_recv.at[p, k, 0], {"fsdp": fb}))

    def spread_a(p, k):
        index, rows, first = pieces[p]
        v = visits[k]
        where = v * 4 + (1 - y) * 2 + x if first == "y" else v * 4 + y * 2 + (1 - x)
        fb = fx if first == "y" else fy
        target = at(index, where, rows)
        arrived(target, a_recv.at[p, k])
        sent.append(send(target, target, b_send.at[p, k, 1], b_recv.at[p, k, 1], {"fsdp": fb}))

    def finish_b(p, k):
        index, rows, first = pieces[p]
        v = visits[k]
        if first == "y":
            spots = v * 4 + y * 2 + (1 - x), v * 4 + (1 - y) * 2 + (1 - x)
        else:
            spots = v * 4 + (1 - y) * 2 + x, v * 4 + (1 - y) * 2 + (1 - x)
        for j in range(2):
            arrived(at(index, spots[j], rows), b_recv.at[p, k, j])

    def swap(k):
        for i in range(count):
            block = outs[i].at[pl.ds(visits[k] * 4, 4), core]
            sent.append(
                send(block, block, c_send.at[i, k], c_recv.at[i, k], {"dp": 1 - core})
            )

    def swapped(k):
        for i in range(count):
            arrived(outs[i].at[pl.ds(visits[k] * 4, 4), 1 - core], c_recv.at[i, k])

    for k in range(LINE + 1):
        if k < LINE:
            for p in range(len(pieces)):
                spread_z(p, k)
        if k > 0:
            for p in range(len(pieces)):
                spread_a(p, k - 1)
    for copy in own:
        copy.wait()
    for k in range(LINE):
        for p in range(len(pieces)):
            finish_b(p, k)
        if with_core:
            swap(k)
    if with_core:
        for k in range(LINE):
            swapped(k)
    for copy in sent:
        copy.wait_send()
    for p in range(len(pieces)):
        index, rows, first = pieces[p]
        for k in range(LINE):
            v = visits[k]
            block = at(index, f, rows)

            @pl.when((v <= z) & (z < LINE - 1))
            def _():
                pltpu.make_async_copy(block, block, z_send.at[p, k, 0]).wait()

            @pl.when((v >= z) & (z > 0))
            def _():
                pltpu.make_async_copy(block, block, z_send.at[p, k, 1]).wait()


def gather_blocks(arrays, splits, with_core, number):
    shards = 4 * LINE
    pieces = []
    for index, parts in enumerate(splits):
        start = 0
        for rows, first in parts:
            pieces.append((index, (start, rows), first))
            start += rows
    lead = (shards, 2) if with_core else (shards,)
    amount = len(pieces)
    dma = pltpu.SemaphoreType.DMA
    outs = pl.pallas_call(
        functools.partial(gather_kernel, pieces, len(arrays), with_core),
        out_shape=[jax.ShapeDtypeStruct(lead + a.shape, a.dtype) for a in arrays],
        in_specs=[pl.BlockSpec(memory_space=pltpu.VMEM)] * len(arrays),
        out_specs=[pl.BlockSpec(memory_space=pl.ANY)] * len(arrays),
        scratch_shapes=[
            dma((amount, LINE, 2)),
            dma((amount, LINE)),
            dma((amount, LINE)),
            dma((amount, LINE)),
            dma((amount, LINE, 2)),
            dma((amount, LINE, 2)),
            dma((len(arrays),)),
            dma((len(arrays), LINE)),
            dma((len(arrays), LINE)),
        ],
        compiler_params=pltpu.CompilerParams(collective_id=number, has_side_effects=True),
        name="gather_blocks_%d" % number,
    )(*arrays)
    return [o.reshape((-1, o.shape[-1])) for o in outs]


def bit_orders(bits):
    rest = list(range(min(bits, 3), bits))
    first = list(range(min(bits, 3)))
    return [first[i % len(first) :] + first[: i % len(first)] + rest for i in range(3)]


def add_rows(target, other):
    rows = target.shape[0]
    step = 16

    @pl.loop(0, rows // step)
    def _(i):
        part = pl.ds(pl.multiple_of(i * step, step), step)
        total = target[part].astype(jnp.float32) + other[part].astype(jnp.float32)
        target[part] = total.astype(target.dtype)


def scatter_kernel(first_ref, second_ref, out_ref, *refs):
    held, c_buf, a_buf, b_buf, z_buf = refs[:5]
    h_sem, c_send, c_recv, a_send, a_recv, b_send, b_recv, z_send, z_recv, o_send, o_recv = refs[5:]
    f, z, y, x, fx, fy, visits = place_of()
    core = lax.axis_index("dp")
    visits = visits[::-1]
    rows = out_ref.shape[0] // 2
    base = pl.multiple_of(core * rows, 16)
    away = pl.multiple_of((1 - core) * rows, 16)
    part = rows // 2
    middle = first_ref.shape[1] // 2
    inputs = ((first_ref, 0, middle), (second_ref, middle, rows - middle))

    def input_rows(i, k, which):
        ref, _, count = inputs[i]
        return ref.at[pl.ds(visits[k] * 4, 4), pl.ds(pl.multiple_of(which * count, 16), count)]

    def came(i, k):
        return c_buf.at[k, pl.ds(0, 4), pl.ds(inputs[i][1], inputs[i][2])]

    loads = []
    for k in range(LINE):
        for i in range(2):
            target = held.at[pl.ds(visits[k] * 4, 4), pl.ds(inputs[i][1], inputs[i][2])]
            copy = pltpu.make_async_copy(input_rows(i, k, core), target, h_sem.at[k, i])
            copy.start()
            loads.append(copy)
    greet(f, z, fx, fy, True)

    def spots(p, v):
        piece = pl.ds(p * part, part)
        both = held.at[v * 4 + (1 - y) * 2 + (1 - x), piece]
        only_x = held.at[v * 4 + y * 2 + (1 - x), piece]
        only_y = held.at[v * 4 + (1 - y) * 2 + x, piece]
        own = held.at[v * 4 + y * 2 + x, piece]
        return (both, only_x, only_y, own) if p == 0 else (both, only_y, only_x, own)

    sent = []
    near = ((fx, fy), (fy, fx))
    for k in range(LINE):
        for i in range(2):
            sent.append(
                send(
                    input_rows(i, k, 1 - core),
                    came(i, k),
                    c_send.at[k, i],
                    c_recv.at[k, i],
                    {"dp": 1 - core},
                )
            )

    def start_a(k):
        for i in range(2):
            loads[2 * k + i].wait()
            arrived(came(i, k), c_recv.at[k, i])
        for j in range(4):
            add_rows(held.at[visits[k] * 4 + j], c_buf.at[k, j])
        for j in range(2):
            for p in range(2):
                sent.append(
                    send(
                        spots(p, visits[k])[j],
                        a_buf.at[p, k, j],
                        a_send.at[p, k, j],
                        a_recv.at[p, k, j],
                        {"fsdp": near[p][0]},
                    )
                )

    def start_b(p, k):
        flipped = spots(p, visits[k])[2]
        arrived(a_buf.at[p, k, 0], a_recv.at[p, k, 0])
        add_rows(flipped, a_buf.at[p, k, 0])
        sent.append(
            send(flipped, b_buf.at[p, k], b_send.at[p, k], b_recv.at[p, k], {"fsdp": near[p][1]})
        )
        arrived(a_buf.at[p, k, 1], a_recv.at[p, k, 1])
        add_rows(spots(p, visits[k])[3], a_buf.at[p, k, 1])

    def take(p, own, slot):
        arrived(z_buf.at[p, slot], z_recv.at[p, slot])
        add_rows(own, z_buf.at[p, slot])

    def start_z(p, k):
        v = visits[k]
        own = spots(p, v)[3]
        arrived(b_buf.at[p, k], b_recv.at[p, k])
        add_rows(own, b_buf.at[p, k])
        if k == LINE - 1:

            @pl.when(z > 0)
            def _():
                take(p, own, z)

            @pl.when(z < LINE - 1)
            def _():
                take(p, own, LINE)

            return

        @pl.when(v > z)
        def _():
            @pl.when(z > 0)
            def _():
                take(p, own, v)

            send(own, z_buf.at[p, v], z_send.at[p, k], z_recv.at[p, v], {"fsdp": f + 4})

        @pl.when(v < z)
        def _():
            @pl.when(z < LINE - 1)
            def _():
                take(p, own, v)

            @pl.when(v == z - 1)
            def _():
                send(own, z_buf.at[p, LINE], z_send.at[p, k], z_recv.at[p, LINE], {"fsdp": f - 4})

            @pl.when(v < z - 1)
            def _():
                send(own, z_buf.at[p, v], z_send.at[p, k], z_recv.at[p, v], {"fsdp": f - 4})

    start_a(0)
    start_a(1)
    for k in range(LINE + 1):
        if k + 2 < LINE:
            start_a(k + 2)
        if k < LINE:
            for p in range(2):
                start_b(p, k)
        if k > 0:
            for p in range(2):
                start_z(p, k - 1)
    step = 16

    @pl.loop(0, rows // step)
    def _(i):
        offset = pl.multiple_of(i * step, step)
        out_ref[pl.ds(pl.multiple_of(base + offset, step), step)] = held[f, pl.ds(offset, step)]

    final = out_ref.at[pl.ds(base, rows)]
    sent.append(send(final, final, o_send.at[0], o_recv.at[0], {"dp": 1 - core}))
    arrived(out_ref.at[pl.ds(away, rows)], o_recv.at[0])
    for copy in sent:
        copy.wait_send()
    for p in range(2):
        for k in range(LINE - 1):
            pltpu.make_async_copy(b_buf.at[p, k], b_buf.at[p, k], z_send.at[p, k]).wait()


def scatter_blocks(first, second, number):
    shards, columns = first.shape[0], first.shape[2]
    rows = first.shape[1] + second.shape[1]
    terms = first
    dma = pltpu.SemaphoreType.DMA
    own = rows // 2
    part = own // 2
    sums = pl.pallas_call(
        scatter_kernel,
        out_shape=jax.ShapeDtypeStruct((rows, columns), terms.dtype),
        in_specs=[pl.BlockSpec(memory_space=pl.ANY)] * 2,
        out_specs=pl.BlockSpec(memory_space=pltpu.VMEM),
        scratch_shapes=[
            pltpu.VMEM((shards, own, columns), terms.dtype),
            pltpu.VMEM((LINE, 4, own, columns), terms.dtype),
            pltpu.VMEM((2, LINE, 2, part, columns), terms.dtype),
            pltpu.VMEM((2, LINE, part, columns), terms.dtype),
            pltpu.VMEM((2, LINE + 1, part, columns), terms.dtype),
            dma((LINE, 2)),
            dma((LINE, 2)),
            dma((LINE, 2)),
            dma((2, LINE, 2)),
            dma((2, LINE, 2)),
            dma((2, LINE)),
            dma((2, LINE)),
            dma((2, LINE)),
            dma((2, LINE + 1)),
            dma((1,)),
            dma((1,)),
        ],
        compiler_params=pltpu.CompilerParams(
            collective_id=number, has_side_effects=True, vmem_limit_bytes=40 * 1024 * 1024
        ),
        name="scatter_blocks_%d" % number,
    )(first, second)
    sums = sums.reshape(2, own, columns)
    middle = first.shape[1] // 2
    return sums[:, :middle].reshape(-1, columns), sums[:, middle:].reshape(-1, columns)


class HalvingSum:
    def __init__(self, terms, place, shards, edges):
        blocks = terms.reshape(shards, terms.shape[0] // shards, terms.shape[1])
        self.place, self.shards, self.kind = place, shards, terms.dtype
        self.bits = shards.bit_length() - 1
        self.orders = bit_orders(self.bits)
        self.held = [
            blocks[:, low:high].reshape((2,) * self.bits + (high - low, terms.shape[1]))
            for low, high in zip(edges[:-1], edges[1:])
        ]
        self.left = [list(range(self.bits))[::-1] for _ in self.held]
        self.step = 0
        self.came = []

    def start(self):
        self.keep, self.came = [], []
        for i, current in enumerate(self.held):
            b = self.orders[i][self.step]
            where, mine = self.left[i].index(b), (self.place >> b) & 1
            self.left[i].remove(b)
            away = lax.dynamic_index_in_dim(current, 1 - mine, where, keepdims=False)
            self.keep.append(lax.dynamic_index_in_dim(current, mine, where, keepdims=False))
            pairs = [(j, j ^ (1 << b)) for j in range(self.shards)]
            self.came.append(lax.ppermute(away, "fsdp", pairs))
        self.step += 1

    def finish(self, came):
        totals = [k.astype(jnp.float32) + c.astype(jnp.float32) for k, c in zip(self.keep, came)]
        if self.step == self.bits:
            self.sum = jnp.concatenate(totals, axis=0)
        else:
            self.held = [t.astype(self.kind) for t in totals]

    def rest(self):
        while self.step < self.bits:
            self.start()
            self.finish(self.came)
        return self.sum


def together(sums, work):
    came, work = lax.optimization_barrier(([s.came for s in sums], work))
    for one, own in zip(sums, came):
        one.finish(own)
    return work


def row_edges(rows):
    third = (rows * 3 // 8) // 16 * 16
    return [0, third, 2 * third, rows]


def scatter_shared(terms, core):
    half = terms.shape[2] // 2
    swap = [(0, 1), (1, 0)]
    own = lax.dynamic_slice_in_dim(terms, core * half, half, 2)
    away = lax.dynamic_slice_in_dim(terms, (1 - core) * half, half, 2)
    return scatter_half(own + lax.ppermute(away, "dp", swap), core)


def scatter_half(both, core):
    swap = [(0, 1), (1, 0)]
    mine = lax.psum_scatter(both, "fsdp", scatter_dimension=0, tiled=False)
    theirs = lax.ppermute(mine, "dp", swap)
    return jnp.where(
        core == 0,
        jnp.concatenate([mine, theirs], axis=1),
        jnp.concatenate([theirs, mine], axis=1),
    )


def pack_rows(terms, shards, width):
    count = width // terms.shape[1]
    parts = terms.reshape(shards, count, -1, terms.shape[1])
    return jnp.concatenate([parts[:, i] for i in range(count)], axis=2)


def unpack_rows(terms, columns):
    count = terms.shape[1] // columns
    return jnp.concatenate(
        [terms[:, i * columns : (i + 1) * columns] for i in range(count)], axis=0
    )


def gather_weights(query, output, key_value, shards):
    if shards == 4 * LINE:
        rows = query.shape[0]
        return gather_blocks(
            [query, output, key_value],
            [[(rows, "y")], [(rows, "x")], [(rows // 2, "y"), (rows // 2, "x")]],
            True,
            1,
        )

    def whole(own):
        return lax.all_gather(own, ("fsdp", "dp"), axis=0, tiled=True)

    return whole(query), whole(output), whole(key_value)


def gather_rows(own, shards, number):
    if shards == 4 * LINE:
        half = own.shape[0] // 2
        return gather_blocks([own], [[(half, "y"), (half, "x")]], False, number)[0]
    return lax.all_gather(own, "fsdp", axis=0, tiled=True)


def local(
    tokens,
    segment_ids,
    gain_attn,
    gain_mlp,
    query_matrix,
    key_matrix,
    value_matrix,
    output_matrix,
    gate_matrix,
    upward_matrix,
    down_matrix,
    query_factor_first,
    query_factor_second,
    key_factor_first,
    key_factor_second,
    value_factor_first,
    value_factor_second,
    output_factor_first,
    output_factor_second,
    gate_factor_first,
    gate_factor_second,
    upward_factor_first,
    upward_factor_second,
    down_factor_first,
    down_factor_second,
    cotangent,
):
    bf16 = jnp.bfloat16
    f32 = jnp.float32
    tok_rows = tokens.shape[1]
    width = tokens.shape[2]
    length = segment_ids.shape[1]
    head_size = key_matrix.shape[1]
    heads = query_matrix.shape[1] // head_size
    unit_rows = gate_matrix.shape[0]
    in_rows = query_matrix.shape[0]
    shards = length // tok_rows
    rank = query_factor_first.shape[1]
    place = lax.axis_index("fsdp")
    core = lax.axis_index("dp")
    offset = place * tok_rows
    input_rows = tokens[0].astype(f32)
    seg_all = segment_ids[0]
    seg_own = lax.dynamic_slice_in_dim(seg_all, offset, tok_rows, 0)
    positions = lax.dynamic_slice_in_dim(doc_positions(seg_all), offset, tok_rows, 0)
    half = head_size // 2
    inverse = 10000.0 ** (-(jnp.arange(half, dtype=f32) * 2.0 / head_size))
    angles = positions.astype(f32)[:, None] * inverse[None, :]
    cosines = jnp.cos(angles)
    sines = jnp.sin(angles)

    core_rows = in_rows // 2

    def split_heads(values):
        return jnp.stack(
            [values[:, h * head_size : (h + 1) * head_size] for h in range(heads)]
        )

    def join_heads(values):
        return jnp.concatenate([values[h] for h in range(heads)], axis=1)

    def merged_rows(matrix, first, second):
        own = lax.dynamic_slice_in_dim(matrix, core * core_rows, core_rows, 0)
        rows = lax.dynamic_slice_in_dim(first, place * in_rows + core * core_rows, core_rows, 0)
        return (own.astype(f32) + matrix_product(rows, second)).astype(bf16)

    query_weight, output_weight, key_value_weight = gather_weights(
        merged_rows(query_matrix, query_factor_first, query_factor_second),
        merged_rows(output_matrix, output_factor_first, output_factor_second),
        jnp.concatenate(
            [
                merged_rows(key_matrix, key_factor_first, key_factor_second),
                merged_rows(value_matrix, value_factor_first, value_factor_second),
            ],
            axis=1,
        ),
        shards,
    )
    cot_own, key_value_weight = lax.optimization_barrier((cotangent[0], key_value_weight))
    columns = width // 2
    cot_first = lax.all_gather(cot_own[:, :columns], "fsdp", axis=0, tiled=True)

    normed_attn, pull_attn = jax.vjp(rms_norm, input_rows, gain_attn)
    attn_in = normed_attn.astype(bf16)
    key_value_lin = matrix_product(attn_in, key_value_weight)
    key = rotate(key_value_lin[:, :head_size], cosines, sines).astype(bf16)
    value = key_value_lin[:, head_size:].astype(bf16)
    key_value = gather_rows(jnp.concatenate([key, value], axis=1), shards, 3)
    query_lin = matrix_product(attn_in, query_weight)
    query = rotate(split_heads(query_lin), cosines[None], sines[None]).astype(bf16)
    keys_all = key_value[:, :head_size]
    values_all = key_value[:, head_size:]
    block = min(512, length)
    scale = head_size ** (-0.5)
    query_index = offset + jnp.arange(tok_rows, dtype=jnp.int32)
    needed = (offset + tok_rows + block - 1) // block
    first_block = (offset - positions[0]) // block

    def scores_of(start):
        key_block = lax.dynamic_slice_in_dim(keys_all, start, block, 0)
        value_block = lax.dynamic_slice_in_dim(values_all, start, block, 0)
        seg_block = lax.dynamic_slice_in_dim(seg_all, start, block, 0)
        key_index = start + jnp.arange(block, dtype=jnp.int32)
        allowed = (seg_own[:, None] == seg_block[None, :]) & (
            key_index[None, :] <= query_index[:, None]
        )
        allowed = allowed[None]
        raw = jnp.einsum("htd,kd->htk", query, key_block, preferred_element_type=f32)
        return (jnp.where(allowed, raw * scale, -1e30), allowed, key_block, value_block)

    def max_step(index, carry):
        top, total = carry
        logits, allowed, key_block, value_block = scores_of(index * block)
        new_top = jnp.maximum(top, jnp.max(logits, axis=-1, keepdims=True))
        weights = jnp.where(allowed, jnp.exp(logits - new_top), 0.0)
        return (new_top, total * jnp.exp(top - new_top) + jnp.sum(weights, axis=-1, keepdims=True))

    start_top = jnp.full((heads, tok_rows, 1), -1e30, f32)
    start_total = jnp.zeros((heads, tok_rows, 1), f32)
    top, total = lax.fori_loop(first_block, needed, max_step, (start_top, start_total))
    log_total = top + jnp.log(total)

    def probs_of(start):
        logits, allowed, key_block, value_block = scores_of(start)
        return (jnp.where(allowed, jnp.exp(logits - log_total), 0.0), key_block, value_block)

    def out_step(index, acc):
        probs, key_block, value_block = probs_of(index * block)
        return acc + jnp.einsum(
            "htk,kd->htd", probs.astype(bf16), value_block, preferred_element_type=f32
        )

    attn_raw = lax.fori_loop(
        first_block, needed, out_step, jnp.zeros((heads, tok_rows, head_size), f32)
    )
    attn = join_heads(attn_raw).astype(bf16)
    resid = input_rows + matrix_product(attn, output_weight)
    normed_mlp, pull_mlp = jax.vjp(rms_norm, resid, gain_mlp)
    mlp_in = normed_mlp.astype(bf16)
    mlp_all = gather_rows(mlp_in, shards, 2)
    mlp_all, cot_rest = lax.optimization_barrier((mlp_all, cot_own[:, columns:]))
    cot_second = lax.all_gather(cot_rest, "fsdp", axis=0, tiled=True)
    cot_all = jnp.concatenate([cot_first, cot_second], axis=1)

    first_unit = place * unit_rows
    gate_second = lax.dynamic_slice_in_dim(gate_factor_second, first_unit, unit_rows, 1)
    up_second = lax.dynamic_slice_in_dim(upward_factor_second, first_unit, unit_rows, 1)
    down_first = lax.dynamic_slice_in_dim(down_factor_first, first_unit, unit_rows, 0)

    def merged_units(matrix, first, second):
        low = lax.dot_general(
            second, first, (((0,), (1,)), ((), ())), preferred_element_type=f32
        )
        return (matrix.astype(f32) + low).astype(bf16)

    gate_weight = merged_units(gate_matrix, gate_factor_first, gate_second)
    up_weight = merged_units(upward_matrix, upward_factor_first, up_second)
    down_weight = (
        down_matrix.astype(f32) + matrix_product(down_first, down_factor_second)
    ).astype(bf16)

    gate = right_product(mlp_all, gate_weight)
    up = right_product(mlp_all, up_weight)
    hidden = geglu(gate, up).astype(bf16)
    edges = row_edges(tok_rows)
    down_product, hidden, gate, up = lax.optimization_barrier(
        (matrix_product(hidden, down_weight).astype(bf16), hidden, gate, up)
    )
    down_terms = HalvingSum(down_product, place, shards, edges)
    down_terms.start()
    pull_geglu = jax.vjp(geglu, gate, up)[1]
    grad_hidden = right_product(cot_all, down_weight)
    grad_gate_full, grad_up_full = pull_geglu(grad_hidden)
    grad_gate, grad_up = together(
        [down_terms], (grad_gate_full.astype(bf16), grad_up_full.astype(bf16))
    )
    down_terms.start()
    in_terms = matrix_product(grad_gate, gate_weight)
    in_terms, grad_gate, grad_up = together([down_terms], (in_terms, grad_gate, grad_up))
    down_terms.start()
    in_terms = (in_terms + matrix_product(grad_up, up_weight)).astype(bf16)
    in_terms, grad_gate, grad_up = together([down_terms], (in_terms, grad_gate, grad_up))
    mlp_terms = HalvingSum(in_terms, place, shards, edges)
    down_terms.start()
    mlp_terms.start()
    gate_rows = left_matrix_product(grad_gate, mlp_all).astype(bf16)
    up_rows = left_matrix_product(grad_up, mlp_all).astype(bf16)
    gate_rows, up_rows, hidden = together([down_terms, mlp_terms], (gate_rows, up_rows, hidden))
    mlp_terms.start()
    down_rows = left_matrix_product(hidden, cot_all).astype(bf16)
    down_rows, gate_rows = together([mlp_terms], (down_rows, gate_rows))
    mlp_terms.start()
    gate_in_term = lax.dot_general(
        gate_rows, gate_second, (((0,), (1,)), ((), ())), preferred_element_type=f32
    ).astype(bf16)
    gate_in_term, up_rows, down_rows = together([mlp_terms], (gate_in_term, up_rows, down_rows))
    mlp_terms.start()
    up_in_term = lax.dot_general(
        up_rows, up_second, (((0,), (1,)), ((), ())), preferred_element_type=f32
    ).astype(bf16)
    few = rank // shards
    early = jnp.concatenate(
        [
            left_matrix_product(down_first, down_rows).astype(bf16).reshape(shards, few, width),
            pack_rows(jnp.concatenate([gate_in_term, up_in_term], axis=1), shards, width),
        ],
        axis=1,
    )
    early = together([mlp_terms], early)
    grad_mlp_in = mlp_terms.rest()
    down_sum = down_terms.rest()
    swap = [(0, 1), (1, 0)]

    def over_cores(rows):
        return rows.astype(f32) + lax.ppermute(rows, "dp", swap).astype(f32)

    def columns_of(first, rows):
        return lax.dot_general(
            first, rows.astype(bf16), (((0,), (1,)), ((), ())), preferred_element_type=f32
        )

    output = (resid + down_sum).astype(bf16)
    grad_resid_norm, gain_mlp_term = pull_mlp(grad_mlp_in)
    grad_resid = cot_own.astype(f32) + grad_resid_norm
    grad_branch = grad_resid.astype(bf16)
    def low_term(left, right):
        return left_matrix_product(left, right).astype(bf16)

    per = in_rows
    grad_attn = right_product(grad_branch, output_weight).astype(bf16)
    lora_output = matrix_product(attn, output_factor_first).astype(bf16)
    lora_query = matrix_product(attn_in, query_factor_first).astype(bf16)
    lora_key = matrix_product(attn_in, key_factor_first).astype(bf16)
    lora_value = matrix_product(attn_in, value_factor_first).astype(bf16)
    def half_of(values, which):
        return lax.dynamic_slice_in_dim(values, which * columns, columns, values.ndim - 1)

    def early_parts(which):
        branch = half_of(grad_branch, which)
        return [
            low_term(attn, branch).reshape(shards, per, columns),
            low_term(lora_output, branch).reshape(shards, few, columns),
            half_of(early, which),
        ]

    early_half = jnp.concatenate(
        [
            own + lax.ppermute(away, "dp", swap)
            for own, away in zip(early_parts(core), early_parts(1 - core))
        ],
        axis=1,
    )
    early_half, grad_attn = lax.optimization_barrier((early_half, grad_attn))
    early_sums = scatter_half(early_half, core).astype(f32)
    g_output_weight = early_sums[:per]
    early_sums = early_sums[per:]
    g_output_out = early_sums[:few]
    g_down_out = early_sums[few : 2 * few]
    pair = unpack_rows(early_sums[2 * few :], 2 * head_size)
    g_gate_in = pair[:, :head_size]
    g_up_in = pair[:, head_size:]

    grad_attn_heads = split_heads(grad_attn)
    delta = jnp.sum(
        grad_attn_heads.astype(f32) * attn_raw, axis=-1, keepdims=True
    )

    def grad_step(index, carry):
        grad_query_acc, key_terms = carry
        start = index * block
        probs, key_block, value_block = probs_of(start)
        grad_probs = jnp.einsum(
            "htd,kd->htk", grad_attn_heads, value_block, preferred_element_type=f32
        )
        grad_scores = (scale * probs * (grad_probs - delta)).astype(bf16)
        grad_query_acc = grad_query_acc + jnp.einsum(
            "htk,kd->htd", grad_scores, key_block, preferred_element_type=f32
        )
        key_part = jnp.einsum("htk,htd->kd", grad_scores, query, preferred_element_type=f32)
        value_part = jnp.einsum(
            "htk,htd->kd", probs.astype(bf16), grad_attn_heads, preferred_element_type=f32
        )
        both = jnp.concatenate([key_part, value_part], axis=1).astype(bf16)
        key_terms = lax.dynamic_update_slice_in_dim(key_terms, both, start, 0)
        return (grad_query_acc, key_terms)

    grad_query_rot, key_terms = lax.fori_loop(
        first_block,
        needed,
        grad_step,
        (
            jnp.zeros((heads, tok_rows, head_size), f32),
            jnp.zeros((length, 2 * head_size), bf16),
        ),
    )
    grad_query_lin = join_heads(
        rotate(grad_query_rot, cosines[None], -sines[None]).astype(bf16)
    )
    key_halves = HalvingSum(key_terms, place, shards, [0, tok_rows // 2, tok_rows])
    key_halves.start()
    g_gate_rows = over_cores(gate_rows)
    g_gate_rows, up_rows = together([key_halves], (g_gate_rows, up_rows))
    key_halves.start()
    g_up_rows = over_cores(up_rows)
    g_up_rows, down_rows = together([key_halves], (g_up_rows, down_rows))
    key_halves.start()
    g_down_rows = over_cores(down_rows)
    g_gate_out = columns_of(gate_factor_first, g_gate_rows)
    g_down_rows, g_gate_out, g_up_rows, grad_query_lin = together(
        [key_halves], (g_down_rows, g_gate_out, g_up_rows, grad_query_lin)
    )
    key_halves.start()
    g_up_out = columns_of(upward_factor_first, g_up_rows)
    g_down_in = right_product(g_down_rows.astype(bf16), down_factor_second)
    query_terms = low_term(attn_in, grad_query_lin)
    query_grad = right_product(grad_query_lin, query_weight)
    g_up_out, g_down_in, query_terms, query_grad = together(
        [key_halves], (g_up_out, g_down_in, query_terms, query_grad)
    )
    key_sums = key_halves.rest()
    grad_key_value_lin = jnp.concatenate(
        [rotate(key_sums[:, :head_size], cosines, -sines), key_sums[:, head_size:]], axis=1
    ).astype(bf16)
    grad_attn_in = query_grad + right_product(grad_key_value_lin, key_value_weight)
    grad_inputs_norm, gain_attn_term = pull_attn(grad_attn_in)
    grad_inputs = grad_resid + grad_inputs_norm

    tiny = jnp.concatenate(
        [
            low_term(lora_key, grad_key_value_lin[:, :head_size]).reshape(shards, few, head_size),
            low_term(lora_value, grad_key_value_lin[:, head_size:]).reshape(shards, few, head_size),
            gain_attn_term.astype(bf16).reshape(shards, few, -1),
            gain_mlp_term.astype(bf16).reshape(shards, few, -1),
        ],
        axis=2,
    )
    tiny = jnp.pad(tiny, ((0, 0), (0, 0), (0, width - tiny.shape[2])))
    late = jnp.concatenate(
        [
            low_term(lora_query, grad_query_lin).reshape(shards, few, width),
            pack_rows(low_term(attn_in, grad_key_value_lin), shards, width),
            tiny,
        ],
        axis=1,
    )
    query_terms = query_terms.reshape(shards, per, width)
    if shards == 4 * LINE:
        g_query_weight, late_sums = scatter_blocks(query_terms, late, 4)
    else:
        late_sums = scatter_shared(jnp.concatenate([query_terms, late], axis=1), core)
        g_query_weight, late_sums = late_sums[:per], late_sums[per:]
    g_query_weight, late_sums = g_query_weight.astype(f32), late_sums.astype(f32)
    g_query_out = late_sums[:few]
    pair = unpack_rows(late_sums[few : late_sums.shape[0] - few], 2 * head_size)
    g_key_weight = pair[:, :head_size]
    g_value_weight = pair[:, head_size:]
    last = late_sums[late_sums.shape[0] - few :]
    g_key_out = last[:, :head_size]
    g_value_out = last[:, head_size : 2 * head_size]
    each = per // few
    g_gain_attn = last[:, 2 * head_size : 2 * head_size + each].reshape(per)
    g_gain_mlp = last[:, 2 * head_size + each : 2 * head_size + 2 * each].reshape(per)
    g_query_in = right_product(g_query_weight.astype(bf16), query_factor_second)
    g_output_in = right_product(g_output_weight.astype(bf16), output_factor_second)
    g_key_in = right_product(g_key_weight.astype(bf16), key_factor_second)
    g_value_in = right_product(g_value_weight.astype(bf16), value_factor_second)
    return (
        output[None],
        grad_inputs[None],
        g_gain_attn,
        g_gain_mlp,
        g_query_weight,
        g_key_weight,
        g_value_weight,
        g_output_weight,
        g_gate_rows,
        g_up_rows,
        g_down_rows,
        g_query_in,
        g_query_out,
        g_key_in,
        g_key_out,
        g_value_in,
        g_value_out,
        g_output_in,
        g_output_out,
        g_gate_in,
        g_gate_out,
        g_up_in,
        g_up_out,
        g_down_in,
        g_down_out,
    )


def solution(mesh):
    in_specs = (
        P("dp", "fsdp", None),
        P("dp", None),
        P(),
        P(),
        P("fsdp", None),
        P("fsdp", None),
        P("fsdp", None),
        P("fsdp", None),
        P("fsdp", None),
        P("fsdp", None),
        P("fsdp", None),
        P(),
        P(),
        P(),
        P(),
        P(),
        P(),
        P(),
        P(),
        P(),
        P(),
        P(),
        P(),
        P(),
        P(),
        P("dp", "fsdp", None),
    )
    out_specs = (
        P("dp", "fsdp", None),
        P("dp", "fsdp", None),
        P("fsdp"),
        P("fsdp"),
        P("fsdp", None),
        P("fsdp", None),
        P("fsdp", None),
        P("fsdp", None),
        P("fsdp", None),
        P("fsdp", None),
        P("fsdp", None),
        P("fsdp", None),
        P("fsdp", None),
        P("fsdp", None),
        P("fsdp", None),
        P("fsdp", None),
        P("fsdp", None),
        P("fsdp", None),
        P("fsdp", None),
        P("fsdp", None),
        P(None, "fsdp"),
        P("fsdp", None),
        P(None, "fsdp"),
        P("fsdp", None),
        P("fsdp", None),
    )
    return jax.shard_map(local, mesh=mesh, in_specs=in_specs, out_specs=out_specs, check_vma=False)
```

```python
import functools

import jax
import jax.numpy as jnp
from jax import lax
from jax.experimental import pallas as pl
from jax.experimental.pallas import tpu as pltpu
from jax.sharding import PartitionSpec as P

EPS = 1e-06
MESH = pl.DeviceIdType.MESH
LINE = 4


def matrix_product(left, right):
    return jnp.dot(left, right, preferred_element_type=jnp.float32)


def left_matrix_product(left, right):
    return lax.dot_general(
        left, right, (((0,), (0,)), ((), ())), preferred_element_type=jnp.float32
    )


def right_product(left, right):
    return lax.dot_general(
        left, right, (((1,), (1,)), ((), ())), preferred_element_type=jnp.float32
    )


def rms_norm(values, gain):
    factor = lax.rsqrt(jnp.mean(values * values, axis=-1, keepdims=True) + EPS)
    return values * factor * gain


def rotate(values, cosines, sines):
    half = values.shape[-1] // 2
    first = values[..., :half]
    second = values[..., half:]
    return jnp.concatenate(
        [first * cosines - second * sines, second * cosines + first * sines], axis=-1
    )


def doc_positions(segments):
    length = segments.shape[0]
    index = jnp.arange(length, dtype=jnp.int32)
    starts = jnp.concatenate([jnp.ones((1,), dtype=bool), segments[1:] != segments[:-1]])
    first = lax.cummax(jnp.where(starts, index, jnp.zeros_like(index)), axis=0)
    return index - first


def geglu(gate, up):
    return jax.nn.gelu(gate, approximate=True) * up


def place_of():
    f = lax.axis_index("fsdp")
    z, y, x = f // 4, (f // 2) % 2, f % 2
    near_end = z // 2
    inner = (z + near_end) % 2
    visits = []
    for k in range(LINE):
        u = k + inner * (1 if k == 0 else -1 if k == 1 else 0)
        visits.append(u + near_end * (3 - 2 * u))
    return f, z, y, x, f + 1 - 2 * x, f + 2 - 4 * y, visits


def greet(f, z, fx, fy, with_core):
    barrier = pltpu.get_barrier_semaphore()

    def signal(target):
        pl.semaphore_signal(barrier, inc=1, device_id=target, device_id_type=MESH)

    signal({"fsdp": fx})
    signal({"fsdp": fy})
    if with_core:
        signal({"dp": 1 - lax.axis_index("dp")})

    @pl.when(z > 0)
    def _():
        signal({"fsdp": f - 4})

    @pl.when(z < LINE - 1)
    def _():
        signal({"fsdp": f + 4})

    peers = 3 if with_core else 2
    ends = jnp.where(z > 0, 1, 0) + jnp.where(z < LINE - 1, 1, 0)
    pl.semaphore_wait(barrier, peers + ends)


def send(source, target, send_sem, recv_sem, device):
    copy = pltpu.make_async_remote_copy(
        src_ref=source,
        dst_ref=target,
        send_sem=send_sem,
        recv_sem=recv_sem,
        device_id=device,
        device_id_type=MESH,
    )
    copy.start()
    return copy


def arrived(ref, sem):
    pltpu.make_async_copy(ref, ref, sem).wait()


def gather_kernel(pieces, count, with_core, *refs):
    ins, outs = refs[:count], refs[count : 2 * count]
    z_send, z_recv, a_send, a_recv, b_send, b_recv, own_sem, c_send, c_recv = refs[2 * count :]
    f, z, y, x, fx, fy, visits = place_of()
    core = lax.axis_index("dp")
    greet(f, z, fx, fy, with_core)

    def at(index, where, rows):
        ref = outs[index].at[where]
        if with_core:
            ref = ref.at[core]
        return ref.at[pl.ds(*rows)]

    own = []
    for i in range(count):
        target = outs[i].at[f, core] if with_core else outs[i].at[f]
        copy = pltpu.make_async_copy(ins[i], target, own_sem.at[i])
        copy.start()
        own.append(copy)
    sent = []

    def spread_z(p, k):
        index, rows, first = pieces[p]
        v = visits[k]
        where = v * 4 + y * 2 + x
        target = at(index, where, rows)
        if k > 0:
            arrived(target, z_recv.at[p, v])
        source = ins[index].at[pl.ds(*rows)] if k == 0 else target

        @pl.when((v <= z) & (z < LINE - 1))
        def _():
            send(source, target, z_send.at[p, k, 0], z_recv.at[p, v], {"fsdp": f + 4})

        @pl.when((v >= z) & (z > 0))
        def _():
            send(source, target, z_send.at[p, k, 1], z_recv.at[p, v], {"fsdp": f - 4})

        fa, fb = (fy, fx) if first == "y" else (fx, fy)
        sent.append(send(source, target, a_send.at[p, k], a_recv.at[p, k], {"fsdp": fa}))
        sent.append(send(source, target, b_send.at[p, k, 0], b_recv.at[p, k, 0], {"fsdp": fb}))

    def spread_a(p, k):
        index, rows, first = pieces[p]
        v = visits[k]
        where = v * 4 + (1 - y) * 2 + x if first == "y" else v * 4 + y * 2 + (1 - x)
        fb = fx if first == "y" else fy
        target = at(index, where, rows)
        arrived(target, a_recv.at[p, k])
        sent.append(send(target, target, b_send.at[p, k, 1], b_recv.at[p, k, 1], {"fsdp": fb}))

    def finish_b(p, k):
        index, rows, first = pieces[p]
        v = visits[k]
        if first == "y":
            spots = v * 4 + y * 2 + (1 - x), v * 4 + (1 - y) * 2 + (1 - x)
        else:
            spots = v * 4 + (1 - y) * 2 + x, v * 4 + (1 - y) * 2 + (1 - x)
        for j in range(2):
            arrived(at(index, spots[j], rows), b_recv.at[p, k, j])

    def swap(k):
        for i in range(count):
            block = outs[i].at[pl.ds(visits[k] * 4, 4), core]
            sent.append(
                send(block, block, c_send.at[i, k], c_recv.at[i, k], {"dp": 1 - core})
            )

    def swapped(k):
        for i in range(count):
            arrived(outs[i].at[pl.ds(visits[k] * 4, 4), 1 - core], c_recv.at[i, k])

    for k in range(LINE + 1):
        if k < LINE:
            for p in range(len(pieces)):
                spread_z(p, k)
        if k > 0:
            for p in range(len(pieces)):
                spread_a(p, k - 1)
    for copy in own:
        copy.wait()
    for k in range(LINE):
        for p in range(len(pieces)):
            finish_b(p, k)
        if with_core:
            swap(k)
    if with_core:
        for k in range(LINE):
            swapped(k)
    for copy in sent:
        copy.wait_send()
    for p in range(len(pieces)):
        index, rows, first = pieces[p]
        for k in range(LINE):
            v = visits[k]
            block = at(index, f, rows)

            @pl.when((v <= z) & (z < LINE - 1))
            def _():
                pltpu.make_async_copy(block, block, z_send.at[p, k, 0]).wait()

            @pl.when((v >= z) & (z > 0))
            def _():
                pltpu.make_async_copy(block, block, z_send.at[p, k, 1]).wait()


def gather_blocks(arrays, splits, with_core, number):
    shards = 4 * LINE
    pieces = []
    for index, parts in enumerate(splits):
        start = 0
        for rows, first in parts:
            pieces.append((index, (start, rows), first))
            start += rows
    lead = (shards, 2) if with_core else (shards,)
    amount = len(pieces)
    dma = pltpu.SemaphoreType.DMA
    outs = pl.pallas_call(
        functools.partial(gather_kernel, pieces, len(arrays), with_core),
        out_shape=[jax.ShapeDtypeStruct(lead + a.shape, a.dtype) for a in arrays],
        in_specs=[pl.BlockSpec(memory_space=pltpu.VMEM)] * len(arrays),
        out_specs=[pl.BlockSpec(memory_space=pl.ANY)] * len(arrays),
        scratch_shapes=[
            dma((amount, LINE, 2)),
            dma((amount, LINE)),
            dma((amount, LINE)),
            dma((amount, LINE)),
            dma((amount, LINE, 2)),
            dma((amount, LINE, 2)),
            dma((len(arrays),)),
            dma((len(arrays), LINE)),
            dma((len(arrays), LINE)),
        ],
        compiler_params=pltpu.CompilerParams(collective_id=number, has_side_effects=True),
        name="gather_blocks_%d" % number,
    )(*arrays)
    return [o.reshape((-1, o.shape[-1])) for o in outs]


def bit_orders(bits):
    rest = list(range(min(bits, 3), bits))
    first = list(range(min(bits, 3)))
    return [first[i % len(first) :] + first[: i % len(first)] + rest for i in range(3)]


def add_rows(target, other):
    rows = target.shape[0]
    step = 16

    @pl.loop(0, rows // step)
    def _(i):
        part = pl.ds(pl.multiple_of(i * step, step), step)
        total = target[part].astype(jnp.float32) + other[part].astype(jnp.float32)
        target[part] = total.astype(target.dtype)


def scatter_kernel(first_ref, second_ref, out_ref, *refs):
    held, c_buf, a_buf, b_buf, z_buf = refs[:5]
    h_sem, c_send, c_recv, a_send, a_recv, b_send, b_recv, z_send, z_recv, o_send, o_recv = refs[5:]
    f, z, y, x, fx, fy, visits = place_of()
    core = lax.axis_index("dp")
    visits = visits[::-1]
    rows = out_ref.shape[0] // 2
    base = pl.multiple_of(core * rows, 16)
    away = pl.multiple_of((1 - core) * rows, 16)
    part = rows // 2
    middle = first_ref.shape[1] // 2
    inputs = ((first_ref, 0, middle), (second_ref, middle, rows - middle))

    def input_rows(i, k, which):
        ref, _, count = inputs[i]
        return ref.at[pl.ds(visits[k] * 4, 4), pl.ds(pl.multiple_of(which * count, 16), count)]

    def came(i, k):
        return c_buf.at[k, pl.ds(0, 4), pl.ds(inputs[i][1], inputs[i][2])]

    loads = []
    for k in range(LINE):
        for i in range(2):
            target = held.at[pl.ds(visits[k] * 4, 4), pl.ds(inputs[i][1], inputs[i][2])]
            copy = pltpu.make_async_copy(input_rows(i, k, core), target, h_sem.at[k, i])
            copy.start()
            loads.append(copy)
    greet(f, z, fx, fy, True)

    def spots(p, v):
        piece = pl.ds(p * part, part)
        both = held.at[v * 4 + (1 - y) * 2 + (1 - x), piece]
        only_x = held.at[v * 4 + y * 2 + (1 - x), piece]
        only_y = held.at[v * 4 + (1 - y) * 2 + x, piece]
        own = held.at[v * 4 + y * 2 + x, piece]
        return (both, only_x, only_y, own) if p == 0 else (both, only_y, only_x, own)

    sent = []
    near = ((fx, fy), (fy, fx))
    for k in range(LINE):
        for i in range(2):
            sent.append(
                send(
                    input_rows(i, k, 1 - core),
                    came(i, k),
                    c_send.at[k, i],
                    c_recv.at[k, i],
                    {"dp": 1 - core},
                )
            )

    def start_a(k):
        for i in range(2):
            loads[2 * k + i].wait()
            arrived(came(i, k), c_recv.at[k, i])
        for j in range(4):
            add_rows(held.at[visits[k] * 4 + j], c_buf.at[k, j])
        for j in range(2):
            for p in range(2):
                sent.append(
                    send(
                        spots(p, visits[k])[j],
                        a_buf.at[p, k, j],
                        a_send.at[p, k, j],
                        a_recv.at[p, k, j],
                        {"fsdp": near[p][0]},
                    )
                )

    def start_b(p, k):
        flipped = spots(p, visits[k])[2]
        arrived(a_buf.at[p, k, 0], a_recv.at[p, k, 0])
        add_rows(flipped, a_buf.at[p, k, 0])
        sent.append(
            send(flipped, b_buf.at[p, k], b_send.at[p, k], b_recv.at[p, k], {"fsdp": near[p][1]})
        )
        arrived(a_buf.at[p, k, 1], a_recv.at[p, k, 1])
        add_rows(spots(p, visits[k])[3], a_buf.at[p, k, 1])

    def take(p, own, slot):
        arrived(z_buf.at[p, slot], z_recv.at[p, slot])
        add_rows(own, z_buf.at[p, slot])

    def start_z(p, k):
        v = visits[k]
        own = spots(p, v)[3]
        arrived(b_buf.at[p, k], b_recv.at[p, k])
        add_rows(own, b_buf.at[p, k])
        if k == LINE - 1:

            @pl.when(z > 0)
            def _():
                take(p, own, z)

            @pl.when(z < LINE - 1)
            def _():
                take(p, own, LINE)

            return

        @pl.when(v > z)
        def _():
            @pl.when(z > 0)
            def _():
                take(p, own, v)

            send(own, z_buf.at[p, v], z_send.at[p, k], z_recv.at[p, v], {"fsdp": f + 4})

        @pl.when(v < z)
        def _():
            @pl.when(z < LINE - 1)
            def _():
                take(p, own, v)

            @pl.when(v == z - 1)
            def _():
                send(own, z_buf.at[p, LINE], z_send.at[p, k], z_recv.at[p, LINE], {"fsdp": f - 4})

            @pl.when(v < z - 1)
            def _():
                send(own, z_buf.at[p, v], z_send.at[p, k], z_recv.at[p, v], {"fsdp": f - 4})

    start_a(0)
    start_a(1)
    for k in range(LINE + 1):
        if k + 2 < LINE:
            start_a(k + 2)
        if k < LINE:
            for p in range(2):
                start_b(p, k)
        if k > 0:
            for p in range(2):
                start_z(p, k - 1)
    step = 16

    @pl.loop(0, rows // step)
    def _(i):
        offset = pl.multiple_of(i * step, step)
        out_ref[pl.ds(pl.multiple_of(base + offset, step), step)] = held[f, pl.ds(offset, step)]

    final = out_ref.at[pl.ds(base, rows)]
    sent.append(send(final, final, o_send.at[0], o_recv.at[0], {"dp": 1 - core}))
    arrived(out_ref.at[pl.ds(away, rows)], o_recv.at[0])
    for copy in sent:
        copy.wait_send()
    for p in range(2):
        for k in range(LINE - 1):
            pltpu.make_async_copy(b_buf.at[p, k], b_buf.at[p, k], z_send.at[p, k]).wait()


def scatter_blocks(first, second, number):
    shards, columns = first.shape[0], first.shape[2]
    rows = first.shape[1] + second.shape[1]
    terms = first
    dma = pltpu.SemaphoreType.DMA
    own = rows // 2
    part = own // 2
    sums = pl.pallas_call(
        scatter_kernel,
        out_shape=jax.ShapeDtypeStruct((rows, columns), terms.dtype),
        in_specs=[pl.BlockSpec(memory_space=pl.ANY)] * 2,
        out_specs=pl.BlockSpec(memory_space=pltpu.VMEM),
        scratch_shapes=[
            pltpu.VMEM((shards, own, columns), terms.dtype),
            pltpu.VMEM((LINE, 4, own, columns), terms.dtype),
            pltpu.VMEM((2, LINE, 2, part, columns), terms.dtype),
            pltpu.VMEM((2, LINE, part, columns), terms.dtype),
            pltpu.VMEM((2, LINE + 1, part, columns), terms.dtype),
            dma((LINE, 2)),
            dma((LINE, 2)),
            dma((LINE, 2)),
            dma((2, LINE, 2)),
            dma((2, LINE, 2)),
            dma((2, LINE)),
            dma((2, LINE)),
            dma((2, LINE)),
            dma((2, LINE + 1)),
            dma((1,)),
            dma((1,)),
        ],
        compiler_params=pltpu.CompilerParams(
            collective_id=number, has_side_effects=True, vmem_limit_bytes=40 * 1024 * 1024
        ),
        name="scatter_blocks_%d" % number,
    )(first, second)
    sums = sums.reshape(2, own, columns)
    middle = first.shape[1] // 2
    return sums[:, :middle].reshape(-1, columns), sums[:, middle:].reshape(-1, columns)


class HalvingSum:
    def __init__(self, terms, place, shards, edges):
        blocks = terms.reshape(shards, terms.shape[0] // shards, terms.shape[1])
        self.place, self.shards, self.kind = place, shards, terms.dtype
        self.bits = shards.bit_length() - 1
        self.orders = bit_orders(self.bits)
        self.held = [
            blocks[:, low:high].reshape((2,) * self.bits + (high - low, terms.shape[1]))
            for low, high in zip(edges[:-1], edges[1:])
        ]
        self.left = [list(range(self.bits))[::-1] for _ in self.held]
        self.step = 0
        self.came = []

    def start(self):
        self.keep, self.came = [], []
        for i, current in enumerate(self.held):
            b = self.orders[i][self.step]
            where, mine = self.left[i].index(b), (self.place >> b) & 1
            self.left[i].remove(b)
            away = lax.dynamic_index_in_dim(current, 1 - mine, where, keepdims=False)
            self.keep.append(lax.dynamic_index_in_dim(current, mine, where, keepdims=False))
            pairs = [(j, j ^ (1 << b)) for j in range(self.shards)]
            self.came.append(lax.ppermute(away, "fsdp", pairs))
        self.step += 1

    def finish(self, came):
        totals = [k.astype(jnp.float32) + c.astype(jnp.float32) for k, c in zip(self.keep, came)]
        if self.step == self.bits:
            self.sum = jnp.concatenate(totals, axis=0)
        else:
            self.held = [t.astype(self.kind) for t in totals]

    def rest(self):
        while self.step < self.bits:
            self.start()
            self.finish(self.came)
        return self.sum


def together(sums, work):
    came, work = lax.optimization_barrier(([s.came for s in sums], work))
    for one, own in zip(sums, came):
        one.finish(own)
    return work


def row_edges(rows):
    third = (rows * 3 // 8) // 16 * 16
    return [0, third, 2 * third, rows]


def scatter_shared(terms, core):
    half = terms.shape[2] // 2
    swap = [(0, 1), (1, 0)]
    own = lax.dynamic_slice_in_dim(terms, core * half, half, 2)
    away = lax.dynamic_slice_in_dim(terms, (1 - core) * half, half, 2)
    return scatter_half(own + lax.ppermute(away, "dp", swap), core)


def scatter_half(both, core):
    swap = [(0, 1), (1, 0)]
    mine = lax.psum_scatter(both, "fsdp", scatter_dimension=0, tiled=False)
    theirs = lax.ppermute(mine, "dp", swap)
    return jnp.where(
        core == 0,
        jnp.concatenate([mine, theirs], axis=1),
        jnp.concatenate([theirs, mine], axis=1),
    )


def pack_rows(terms, shards, width):
    count = width // terms.shape[1]
    parts = terms.reshape(shards, count, -1, terms.shape[1])
    return jnp.concatenate([parts[:, i] for i in range(count)], axis=2)


def unpack_rows(terms, columns):
    count = terms.shape[1] // columns
    return jnp.concatenate(
        [terms[:, i * columns : (i + 1) * columns] for i in range(count)], axis=0
    )


def gather_weights(query, output, key_value, shards):
    if shards == 4 * LINE:
        half = query.shape[0] // 2
        return gather_blocks(
            [query, output, key_value],
            [[(half, "y"), (half, "x")]] * 3,
            True,
            1,
        )

    def whole(own):
        return lax.all_gather(own, ("fsdp", "dp"), axis=0, tiled=True)

    return whole(query), whole(output), whole(key_value)


def gather_rows(own, shards, number):
    if shards == 4 * LINE:
        fourth = own.shape[0] // 4
        return gather_blocks([own], [[(fourth, "y"), (fourth, "x")] * 2], False, number)[0]
    return lax.all_gather(own, "fsdp", axis=0, tiled=True)


def local(
    tokens,
    segment_ids,
    gain_attn,
    gain_mlp,
    query_matrix,
    key_matrix,
    value_matrix,
    output_matrix,
    gate_matrix,
    upward_matrix,
    down_matrix,
    query_factor_first,
    query_factor_second,
    key_factor_first,
    key_factor_second,
    value_factor_first,
    value_factor_second,
    output_factor_first,
    output_factor_second,
    gate_factor_first,
    gate_factor_second,
    upward_factor_first,
    upward_factor_second,
    down_factor_first,
    down_factor_second,
    cotangent,
):
    bf16 = jnp.bfloat16
    f32 = jnp.float32
    tok_rows = tokens.shape[1]
    width = tokens.shape[2]
    length = segment_ids.shape[1]
    head_size = key_matrix.shape[1]
    heads = query_matrix.shape[1] // head_size
    unit_rows = gate_matrix.shape[0]
    in_rows = query_matrix.shape[0]
    shards = length // tok_rows
    rank = query_factor_first.shape[1]
    place = lax.axis_index("fsdp")
    core = lax.axis_index("dp")
    offset = place * tok_rows
    input_rows = tokens[0].astype(f32)
    seg_all = segment_ids[0]
    seg_own = lax.dynamic_slice_in_dim(seg_all, offset, tok_rows, 0)
    positions = lax.dynamic_slice_in_dim(doc_positions(seg_all), offset, tok_rows, 0)
    half = head_size // 2
    inverse = 10000.0 ** (-(jnp.arange(half, dtype=f32) * 2.0 / head_size))
    angles = positions.astype(f32)[:, None] * inverse[None, :]
    cosines = jnp.cos(angles)
    sines = jnp.sin(angles)

    core_rows = in_rows // 2

    def split_heads(values):
        return jnp.stack(
            [values[:, h * head_size : (h + 1) * head_size] for h in range(heads)]
        )

    def join_heads(values):
        return jnp.concatenate([values[h] for h in range(heads)], axis=1)

    def merged_rows(matrix, first, second):
        own = lax.dynamic_slice_in_dim(matrix, core * core_rows, core_rows, 0)
        rows = lax.dynamic_slice_in_dim(first, place * in_rows + core * core_rows, core_rows, 0)
        return (own.astype(f32) + matrix_product(rows, second)).astype(bf16)

    query_weight, output_weight, key_value_weight = gather_weights(
        merged_rows(query_matrix, query_factor_first, query_factor_second),
        merged_rows(output_matrix, output_factor_first, output_factor_second),
        jnp.concatenate(
            [
                merged_rows(key_matrix, key_factor_first, key_factor_second),
                merged_rows(value_matrix, value_factor_first, value_factor_second),
            ],
            axis=1,
        ),
        shards,
    )
    cot_own, key_value_weight = lax.optimization_barrier((cotangent[0], key_value_weight))
    columns = width // 2
    cot_first = lax.all_gather(cot_own[:, :columns], "fsdp", axis=0, tiled=True)

    normed_attn, pull_attn = jax.vjp(rms_norm, input_rows, gain_attn)
    attn_in = normed_attn.astype(bf16)
    key_value_lin = matrix_product(attn_in, key_value_weight)
    key = rotate(key_value_lin[:, :head_size], cosines, sines).astype(bf16)
    value = key_value_lin[:, head_size:].astype(bf16)
    key_value = gather_rows(jnp.concatenate([key, value], axis=1), shards, 3)
    query_lin = matrix_product(attn_in, query_weight)
    query = rotate(split_heads(query_lin), cosines[None], sines[None]).astype(bf16)
    keys_all = key_value[:, :head_size]
    values_all = key_value[:, head_size:]
    block = min(512, length)
    scale = head_size ** (-0.5)
    query_index = offset + jnp.arange(tok_rows, dtype=jnp.int32)
    needed = (offset + tok_rows + block - 1) // block
    first_block = (offset - positions[0]) // block

    def scores_of(start):
        key_block = lax.dynamic_slice_in_dim(keys_all, start, block, 0)
        value_block = lax.dynamic_slice_in_dim(values_all, start, block, 0)
        seg_block = lax.dynamic_slice_in_dim(seg_all, start, block, 0)
        key_index = start + jnp.arange(block, dtype=jnp.int32)
        allowed = (seg_own[:, None] == seg_block[None, :]) & (
            key_index[None, :] <= query_index[:, None]
        )
        allowed = allowed[None]
        raw = jnp.einsum("htd,kd->htk", query, key_block, preferred_element_type=f32)
        return (jnp.where(allowed, raw * scale, -1e30), allowed, key_block, value_block)

    def max_step(index, carry):
        top, total = carry
        logits, allowed, key_block, value_block = scores_of(index * block)
        new_top = jnp.maximum(top, jnp.max(logits, axis=-1, keepdims=True))
        weights = jnp.where(allowed, jnp.exp(logits - new_top), 0.0)
        return (new_top, total * jnp.exp(top - new_top) + jnp.sum(weights, axis=-1, keepdims=True))

    start_top = jnp.full((heads, tok_rows, 1), -1e30, f32)
    start_total = jnp.zeros((heads, tok_rows, 1), f32)
    top, total = lax.fori_loop(first_block, needed, max_step, (start_top, start_total))
    log_total = top + jnp.log(total)

    def probs_of(start):
        logits, allowed, key_block, value_block = scores_of(start)
        return (jnp.where(allowed, jnp.exp(logits - log_total), 0.0), key_block, value_block)

    def out_step(index, acc):
        probs, key_block, value_block = probs_of(index * block)
        return acc + jnp.einsum(
            "htk,kd->htd", probs.astype(bf16), value_block, preferred_element_type=f32
        )

    attn_raw = lax.fori_loop(
        first_block, needed, out_step, jnp.zeros((heads, tok_rows, head_size), f32)
    )
    attn = join_heads(attn_raw).astype(bf16)
    resid = input_rows + matrix_product(attn, output_weight)
    normed_mlp, pull_mlp = jax.vjp(rms_norm, resid, gain_mlp)
    mlp_in = normed_mlp.astype(bf16)
    mlp_all = gather_rows(mlp_in, shards, 2)
    mlp_all, cot_rest = lax.optimization_barrier((mlp_all, cot_own[:, columns:]))
    cot_second = lax.all_gather(cot_rest, "fsdp", axis=0, tiled=True)
    cot_all = jnp.concatenate([cot_first, cot_second], axis=1)

    first_unit = place * unit_rows
    gate_second = lax.dynamic_slice_in_dim(gate_factor_second, first_unit, unit_rows, 1)
    up_second = lax.dynamic_slice_in_dim(upward_factor_second, first_unit, unit_rows, 1)
    down_first = lax.dynamic_slice_in_dim(down_factor_first, first_unit, unit_rows, 0)

    def merged_units(matrix, first, second):
        low = lax.dot_general(
            second, first, (((0,), (1,)), ((), ())), preferred_element_type=f32
        )
        return (matrix.astype(f32) + low).astype(bf16)

    gate_weight = merged_units(gate_matrix, gate_factor_first, gate_second)
    up_weight = merged_units(upward_matrix, upward_factor_first, up_second)
    down_weight = (
        down_matrix.astype(f32) + matrix_product(down_first, down_factor_second)
    ).astype(bf16)

    gate = right_product(mlp_all, gate_weight)
    up = right_product(mlp_all, up_weight)
    hidden = geglu(gate, up).astype(bf16)
    edges = row_edges(tok_rows)
    down_product, hidden, gate, up = lax.optimization_barrier(
        (matrix_product(hidden, down_weight).astype(bf16), hidden, gate, up)
    )
    down_terms = HalvingSum(down_product, place, shards, edges)
    down_terms.start()
    pull_geglu = jax.vjp(geglu, gate, up)[1]
    grad_hidden = right_product(cot_all, down_weight)
    grad_gate_full, grad_up_full = pull_geglu(grad_hidden)
    grad_gate, grad_up = together(
        [down_terms], (grad_gate_full.astype(bf16), grad_up_full.astype(bf16))
    )
    down_terms.start()
    in_terms = matrix_product(grad_gate, gate_weight)
    in_terms, grad_gate, grad_up = together([down_terms], (in_terms, grad_gate, grad_up))
    down_terms.start()
    in_terms = (in_terms + matrix_product(grad_up, up_weight)).astype(bf16)
    in_terms, grad_gate, grad_up = together([down_terms], (in_terms, grad_gate, grad_up))
    mlp_terms = HalvingSum(in_terms, place, shards, edges)
    down_terms.start()
    mlp_terms.start()
    gate_rows = left_matrix_product(grad_gate, mlp_all).astype(bf16)
    up_rows = left_matrix_product(grad_up, mlp_all).astype(bf16)
    gate_rows, up_rows, hidden = together([down_terms, mlp_terms], (gate_rows, up_rows, hidden))
    mlp_terms.start()
    down_rows = left_matrix_product(hidden, cot_all).astype(bf16)
    down_rows, gate_rows = together([mlp_terms], (down_rows, gate_rows))
    mlp_terms.start()
    gate_in_term = lax.dot_general(
        gate_rows, gate_second, (((0,), (1,)), ((), ())), preferred_element_type=f32
    ).astype(bf16)
    gate_in_term, up_rows, down_rows = together([mlp_terms], (gate_in_term, up_rows, down_rows))
    mlp_terms.start()
    up_in_term = lax.dot_general(
        up_rows, up_second, (((0,), (1,)), ((), ())), preferred_element_type=f32
    ).astype(bf16)
    few = rank // shards
    early = jnp.concatenate(
        [
            left_matrix_product(down_first, down_rows).astype(bf16).reshape(shards, few, width),
            pack_rows(jnp.concatenate([gate_in_term, up_in_term], axis=1), shards, width),
        ],
        axis=1,
    )
    early = together([mlp_terms], early)
    grad_mlp_in = mlp_terms.rest()
    down_sum = down_terms.rest()
    swap = [(0, 1), (1, 0)]

    def over_cores(rows):
        return rows.astype(f32) + lax.ppermute(rows, "dp", swap).astype(f32)

    def columns_of(first, rows):
        return lax.dot_general(
            first, rows.astype(bf16), (((0,), (1,)), ((), ())), preferred_element_type=f32
        )

    output = (resid + down_sum).astype(bf16)
    grad_resid_norm, gain_mlp_term = pull_mlp(grad_mlp_in)
    grad_resid = cot_own.astype(f32) + grad_resid_norm
    grad_branch = grad_resid.astype(bf16)
    def low_term(left, right):
        return left_matrix_product(left, right).astype(bf16)

    per = in_rows
    grad_attn = right_product(grad_branch, output_weight).astype(bf16)
    lora_output = matrix_product(attn, output_factor_first).astype(bf16)
    lora_query = matrix_product(attn_in, query_factor_first).astype(bf16)
    lora_key = matrix_product(attn_in, key_factor_first).astype(bf16)
    lora_value = matrix_product(attn_in, value_factor_first).astype(bf16)
    def half_of(values, which):
        return lax.dynamic_slice_in_dim(values, which * columns, columns, values.ndim - 1)

    def early_parts(which):
        branch = half_of(grad_branch, which)
        return [
            low_term(attn, branch).reshape(shards, per, columns),
            low_term(lora_output, branch).reshape(shards, few, columns),
            half_of(early, which),
        ]

    early_half = jnp.concatenate(
        [
            own + lax.ppermute(away, "dp", swap)
            for own, away in zip(early_parts(core), early_parts(1 - core))
        ],
        axis=1,
    )
    early_half, grad_attn = lax.optimization_barrier((early_half, grad_attn))
    early_sums = scatter_half(early_half, core).astype(f32)
    g_output_weight = early_sums[:per]
    early_sums = early_sums[per:]
    g_output_out = early_sums[:few]
    g_down_out = early_sums[few : 2 * few]
    pair = unpack_rows(early_sums[2 * few :], 2 * head_size)
    g_gate_in = pair[:, :head_size]
    g_up_in = pair[:, head_size:]

    grad_attn_heads = split_heads(grad_attn)
    delta = jnp.sum(
        grad_attn_heads.astype(f32) * attn_raw, axis=-1, keepdims=True
    )

    def grad_step(index, carry):
        grad_query_acc, key_terms = carry
        start = index * block
        probs, key_block, value_block = probs_of(start)
        grad_probs = jnp.einsum(
            "htd,kd->htk", grad_attn_heads, value_block, preferred_element_type=f32
        )
        grad_scores = (scale * probs * (grad_probs - delta)).astype(bf16)
        grad_query_acc = grad_query_acc + jnp.einsum(
            "htk,kd->htd", grad_scores, key_block, preferred_element_type=f32
        )
        key_part = jnp.einsum("htk,htd->kd", grad_scores, query, preferred_element_type=f32)
        value_part = jnp.einsum(
            "htk,htd->kd", probs.astype(bf16), grad_attn_heads, preferred_element_type=f32
        )
        both = jnp.concatenate([key_part, value_part], axis=1).astype(bf16)
        key_terms = lax.dynamic_update_slice_in_dim(key_terms, both, start, 0)
        return (grad_query_acc, key_terms)

    grad_query_rot, key_terms = lax.fori_loop(
        first_block,
        needed,
        grad_step,
        (
            jnp.zeros((heads, tok_rows, head_size), f32),
            jnp.zeros((length, 2 * head_size), bf16),
        ),
    )
    grad_query_lin = join_heads(
        rotate(grad_query_rot, cosines[None], -sines[None]).astype(bf16)
    )
    key_halves = HalvingSum(key_terms, place, shards, [0, tok_rows // 2, tok_rows])
    key_halves.start()
    g_gate_rows = over_cores(gate_rows)
    g_gate_rows, up_rows = together([key_halves], (g_gate_rows, up_rows))
    key_halves.start()
    g_up_rows = over_cores(up_rows)
    g_up_rows, down_rows = together([key_halves], (g_up_rows, down_rows))
    key_halves.start()
    g_down_rows = over_cores(down_rows)
    g_gate_out = columns_of(gate_factor_first, g_gate_rows)
    g_down_rows, g_gate_out, g_up_rows, grad_query_lin = together(
        [key_halves], (g_down_rows, g_gate_out, g_up_rows, grad_query_lin)
    )
    key_halves.start()
    g_up_out = columns_of(upward_factor_first, g_up_rows)
    g_down_in = right_product(g_down_rows.astype(bf16), down_factor_second)
    query_terms = low_term(attn_in, grad_query_lin)
    query_grad = right_product(grad_query_lin, query_weight)
    g_up_out, g_down_in, query_terms, query_grad = together(
        [key_halves], (g_up_out, g_down_in, query_terms, query_grad)
    )
    key_sums = key_halves.rest()
    grad_key_value_lin = jnp.concatenate(
        [rotate(key_sums[:, :head_size], cosines, -sines), key_sums[:, head_size:]], axis=1
    ).astype(bf16)
    grad_attn_in = query_grad + right_product(grad_key_value_lin, key_value_weight)
    grad_inputs_norm, gain_attn_term = pull_attn(grad_attn_in)
    grad_inputs = grad_resid + grad_inputs_norm

    tiny = jnp.concatenate(
        [
            low_term(lora_key, grad_key_value_lin[:, :head_size]).reshape(shards, few, head_size),
            low_term(lora_value, grad_key_value_lin[:, head_size:]).reshape(shards, few, head_size),
            gain_attn_term.astype(bf16).reshape(shards, few, -1),
            gain_mlp_term.astype(bf16).reshape(shards, few, -1),
        ],
        axis=2,
    )
    tiny = jnp.pad(tiny, ((0, 0), (0, 0), (0, width - tiny.shape[2])))
    late = jnp.concatenate(
        [
            low_term(lora_query, grad_query_lin).reshape(shards, few, width),
            pack_rows(low_term(attn_in, grad_key_value_lin), shards, width),
            tiny,
        ],
        axis=1,
    )
    query_terms = query_terms.reshape(shards, per, width)
    if shards == 4 * LINE:
        g_query_weight, late_sums = scatter_blocks(query_terms, late, 4)
    else:
        late_sums = scatter_shared(jnp.concatenate([query_terms, late], axis=1), core)
        g_query_weight, late_sums = late_sums[:per], late_sums[per:]
    g_query_weight, late_sums = g_query_weight.astype(f32), late_sums.astype(f32)
    g_query_out = late_sums[:few]
    pair = unpack_rows(late_sums[few : late_sums.shape[0] - few], 2 * head_size)
    g_key_weight = pair[:, :head_size]
    g_value_weight = pair[:, head_size:]
    last = late_sums[late_sums.shape[0] - few :]
    g_key_out = last[:, :head_size]
    g_value_out = last[:, head_size : 2 * head_size]
    each = per // few
    g_gain_attn = last[:, 2 * head_size : 2 * head_size + each].reshape(per)
    g_gain_mlp = last[:, 2 * head_size + each : 2 * head_size + 2 * each].reshape(per)
    g_query_in = right_product(g_query_weight.astype(bf16), query_factor_second)
    g_output_in = right_product(g_output_weight.astype(bf16), output_factor_second)
    g_key_in = right_product(g_key_weight.astype(bf16), key_factor_second)
    g_value_in = right_product(g_value_weight.astype(bf16), value_factor_second)
    return (
        output[None],
        grad_inputs[None],
        g_gain_attn,
        g_gain_mlp,
        g_query_weight,
        g_key_weight,
        g_value_weight,
        g_output_weight,
        g_gate_rows,
        g_up_rows,
        g_down_rows,
        g_query_in,
        g_query_out,
        g_key_in,
        g_key_out,
        g_value_in,
        g_value_out,
        g_output_in,
        g_output_out,
        g_gate_in,
        g_gate_out,
        g_up_in,
        g_up_out,
        g_down_in,
        g_down_out,
    )


def solution(mesh):
    in_specs = (
        P("dp", "fsdp", None),
        P("dp", None),
        P(),
        P(),
        P("fsdp", None),
        P("fsdp", None),
        P("fsdp", None),
        P("fsdp", None),
        P("fsdp", None),
        P("fsdp", None),
        P("fsdp", None),
        P(),
        P(),
        P(),
        P(),
        P(),
        P(),
        P(),
        P(),
        P(),
        P(),
        P(),
        P(),
        P(),
        P(),
        P("dp", "fsdp", None),
    )
    out_specs = (
        P("dp", "fsdp", None),
        P("dp", "fsdp", None),
        P("fsdp"),
        P("fsdp"),
        P("fsdp", None),
        P("fsdp", None),
        P("fsdp", None),
        P("fsdp", None),
        P("fsdp", None),
        P("fsdp", None),
        P("fsdp", None),
        P("fsdp", None),
        P("fsdp", None),
        P("fsdp", None),
        P("fsdp", None),
        P("fsdp", None),
        P("fsdp", None),
        P("fsdp", None),
        P("fsdp", None),
        P("fsdp", None),
        P(None, "fsdp"),
        P("fsdp", None),
        P(None, "fsdp"),
        P("fsdp", None),
        P("fsdp", None),
    )
    return jax.shard_map(local, mesh=mesh, in_specs=in_specs, out_specs=out_specs, check_vma=False)
```
